32 devices in a mesh: dp: 8 (over z, y), tensor: 4 (over x, core).
Axes of the slice: x: 2, y: 2, z: 4, core: 2. Of those that a mesh axis runs over, the one named last changes fastest.
Arguments:
- block_input: bfloat16 [8192, 1536], P(('dp', 'tensor')), may hold values from -6 to 6
- segment_ids: int32 [8, 1024], P('dp'), may hold values from 0 to 3, as said below
- gain_attn: float32 [1536], replicated, may hold values from 0.5 to 1.5
- w_query: bfloat16 [1536, 1536], P('dp', 'tensor'), may hold values from -0.15625 to 0.15625
- b_query: float32 [1536], P('tensor'), may hold values from -3 to 3
- w_keyval: bfloat16 [1536, 512], P('dp'), may hold values from -0.15625 to 0.15625
- b_keyval: float32 [512], replicated, may hold values from -3 to 3
- w_out: bfloat16 [1536, 1536], P('tensor', 'dp'), may hold values from -0.625 to 0.625
- gain_ffn: float32 [1536], replicated, may hold values from 0.5 to 1.5
- w_gate: bfloat16 [1536, 8960], P('dp', 'tensor'), may hold values from -0.15625 to 0.15625
- w_up: bfloat16 [1536, 8960], P('dp', 'tensor'), may hold values from -0.15625 to 0.15625
- w_down: bfloat16 [8960, 1536], P('tensor', 'dp'), may hold values from -0.0625 to 0.0625
- cotangent: bfloat16 [8192, 1536], P(('dp', 'tensor')), may hold values from -6 to 6
Outputs:
- block_output: bfloat16 [8192, 1536], P(('dp', 'tensor'))
- grad_input: bfloat16 [8192, 1536], P(('dp', 'tensor'))
- grad_gain_attn: float32 [1536], P(('dp', 'tensor'))
- grad_w_query: float32 [1536, 1536], P('dp', 'tensor')
- grad_b_query: float32 [1536], P(('dp', 'tensor'))
- grad_w_keyval: float32 [1536, 512], P(('dp', 'tensor'))
- grad_b_keyval: float32 [512], P(('dp', 'tensor'))
- grad_w_out: float32 [1536, 1536], P('tensor', 'dp')
- grad_gain_ffn: float32 [1536], P(('dp', 'tensor'))
- grad_w_gate: float32 [1536, 8960], P('dp', 'tensor')
- grad_w_up: float32 [1536, 8960], P('dp', 'tensor')
- grad_w_down: float32 [8960, 1536], P('tensor', 'dp')
The draws below stay inside these ranges and needn't reach their ends.
Inputs may be any that keep to these rules, and one draw needn't show every extreme that they name: `segment_ids`: ids start at 0 and never fall along a sequence, each rising by one at a document's start; a sequence holds 2 to 4 documents, each of 204 tokens or more; some sequence holds 4.
All inputs are finite; a program needn't handle non-finite values.
Results may differ from the reference program's by a relative error of at most 0.018.
Values may be sent and summed in bfloat16 or wider, within the bound.
No kernel may reach another device: no remote copies, remote signals or barrier semaphores. Data moves between devices by JAX's collectives and lax.ppermute only.
A program may use at most 256 MiB of HBM per device.

```python
import math
import jax
import jax.numpy as jnp
from jax import lax

D = 1536
HQ = 12
KV = 2
HD = 128
FF = 8960
SEQ_LEN = 1024
SEQS = 8
TOKENS = 8192
N_TENSOR = 4


def draw_segment_ids(key, part):
    least = SEQ_LEN // 5
    doc_count = jax.random.randint(jax.random.fold_in(key, 21), (SEQS,), 2, 5)
    doc_count = doc_count.at[0].set(4)
    spare = SEQ_LEN - doc_count * least
    cuts = jax.random.randint(jax.random.fold_in(key, 22), (SEQS, 3), 0, SEQ_LEN)
    cuts = cuts % (spare[:, None] + 1)
    slot = jnp.arange(3, dtype=jnp.int32)
    cuts = jnp.where(slot[None, :] < doc_count[:, None] - 1, cuts, spare[:, None])
    cuts = jnp.sort(cuts, axis=1)
    bounds = (slot[None, :] + 1) * least + cuts
    index_row = jnp.arange(SEQ_LEN, dtype=jnp.int32)
    passed = (index_row[None, :, None] >= bounds[:, None, :]).astype(jnp.int32)
    return jnp.sum(passed, axis=2).astype(jnp.int32)


def level_of(stream_key, dims, split, low, largest):
    def one(axis_at, parts):
        steps = jax.random.uniform(jax.random.fold_in(jax.random.fold_in(stream_key, 6), axis_at), (parts,), jnp.float32, low / len(split), largest / len(split))
        return jnp.repeat(jnp.exp(steps), dims[axis_at] // parts).reshape((-1,) + (1,) * (len(dims) - axis_at - 1))

    level = one(*split[0])
    for cut in split[1:]:
        level = level * one(*cut)
    return level


def bell_draw(rng, dims, deviation, limit, shards=(), held_as=jnp.bfloat16):
    level = level_of(rng, dims, shards, -0.22, 0.18) if shards else 1.0
    result = jax.random.normal(rng, dims, jnp.float32) * deviation * level
    return jnp.minimum(jnp.maximum(result, -limit), limit).astype(held_as)


def setup_inputs(seed: int = 0) -> dict:
    key_of = jax.random.split(jax.random.key(seed), 14)
    block_input = bell_draw(key_of[0], (TOKENS, D), 1.0, 6.0, ((0, 32),))
    segment_ids = draw_segment_ids(jax.random.fold_in(key_of[13], 71), 0)
    gain_attn = jnp.clip(1.0 + 0.1 * jax.random.normal(key_of[2], (D,), jnp.float32), 0.5, 1.5)
    w_query = bell_draw(key_of[3], (D, HQ * HD), D ** -0.5, 0.15625, ((0, 8), (1, 4)))
    b_query = bell_draw(key_of[4], (HQ * HD,), 0.5, 3.0, ((0, 4),), jnp.float32)
    w_keyval = bell_draw(key_of[5], (D, 2 * KV * HD), D ** -0.5, 0.15625, ((0, 8),))
    b_keyval = bell_draw(key_of[6], (2 * KV * HD,), 0.5, 3.0, (), jnp.float32)
    w_out = bell_draw(key_of[7], (HQ * HD, D), (HQ * HD // 16) ** -0.5, 0.625, ((0, 4), (1, 8)))
    gain_ffn = jnp.clip(1.0 + 0.1 * jax.random.normal(key_of[8], (D,), jnp.float32), 0.5, 1.5)
    w_gate = bell_draw(key_of[9], (D, FF), D ** -0.5, 0.15625, ((0, 8), (1, 4)))
    w_up = bell_draw(key_of[10], (D, FF), D ** -0.5, 0.15625, ((0, 8), (1, 4)))
    w_down = bell_draw(key_of[11], (FF, D), FF ** -0.5, 0.0625, ((0, 4), (1, 8)))
    cotangent = bell_draw(key_of[12], (TOKENS, D), 1.0, 6.0, ((0, 32),))
    return {"block_input": block_input, "segment_ids": segment_ids, "gain_attn": gain_attn, "w_query": w_query, "b_query": b_query, "w_keyval": w_keyval, "b_keyval": b_keyval, "w_out": w_out, "gain_ffn": gain_ffn, "w_gate": w_gate, "w_up": w_up, "w_down": w_down, "cotangent": cotangent}


epsilon = 1e-06
rope_base = 1000000.0
masked_score = -1e+30

def matmul(left, right):
    return jnp.dot(left, right, preferred_element_type=jnp.float32)

def lowered(values_in):
    return lax.optimization_barrier(values_in.astype(jnp.bfloat16))

def positions_of(segment_row):
    index_row = jnp.arange(segment_row.shape[0], dtype=jnp.int32)
    starts = jnp.concatenate([jnp.ones((1,), jnp.int32), (segment_row[1:] != segment_row[:-1]).astype(jnp.int32)])
    first_index = lax.cummax(jnp.where(starts > 0, index_row, 0), axis=0)
    return index_row - first_index

def allowed_of(segment_row):
    index_row = jnp.arange(segment_row.shape[0], dtype=jnp.int32)
    causal = index_row[:, None] >= index_row[None, :]
    return causal & (segment_row[:, None] == segment_row[None, :])

def rotary(positions):
    inverse = rope_base ** (-(jnp.arange(HD // 2, dtype=jnp.float32) * 2.0 / HD))
    angles = positions.astype(jnp.float32)[:, None] * inverse[None, :]
    angles = jnp.concatenate([angles, angles], axis=1)
    return (jnp.cos(angles), jnp.sin(angles))

def turn(values_in, cosine_table, sine_table):
    half_size = values_in.shape[-1] // 2
    rolled = jnp.concatenate([-values_in[..., half_size:], values_in[..., :half_size]], axis=-1)
    return values_in * cosine_table + rolled * sine_table

def norm_forward(values_in):
    row_scale = lax.rsqrt(lax.optimization_barrier(jnp.mean(values_in * values_in, axis=-1, keepdims=True)) + epsilon)
    return (values_in * row_scale, row_scale)

def norm_backward(grad_out, normed, row_scale, gain_vec):
    grad_normed = grad_out * gain_vec
    grad_in = row_scale * (grad_normed - normed * lax.optimization_barrier(jnp.mean(grad_normed * normed, axis=-1, keepdims=True)))
    return (grad_in, lax.optimization_barrier(jnp.sum(grad_out * normed, axis=0)))

def reference(block_input, segment_ids, gain_attn, w_query, b_query, w_keyval, b_keyval, w_out, gain_ffn, w_gate, w_up, w_down, cotangent):
    seq_count = segment_ids.shape[0]
    seq_length = segment_ids.shape[1]
    heads_dev = HQ // N_TENSOR
    group_size = HQ // KV
    kv_of = jnp.arange(HQ, dtype=jnp.int32) // group_size
    root_size = math.sqrt(HD)
    inputs_seq = block_input.reshape(seq_count, seq_length, D)
    cot_seq = cotangent.reshape(seq_count, seq_length, D)

    def one_sequence(totals, seq_items):
        rows_in, segment_row, rows_cot = seq_items
        rows_float = rows_in.astype(jnp.float32)
        normed_one, scale_one = norm_forward(rows_float)
        act_one = lowered(normed_one * gain_attn)
        query_rows = matmul(act_one, w_query) + b_query
        keyval = matmul(act_one, w_keyval) + b_keyval
        cosine_table, sine_table = rotary(positions_of(segment_row))
        cos_heads = cosine_table[:, None, :]
        sin_heads = sine_table[:, None, :]
        query_rot = lowered(turn(query_rows.reshape(seq_length, HQ, HD), cos_heads, sin_heads)).astype(jnp.float32)
        key_rot = lowered(turn(keyval[:, :KV * HD].reshape(seq_length, KV, HD), cos_heads, sin_heads)).astype(jnp.float32)
        value_rows = lowered(keyval[:, KV * HD:].reshape(seq_length, KV, HD)).astype(jnp.float32)
        key_heads = key_rot[:, kv_of]
        value_heads = value_rows[:, kv_of]
        allowed = allowed_of(segment_row)
        raw_scores = jnp.einsum('qhd,khd->hqk', query_rot, key_heads) / root_size
        scores = jnp.where(allowed[None], raw_scores, masked_score)
        row_max = lax.optimization_barrier(jnp.max(scores, axis=2, keepdims=True))
        log_total = row_max + jnp.log(lax.optimization_barrier(jnp.sum(jnp.exp(scores - row_max), axis=2, keepdims=True)))
        attn_probs = jnp.exp(scores - log_total)
        probs_low = lowered(attn_probs).astype(jnp.float32)
        attn_result = jnp.einsum('hqk,khd->qhd', probs_low, value_heads)
        context = lowered(attn_result.reshape(seq_length, HQ * HD))
        hidden = rows_float + matmul(context, w_out)
        normed_two, scale_two = norm_forward(hidden)
        act_two = lowered(normed_two * gain_ffn)
        gate_pre = matmul(act_two, w_gate)
        up_part = matmul(act_two, w_up)
        sigmoid_gate = jax.nn.sigmoid(gate_pre)
        silu_gate = gate_pre * sigmoid_gate
        mixed_rows = lowered(silu_gate * up_part)
        block_out = (hidden + matmul(mixed_rows, w_down)).astype(jnp.bfloat16)
        grad_mixed = matmul(rows_cot, w_down.T)
        grad_gate = lowered(grad_mixed * up_part * sigmoid_gate * (1.0 + gate_pre * (1.0 - sigmoid_gate)))
        grad_up = lowered(grad_mixed * silu_gate)
        grad_act_two = matmul(grad_gate, w_gate.T) + matmul(grad_up, w_up.T)
        back_two, gain_two = norm_backward(grad_act_two, normed_two, scale_two, gain_ffn)
        grad_hidden = rows_cot.astype(jnp.float32) + back_two
        grad_attn = lowered(grad_hidden)
        grad_context = lowered(matmul(grad_attn, w_out.T)).astype(jnp.float32).reshape(seq_length, HQ, HD)
        grad_probs = jnp.einsum('qhd,khd->hqk', grad_context, value_heads)
        row_delta = lax.optimization_barrier(jnp.sum(grad_context * attn_result, axis=2)).T[:, :, None]
        grad_scores = lowered(attn_probs * (grad_probs - row_delta)).astype(jnp.float32)
        grad_query_rot = jnp.einsum('hqk,khd->qhd', grad_scores, key_heads) / root_size
        grad_key_heads = jnp.einsum('hqk,qhd->khd', grad_scores, query_rot) / root_size
        grad_value_heads = jnp.einsum('hqk,qhd->khd', probs_low, grad_context)
        grad_query = turn(grad_query_rot, cos_heads, -sin_heads).reshape(seq_length, HQ * HD)
        grad_key_dev = turn(grad_key_heads.reshape(seq_length, N_TENSOR, heads_dev, HD).sum(axis=2), cos_heads, -sin_heads)
        grad_value_dev = grad_value_heads.reshape(seq_length, N_TENSOR, heads_dev, HD).sum(axis=2)
        grad_query_low = lowered(grad_query)
        grad_act_one = matmul(grad_query_low, w_query.T)
        grad_wkv = jnp.zeros((D, 2 * KV * HD), jnp.float32)
        grad_bkv = jnp.zeros((2 * KV * HD,), jnp.float32)
        for tensor_slot in range(N_TENSOR):
            head_kv = tensor_slot * heads_dev // group_size
            key_col = head_kv * HD
            value_col = KV * HD + head_kv * HD
            key_low = lowered(grad_key_dev[:, tensor_slot])
            value_low = lowered(grad_value_dev[:, tensor_slot])
            grad_wkv = grad_wkv.at[:, key_col:key_col + HD].add(matmul(act_one.T, key_low))
            grad_wkv = grad_wkv.at[:, value_col:value_col + HD].add(matmul(act_one.T, value_low))
            grad_act_one = grad_act_one + matmul(key_low, w_keyval[:, key_col:key_col + HD].T)
            grad_act_one = grad_act_one + matmul(value_low, w_keyval[:, value_col:value_col + HD].T)
            grad_bkv = grad_bkv.at[key_col:key_col + HD].add(lax.optimization_barrier(jnp.sum(grad_key_dev[:, tensor_slot], axis=0)))
            grad_bkv = grad_bkv.at[value_col:value_col + HD].add(lax.optimization_barrier(jnp.sum(grad_value_dev[:, tensor_slot], axis=0)))
        back_one, gain_one = norm_backward(grad_act_one, normed_one, scale_one, gain_attn)
        grad_rows = (grad_hidden + back_one).astype(jnp.bfloat16)
        new_totals = (totals[0] + gain_one, totals[1] + matmul(act_one.T, grad_query_low), totals[2] + lax.optimization_barrier(jnp.sum(grad_query, axis=0)), totals[3] + grad_wkv, totals[4] + grad_bkv, totals[5] + matmul(context.T, grad_attn), totals[6] + gain_two, totals[7] + matmul(act_two.T, grad_gate), totals[8] + matmul(act_two.T, grad_up), totals[9] + matmul(mixed_rows.T, rows_cot))
        return (new_totals, (block_out, grad_rows))
    init_totals = (jnp.zeros((D,), jnp.float32), jnp.zeros((D, HQ * HD), jnp.float32), jnp.zeros((HQ * HD,), jnp.float32), jnp.zeros((D, 2 * KV * HD), jnp.float32), jnp.zeros((2 * KV * HD,), jnp.float32), jnp.zeros((HQ * HD, D), jnp.float32), jnp.zeros((D,), jnp.float32), jnp.zeros((D, FF), jnp.float32), jnp.zeros((D, FF), jnp.float32), jnp.zeros((FF, D), jnp.float32))
    totals, (outputs, grads) = lax.scan(one_sequence, init_totals, (inputs_seq, segment_ids, cot_seq))
    return (outputs.reshape(seq_count * seq_length, D), grads.reshape(seq_count * seq_length, D), totals[0], totals[1], totals[2], totals[3], totals[4], totals[5], totals[6], totals[7], totals[8], totals[9])
```

```python
import math

import jax
import jax.numpy as jnp
from jax import lax
from jax.sharding import PartitionSpec as P

HQ = 12
KV = 2
HD = 128


epsilon = 1e-06
rope_base = 1000000.0
masked_score = -1e30
bf16 = jnp.bfloat16
f32 = jnp.float32


def dot(left, right, left_dim, right_dim, out=f32):
    return lax.dot_general(
        left, right, (((left_dim,), (right_dim,)), ((), ())), preferred_element_type=f32
    ).astype(out)


def positions_of(segment_row):
    index_row = jnp.arange(segment_row.shape[0], dtype=jnp.int32)
    starts = jnp.concatenate(
        [jnp.ones((1,), jnp.int32), (segment_row[1:] != segment_row[:-1]).astype(jnp.int32)]
    )
    first_index = lax.cummax(jnp.where(starts > 0, index_row, 0), axis=0)
    return index_row - first_index


def allowed_of(segment_row):
    index_row = jnp.arange(segment_row.shape[0], dtype=jnp.int32)
    causal = index_row[:, None] >= index_row[None, :]
    return causal & (segment_row[:, None] == segment_row[None, :])


def rotary(positions):
    inverse = rope_base ** (-(jnp.arange(HD // 2, dtype=jnp.float32) * 2.0 / HD))
    angles = positions.astype(jnp.float32)[:, None] * inverse[None, :]
    angles = jnp.concatenate([angles, angles], axis=1)
    return (jnp.cos(angles), jnp.sin(angles))


def turn(values_in, cosine_table, sine_table):
    half_size = values_in.shape[-1] // 2
    rolled = jnp.concatenate([-values_in[..., half_size:], values_in[..., :half_size]], axis=-1)
    return values_in * cosine_table + rolled * sine_table


def norm_forward(values_in):
    row_scale = lax.rsqrt(jnp.mean(values_in * values_in, axis=-1, keepdims=True) + epsilon)
    return (values_in * row_scale, row_scale)


def norm_backward(grad_out, normed, row_scale, gain_vec):
    grad_normed = grad_out * gain_vec
    grad_in = row_scale * (
        grad_normed - normed * jnp.mean(grad_normed * normed, axis=-1, keepdims=True)
    )
    return (grad_in, jnp.sum(grad_out * normed, axis=0))


def twist(array, axis, index, codes, bits, back=False):
    count = len(codes)
    blocks = jnp.split(array, count, axis=axis)
    if not back:
        blocks = [blocks[code] for code in codes]
    place = {code: at for at, code in enumerate(codes)}
    bit = 1
    while bit < 2 * count:
        if bits & bit:
            flag = (index & bit) != 0
            blocks = [
                jnp.where(flag, blocks[place[code ^ bit]], blocks[at])
                for at, code in enumerate(codes)
            ]
        bit *= 2
    if back:
        blocks = [blocks[place[at]] for at in range(count)]
    return jnp.concatenate(blocks, axis=axis)


def solution(mesh):
    dp_size = mesh.shape["dp"]
    tensor_size = mesh.shape["tensor"]
    pair_bit = 2
    dp_bits = []
    bit = dp_size // 2
    while bit:
        dp_bits.append(bit)
        bit //= 2
    ring_bits = [bit for bit in dp_bits if bit != pair_bit]
    ring_mask = sum(ring_bits)

    def swap(array, axis, bit):
        size = mesh.shape[axis]
        return lax.ppermute(array, axis, [(i, i ^ bit) for i in range(size)])

    def masks_of(bits):
        masks = [0]
        for bit in bits:
            masks = masks + [mask ^ bit for mask in masks]
        return masks

    def gather_rows(piece, bits):
        pieces = [piece]
        for bit in bits:
            if len(pieces) <= 4:
                pieces = pieces + [swap(part, "dp", bit) for part in pieces]
            else:
                joined = swap(jnp.concatenate(pieces, axis=0), "dp", bit)
                pieces = pieces + jnp.split(joined, len(pieces), axis=0)
        return jnp.concatenate(pieces, axis=0)

    def scatter_rows(total, bits):
        for bit in reversed(bits):
            half = total.shape[0] // 2
            arrived = swap(total[half:].astype(bf16), "dp", bit)
            total = total[:half].astype(f32) + arrived.astype(f32)
        return total

    token_codes = [0, 2, 1, 3]

    def gather_four(rows):
        pair = jnp.concatenate([rows, swap(rows, "tensor", 2)], axis=0)
        return jnp.concatenate([pair, swap(pair, "tensor", 1)], axis=0)

    def scatter_four(partial):
        half = partial.shape[0] // 2
        arrived = swap(partial[half:], "tensor", 1)
        pair = partial[:half].astype(f32) + arrived.astype(f32)
        half = half // 2
        arrived = swap(pair[half:].astype(bf16), "tensor", 2)
        return pair[:half] + arrived.astype(f32)

    def gather_eight(rows):
        half = rows.shape[0] // 2
        over_x = swap(rows, "tensor", 2)
        over_pair = swap(rows, "dp", pair_bit)
        far_a = swap(over_pair[:half], "tensor", 2)
        far_b = swap(over_x[half:], "dp", pair_bit)
        four = jnp.concatenate([rows, over_x, over_pair, far_a, far_b], axis=0)
        return jnp.concatenate([four, swap(four, "tensor", 1)], axis=0)

    def scatter_eight(partial):
        rows = partial.shape[0] // 8
        half = rows // 2
        arrived = swap(partial[4 * rows :], "tensor", 1)
        four = partial[: 4 * rows].astype(f32) + arrived.astype(f32)
        own, to_x, to_pair, far = jnp.split(four, 4, axis=0)
        far_low = far.astype(bf16)
        far_x = swap(far_low[:half], "tensor", 2)
        far_pair = swap(far_low[half:], "dp", pair_bit)
        to_pair = jnp.concatenate([to_pair[:half] + far_x.astype(f32), to_pair[half:]], axis=0)
        to_x = jnp.concatenate([to_x[:half], to_x[half:] + far_pair.astype(f32)], axis=0)
        from_x = swap(to_x.astype(bf16), "tensor", 2)
        from_pair = swap(to_pair.astype(bf16), "dp", pair_bit)
        return own + from_x.astype(f32) + from_pair.astype(f32)

    def local(
        block_input,
        segment_ids,
        gain_attn,
        w_query,
        b_query,
        w_keyval,
        b_keyval,
        w_out,
        gain_ffn,
        w_gate,
        w_up,
        w_down,
        cotangent,
    ):
        dp_index = lax.axis_index("dp")
        tensor_index = lax.axis_index("tensor")
        seq_length = segment_ids.shape[1]
        local_heads = b_query.shape[0] // HD
        head_kv = tensor_index * local_heads // (HQ // KV)
        is_value = tensor_index % 2
        kv_column = is_value * (KV * HD) + head_kv * HD
        width = local_heads * HD
        all_masks = masks_of(dp_bits)
        ring_codes = [mask | low for mask in masks_of(ring_bits) for low in (0, pair_bit)]

        def twist_all(array, back=False):
            return twist(array, 1, dp_index, all_masks, dp_size - 1, back)

        def twist_ring(array, back=False):
            return twist(array, 1, dp_index, ring_codes, ring_mask, back)

        def token_order(array, back=False):
            return twist(array, 0, tensor_index, token_codes, 3, back)

        keyval_cols = lax.dynamic_slice_in_dim(w_keyval, kv_column, HD, 1)
        qkv_w = gather_rows(jnp.concatenate([w_query, keyval_cols], axis=1), dp_bits)
        out_wt = gather_rows(w_out.T, dp_bits)

        pair_flag = (dp_index & pair_bit) != 0

        def ffn_rows(shard):
            half = shard.shape[1] // 2
            low, high = shard[:, :half], shard[:, half:]
            mine = jnp.where(pair_flag, high, low)
            theirs = swap(jnp.where(pair_flag, low, high), "dp", pair_bit)
            piece = jnp.concatenate(
                [jnp.where(pair_flag, theirs, mine), jnp.where(pair_flag, mine, theirs)], axis=0
            )
            return gather_rows(piece, ring_bits)

        gate_w = ffn_rows(w_gate)
        up_w = ffn_rows(w_up)
        down_wt = ffn_rows(w_down.T)

        rows_float = block_input.astype(f32)
        normed_one, scale_one = norm_forward(rows_float)
        act_one = gather_four(twist_all((normed_one * gain_attn).astype(bf16)))
        qkv_bias = jnp.concatenate([b_query, lax.dynamic_slice_in_dim(b_keyval, kv_column, HD, 0)])
        qkv = token_order(dot(act_one, qkv_w, 1, 0) + qkv_bias, back=True)
        cosine_table, sine_table = rotary(positions_of(segment_ids[0]))
        cos_heads = cosine_table[:, None, :]
        sin_heads = sine_table[:, None, :]
        query_rot = turn(
            qkv[:, :width].reshape(seq_length, local_heads, HD), cos_heads, sin_heads
        ).astype(bf16)
        kv_part = qkv[:, width:]
        kv_own = jnp.where(is_value == 1, kv_part, turn(kv_part, cosine_table, sine_table)).astype(
            bf16
        )
        kv_other = swap(kv_own, "tensor", 1)
        key_rot = jnp.where(is_value == 1, kv_other, kv_own)
        value_rows = jnp.where(is_value == 1, kv_own, kv_other)

        allowed = allowed_of(segment_ids[0])[None]
        raw_scores = jnp.einsum(
            "qhd,kd->hqk", query_rot, key_rot, preferred_element_type=f32
        ) / math.sqrt(HD)
        scores = jnp.where(allowed, raw_scores, masked_score)
        row_max = jnp.max(scores, axis=2, keepdims=True)
        log_total = row_max + jnp.log(jnp.sum(jnp.exp(scores - row_max), axis=2, keepdims=True))
        attn_probs = jnp.exp(scores - log_total)
        probs_low = attn_probs.astype(bf16)
        attn_result = jnp.einsum("hqk,kd->qhd", probs_low, value_rows, preferred_element_type=f32)
        context = token_order(attn_result.reshape(seq_length, width).astype(bf16))
        hidden = rows_float + twist_all(
            scatter_four(dot(context, out_wt, 1, 1, bf16)), back=True
        )

        normed_two, scale_two = norm_forward(hidden)
        act_two = gather_eight(twist_ring((normed_two * gain_ffn).astype(bf16)))
        cot_rows = gather_eight(twist_ring(cotangent))
        gate_pre = dot(act_two, gate_w, 1, 0)
        up_part = dot(act_two, up_w, 1, 0)
        sigmoid_gate = jax.nn.sigmoid(gate_pre)
        silu_gate = gate_pre * sigmoid_gate
        mixed_rows = (silu_gate * up_part).astype(bf16)
        grad_mixed = dot(cot_rows, down_wt, 1, 0)
        grad_gate = (
            grad_mixed * up_part * sigmoid_gate * (1.0 + gate_pre * (1.0 - sigmoid_gate))
        ).astype(bf16)
        grad_up = (grad_mixed * silu_gate).astype(bf16)
        grad_act_two = twist_ring(
            scatter_eight((dot(grad_gate, gate_w, 1, 1) + dot(grad_up, up_w, 1, 1)).astype(bf16)),
            back=True,
        )
        block_out = (
            hidden
            + twist_ring(scatter_eight(dot(mixed_rows, down_wt, 1, 1, bf16)), back=True)
        ).astype(bf16)
        back_two, gain_two = norm_backward(grad_act_two, normed_two, scale_two, gain_ffn)
        grad_hidden = cotangent.astype(f32) + back_two

        def ffn_grad(grad_rows_w):
            own = scatter_rows(grad_rows_w, ring_bits).astype(bf16)
            low, high = jnp.split(own, 2, axis=0)
            mine = jnp.where(pair_flag, high, low)
            theirs = swap(jnp.where(pair_flag, low, high), "dp", pair_bit)
            return jnp.concatenate(
                [jnp.where(pair_flag, theirs, mine), jnp.where(pair_flag, mine, theirs)], axis=1
            ).astype(f32)

        down_share = ffn_grad(dot(cot_rows, mixed_rows, 0, 0, bf16)).T
        gate_share = ffn_grad(dot(act_two, grad_gate, 0, 0, bf16))
        up_share = ffn_grad(dot(act_two, grad_up, 0, 0, bf16))

        grad_attn = gather_four(twist_all(grad_hidden.astype(bf16)))
        out_share = scatter_rows(dot(grad_attn, context, 0, 0, bf16), dp_bits).T
        grad_context = token_order(dot(grad_attn, out_wt, 1, 0, bf16), back=True).reshape(
            seq_length, local_heads, HD
        )
        grad_probs = jnp.einsum("qhd,kd->hqk", grad_context, value_rows, preferred_element_type=f32)
        row_delta = jnp.sum(grad_context.astype(f32) * attn_result, axis=2).T[:, :, None]
        grad_scores = (attn_probs * (grad_probs - row_delta)).astype(bf16)
        grad_query_rot = jnp.einsum(
            "hqk,kd->qhd", grad_scores, key_rot, preferred_element_type=f32
        ) / math.sqrt(HD)
        grad_key_rot = jnp.einsum(
            "hqk,qhd->kd", grad_scores, query_rot, preferred_element_type=f32
        ) / math.sqrt(HD)
        grad_value = jnp.einsum("hqk,qhd->kd", probs_low, grad_context, preferred_element_type=f32)
        grad_query = turn(grad_query_rot, cos_heads, -sin_heads).reshape(seq_length, width)
        grad_key = turn(grad_key_rot, cosine_table, -sine_table)

        kv_sent = swap(jnp.where(is_value == 1, grad_key, grad_value).astype(bf16), "tensor", 1)
        kv_kept = jnp.where(is_value == 1, grad_value, grad_key)
        kv_total = (kv_kept + kv_sent.astype(f32)).astype(bf16)
        grad_qkv = token_order(jnp.concatenate([grad_query.astype(bf16), kv_total], axis=1))
        grad_act_one = twist_all(scatter_four(dot(grad_qkv, qkv_w, 1, 1, bf16)), back=True)
        back_one, gain_one = norm_backward(grad_act_one, normed_one, scale_one, gain_attn)
        grad_rows = (grad_hidden + back_one).astype(bf16)

        qkv_share = scatter_rows(dot(act_one, grad_qkv, 0, 0, bf16), dp_bits)
        query_share = qkv_share[:, :width]
        kv_rows = qkv_share[:, width:]
        share_rows = kv_rows.shape[0] // tensor_size
        keyval_share = jnp.zeros((share_rows, 2 * KV * HD), f32)
        for mask in range(tensor_size):
            block = lax.dynamic_slice_in_dim(
                kv_rows, (tensor_index ^ mask) * share_rows, share_rows, 0
            )
            if mask:
                block = swap(block, "tensor", mask)
            sender = tensor_index ^ mask
            column = (sender % 2) * (KV * HD) + (sender * local_heads // (HQ // KV)) * HD
            keyval_share = lax.dynamic_update_slice_in_dim(keyval_share, block, column, 1)

        bias_keyval = jnp.zeros((2 * KV * HD,), f32)
        bias_keyval = lax.dynamic_update_slice_in_dim(
            bias_keyval, jnp.sum(grad_key, axis=0), head_kv * HD, 0
        )
        bias_keyval = lax.dynamic_update_slice_in_dim(
            bias_keyval, jnp.sum(grad_value, axis=0), KV * HD + head_kv * HD, 0
        )
        bias_query = lax.dynamic_update_slice_in_dim(
            jnp.zeros((HQ * HD,), f32), jnp.sum(grad_query, axis=0), tensor_index * width, 0
        )
        devices = dp_size * tensor_size
        sizes = [part.shape[0] // devices for part in (gain_one, gain_two, bias_query, bias_keyval)]
        small = jnp.concatenate(
            [part.reshape(devices, -1) for part in (gain_one, gain_two, bias_query, bias_keyval)],
            axis=1,
        )
        small = lax.all_to_all(small, ("dp", "tensor"), 0, 0, tiled=True)
        small = jnp.sum(small, axis=0)
        ends = [sum(sizes[: at + 1]) for at in range(4)]
        gain_one_share = small[: ends[0]]
        gain_two_share = small[ends[0] : ends[1]]
        query_bias_share = small[ends[1] : ends[2]]
        keyval_bias_share = small[ends[2] :]
        return (
            block_out,
            grad_rows,
            gain_one_share,
            query_share,
            query_bias_share,
            keyval_share,
            keyval_bias_share,
            out_share,
            gain_two_share,
            gate_share,
            up_share,
            down_share,
        )

    placed = (
        P(("dp", "tensor"), None),
        P("dp", None),
        P(),
        P("dp", "tensor"),
        P("tensor"),
        P("dp", None),
        P(),
        P("tensor", "dp"),
        P(),
        P("dp", "tensor"),
        P("dp", "tensor"),
        P("tensor", "dp"),
        P(("dp", "tensor"), None),
    )
    return jax.shard_map(
        local,
        mesh=mesh,
        in_specs=placed,
        out_specs=(
            P(("dp", "tensor"), None),
            P(("dp", "tensor"), None),
            P(("dp", "tensor")),
            P("dp", "tensor"),
            P(("dp", "tensor")),
            P(("dp", "tensor"), None),
            P(("dp", "tensor")),
            P("tensor", "dp"),
            P(("dp", "tensor")),
            P("dp", "tensor"),
            P("dp", "tensor"),
            P("tensor", "dp"),
        ),
        check_vma=False,
    )
```

```python
import math

import jax
import jax.numpy as jnp
from jax import lax
from jax.experimental import pallas as pl
from jax.experimental.pallas import tpu as pltpu
from jax.sharding import PartitionSpec as P

HQ = 12
KV = 2
HD = 128


epsilon = 1e-06
rope_base = 1000000.0
masked_score = -1e30
bf16 = jnp.bfloat16
f32 = jnp.float32


def positions_of(segment_row):
    index_row = jnp.arange(segment_row.shape[0], dtype=jnp.int32)
    starts = jnp.concatenate(
        [jnp.ones((1,), jnp.int32), (segment_row[1:] != segment_row[:-1]).astype(jnp.int32)]
    )
    first_index = lax.cummax(jnp.where(starts > 0, index_row, 0), axis=0)
    return index_row - first_index


def rotary(positions):
    inverse = rope_base ** (-(jnp.arange(HD // 2, dtype=jnp.float32) * 2.0 / HD))
    angles = positions.astype(jnp.float32)[:, None] * inverse[None, :]
    angles = jnp.concatenate([angles, angles], axis=1)
    return (jnp.cos(angles), jnp.sin(angles))


def norm_forward(values_in):
    row_scale = lax.rsqrt(jnp.mean(values_in * values_in, axis=-1, keepdims=True) + epsilon)
    return (values_in * row_scale, row_scale)


def norm_backward(grad_out, normed, row_scale, gain_vec):
    grad_normed = grad_out * gain_vec
    grad_in = row_scale * (
        grad_normed - normed * jnp.mean(grad_normed * normed, axis=-1, keepdims=True)
    )
    return (grad_in, jnp.sum(grad_out * normed, axis=0))


ANY = pl.BlockSpec(memory_space=pl.ANY)
WHOLE = pl.BlockSpec(memory_space=pltpu.VMEM)
SCALARS = pl.BlockSpec(memory_space=pltpu.SMEM)


def made(jobs, sems, first=0):
    return [
        pltpu.make_async_copy(src, dst, sems.at[first + at]) for at, (src, dst) in enumerate(jobs)
    ]


def start_all(jobs, sems):
    copies = made(jobs, sems)
    for copy in copies:
        copy.start()
    return copies


def wait_all(copies):
    for copy in copies:
        copy.wait()


def block(ref, at, rows):
    return ref.at[pl.ds(pl.multiple_of(at * rows, rows), rows)]


def turned(values, cosine, sine, sign):
    return values * cosine + sign * (pltpu.roll(values, HD // 2, 1) * sine)


def mm(left, right):
    return lax.dot_general(left, right, (((1,), (0,)), ((), ())), preferred_element_type=f32)


def mm_nt(left, right):
    return lax.dot_general(left, right, (((1,), (1,)), ((), ())), preferred_element_type=f32)


def mm_tn(left, right):
    return lax.dot_general(left, right, (((0,), (0,)), ((), ())), preferred_element_type=f32)


def hold(due, release):
    out = lax.optimization_barrier((tuple(due), tuple(release)))
    return out[1]


def section(body):
    outs = jax.eval_shape(body)
    return lax.cond(
        lax.optimization_barrier(jnp.bool_(True)),
        body,
        lambda: jax.tree.map(lambda out: jnp.zeros(out.shape, out.dtype), outs),
    )


def solution(mesh):
    dp_size = mesh.shape["dp"]
    tensor_size = mesh.shape["tensor"]
    pair_bit = 2
    far_bits = []
    bit = dp_size // 2
    while bit > pair_bit:
        far_bits.append(bit)
        bit //= 2
    ring_bits = far_bits + [1]

    def swap(array, axis, bit):
        size = mesh.shape[axis]
        return lax.ppermute(array, axis, [(i, i ^ bit) for i in range(size)])

    def masks_of(bits):
        masks = [0]
        for bit in bits:
            masks = masks + [mask ^ bit for mask in masks]
        return masks

    def rows_of(*pieces):
        return jnp.concatenate(pieces, axis=0)

    def far_pieces(piece):
        pieces = [piece]
        for bit in far_bits:
            pieces = pieces + [swap(part, "dp", bit) for part in pieces]
        return pieces

    def fold(total, axis, bit):
        half = total.shape[0] // 2
        return total[:half], swap(total[half:].astype(bf16), axis, bit)

    def add(kept, arrived):
        return kept.astype(f32) + arrived.astype(f32)

    ring_masks = masks_of(ring_bits)
    ring_mask = sum(ring_bits)
    count = len(ring_masks)


    def ffn_jobs(dp_index, refs, offsets, held):
        rows = held.shape[0] // dp_size
        jobs = []
        for mask, ref, offset in zip(ring_masks, refs, offsets):
            base = jnp.bitwise_xor(jnp.bitwise_and(dp_index, ring_mask), mask)
            for low in (0, 1):
                jobs.append(
                    (
                        ref.at[pl.ds(offset + low * rows, rows)],
                        block(held, base + low * pair_bit, rows),
                    )
                )
        return jobs

    def row_jobs(refs, held):
        jobs, start = [], 0
        for ref in refs:
            jobs.append((ref, held.at[pl.ds(start, ref.shape[0])]))
            start += ref.shape[0]
        return jobs

    def attn_jobs(dp_index, refs, pieces, held):
        rows = held.shape[0] // dp_size
        return [
            (
                ref.at[pl.ds(first, rows)],
                block(held, jnp.bitwise_xor(dp_index, mask), rows),
            )
            for ref, (_, first, mask) in zip(refs, pieces)
        ]

    def arrays_of(pieces):
        return [piece[0] for piece in pieces]

    token_masks = ((0, 2), (1, 3))

    def token_jobs(tensor_index, pair, other, held):
        rows = held.shape[0] // 4
        jobs = []
        for masks, ref in zip(token_masks, (pair, other)):
            for at, mask in enumerate(masks):
                spot = jnp.bitwise_xor(tensor_index, mask)
                jobs.append((ref.at[pl.ds(at * rows, rows)], block(held, spot, rows)))
        return jobs

    def back(jobs):
        return [(dst, src) for src, dst in jobs]

    def ffn_up(scalars, pieces, gate_pieces, up_pieces):
        tokens, model = sum(piece.shape[0] for piece in pieces), pieces[0].shape[1]
        units = gate_pieces[0][0].shape[1]
        rows = tokens // 2
        many = len(pieces)
        early = 2

        def kernel(scal, *refs):
            parts = refs[:many]
            gates = refs[many : many + count]
            ups = refs[many + count : many + 2 * count]
            acts_ref, mixed_ref, silu_ref, back_ref, acts, gate_w, up_w, sems = refs[
                many + 2 * count :
            ]
            jobs = row_jobs(parts, acts)
            gate_jobs = ffn_jobs(scal[0], gates, [at for _, at in gate_pieces], gate_w)
            up_jobs = ffn_jobs(scal[0], ups, [at for _, at in up_pieces], up_w)
            step = pl.program_id(0)

            @pl.when(step == 0)
            def _():
                copies = start_all(jobs[:early] + gate_jobs + jobs[early:] + up_jobs, sems)
                wait_all(copies[: early + 2 * count])

            @pl.when(step == 1)
            def _():
                wait_all(made(jobs[early:], sems, early + 2 * count))

            spot = pl.ds(pl.multiple_of(step * rows, rows), rows)
            rows_in = acts[spot, :]
            acts_ref[...] = rows_in
            gate = mm(rows_in, gate_w[...])

            @pl.when(step == 0)
            def _():
                wait_all(made(up_jobs, sems, many + 2 * count))

            up = mm(rows_in, up_w[...])
            sig = jax.nn.sigmoid(gate)
            silu = gate * sig
            mixed_ref[...] = (silu * up).astype(bf16)
            silu_ref[...] = silu.astype(bf16)
            back_ref[...] = (up * sig * (1.0 + gate * (1.0 - sig))).astype(bf16)

        out = jax.ShapeDtypeStruct((tokens, units), bf16)
        spec = pl.BlockSpec((rows, units), lambda i: (i, 0))
        return pl.pallas_call(
            kernel,
            grid=(2,),
            in_specs=[SCALARS] + [ANY] * (many + 2 * count),
            out_specs=[pl.BlockSpec((rows, model), lambda i: (i, 0))] + [spec] * 3,
            out_shape=[jax.ShapeDtypeStruct((tokens, model), bf16)] + [out] * 3,
            scratch_shapes=[
                pltpu.VMEM((tokens, model), bf16),
                pltpu.VMEM((model, units), bf16),
                pltpu.VMEM((model, units), bf16),
                pltpu.SemaphoreType.DMA((many + 4 * count,)),
            ],
            name="ffn_up",
        )(
            scalars,
            *pieces,
            *[ref for ref, _ in gate_pieces],
            *[ref for ref, _ in up_pieces],
        )

    def ffn_back(scalars, cots, down_pieces, gate_pieces, up_pieces, silu, back_part):
        many = len(cots)
        tokens, model = sum(piece.shape[0] for piece in cots), cots[0].shape[1]
        units = silu.shape[1]
        rows = tokens // 2
        lists = (down_pieces, gate_pieces, up_pieces)

        def kernel(scal, *refs):
            parts = refs[:many]
            pieces = [refs[many + at * count : many + (at + 1) * count] for at in range(3)]
            silu_ref, back_ref, grad_gate_ref, grad_up_ref, out_ref = refs[
                many + 3 * count : many + 3 * count + 5
            ]
            cot, *held = refs[many + 3 * count + 5 : -1]
            sems = refs[-1]
            jobs = row_jobs(parts, cot)
            for at in range(3):
                jobs += ffn_jobs(scal[0], pieces[at], [spot for _, spot in lists[at]], held[at])
            first = pl.program_id(0) == 0
            early = many + 2 * count

            @pl.when(first)
            def _():
                wait_all(start_all(jobs, sems)[:early])

            spot = pl.ds(pl.multiple_of(pl.program_id(0) * rows, rows), rows)
            grad_mixed = mm(cot[spot, :], held[0][...])
            grad_gate = (grad_mixed * back_ref[...].astype(f32)).astype(bf16)
            grad_up = (grad_mixed * silu_ref[...].astype(f32)).astype(bf16)
            grad_gate_ref[...] = grad_gate
            grad_up_ref[...] = grad_up

            @pl.when(first)
            def _():
                wait_all(made(jobs[early:], sems, early))

            out_ref[...] = (
                mm_nt(grad_gate, held[1][...]) + mm_nt(grad_up, held[2][...])
            ).astype(bf16)

        out = jax.ShapeDtypeStruct((tokens, units), bf16)
        spec = pl.BlockSpec((rows, units), lambda i: (i, 0))
        wide = pl.BlockSpec((rows, model), lambda i: (i, 0))
        return pl.pallas_call(
            kernel,
            grid=(2,),
            in_specs=[SCALARS] + [ANY] * (many + 3 * count) + [spec, spec],
            out_specs=[spec, spec, wide],
            out_shape=[out, out, jax.ShapeDtypeStruct((tokens, model), bf16)],
            scratch_shapes=[pltpu.VMEM((tokens, model), bf16)]
            + [pltpu.VMEM((model, units), bf16)] * 3
            + [pltpu.SemaphoreType.DMA((many + 6 * count,))],
            name="ffn_back",
        )(scalars, *cots, *[ref for pieces in lists for ref, _ in pieces], silu, back_part)

    def ffn_rows(scalars, left, pieces, model, name):
        tokens, units = left.shape
        rows = tokens // 2

        def kernel(scal, left_ref, *refs):
            parts = refs[:count]
            out_ref, held, sems = refs[count:]

            @pl.when(pl.program_id(0) == 0)
            def _():
                wait_all(
                    start_all(ffn_jobs(scal[0], parts, [at for _, at in pieces], held), sems)
                )

            out_ref[...] = mm_nt(left_ref[...], held[...]).astype(bf16)

        return pl.pallas_call(
            kernel,
            grid=(2,),
            in_specs=[SCALARS, pl.BlockSpec((rows, units), lambda i: (i, 0))] + [ANY] * count,
            out_specs=pl.BlockSpec((rows, model), lambda i: (i, 0)),
            out_shape=jax.ShapeDtypeStruct((tokens, model), bf16),
            scratch_shapes=[
                pltpu.VMEM((model, units), bf16),
                pltpu.SemaphoreType.DMA((2 * count,)),
            ],
            name=name,
        )(scalars, left, *[ref for ref, _ in pieces])

    def ffn_grad(scalars, own_pieces, core_pieces, low, high, name):
        pieces = [*own_pieces, *core_pieces]
        many = len(own_pieces)
        tokens, model = low.shape[0], pieces[0].shape[1]
        units = low.shape[1]
        shard = model // dp_size
        wide = 384
        groups = wide // (2 * shard)

        def kernel(scal, *refs):
            def stack(parts):
                values = [part[...] for part in parts]
                return values[0] if len(values) == 1 else jnp.concatenate(values, axis=0)

            low_ref, high_ref, kept_ref, sent_ref = refs[2 * many :]
            total = mm_tn(stack(refs[:many]), low_ref[...])
            total = total + mm_tn(stack(refs[many : 2 * many]), high_ref[...])
            total = total.astype(bf16)
            odd = jnp.bitwise_and(scal[0], 1) == 1
            for group in range(groups):
                first = total[group * 2 * shard : group * 2 * shard + shard]
                second = total[group * 2 * shard + shard : (group + 1) * 2 * shard]
                spot = pl.ds(group * shard, shard)
                kept_ref[spot, :] = jnp.where(odd, second, first)
                sent_ref[spot, :] = jnp.where(odd, first, second)

        out = jax.ShapeDtypeStruct((model // 2, units), bf16)
        spec = pl.BlockSpec((wide // 2, units), lambda i: (i, 0))
        whole = pl.BlockSpec((tokens, units), lambda i: (0, 0))
        return pl.pallas_call(
            kernel,
            grid=(model // wide,),
            in_specs=[SCALARS]
            + [pl.BlockSpec((piece.shape[0], wide), lambda i: (0, i)) for piece in pieces]
            + [whole, whole],
            out_specs=[spec] * 2,
            out_shape=[out] * 2,
            name=name,
        )(scalars, *pieces, low, high)

    def is_high(scal, bit):
        return jnp.bitwise_and(scal[0], bit) != 0

    def whole_call(kernel, outs, name, *args):
        return pl.pallas_call(
            kernel,
            in_specs=[SCALARS] + [WHOLE] * (len(args) - 1),
            out_specs=[WHOLE] * len(outs),
            out_shape=[jax.ShapeDtypeStruct(shape, kind) for shape, kind in outs],
            name=name,
        )(*args)

    def split_cols(scalars, *arrays):
        rows, half = arrays[0].shape[0], arrays[0].shape[1] // 2
        wide = -(-half // 128) * 128
        many = len(arrays)

        def kernel(scal, *refs):
            mine_ref, sent_ref = refs[many:]
            flag = is_high(scal, pair_bit)
            mine_ref[...] = jnp.zeros_like(mine_ref)
            sent_ref[...] = jnp.zeros_like(sent_ref)
            for at in range(many):
                low, high = refs[at][:, :half], refs[at][:, half:]
                mine_ref[at * rows : (at + 1) * rows, :half] = jnp.where(flag, high, low)
                sent_ref[at * rows : (at + 1) * rows, :half] = jnp.where(flag, low, high)

        return whole_call(
            kernel, [((many * rows, wide), bf16)] * 2, "split_cols", scalars, *arrays
        )

    def join_rows(scalars, mine, theirs, at, many):
        rows, columns = mine.shape[0] // many, mine.shape[1]
        spot = pl.ds(at * rows, rows)

        def kernel(scal, mine_ref, theirs_ref, out_ref):
            flag = is_high(scal, pair_bit)
            out_ref[:rows, :] = jnp.where(flag, theirs_ref[spot, :], mine_ref[spot, :])
            out_ref[rows:, :] = jnp.where(flag, mine_ref[spot, :], theirs_ref[spot, :])

        return whole_call(
            kernel, [((2 * rows, columns), bf16)], "join_rows", scalars, mine, theirs
        )[0]

    def join_cols(scalars, mine, theirs, columns):
        rows = mine.shape[0]

        def kernel(scal, mine_ref, theirs_ref, out_ref):
            flag = is_high(scal, pair_bit)
            mine = mine_ref[:, :columns].astype(f32)
            theirs = theirs_ref[:, :columns].astype(f32)
            out_ref[:, :columns] = jnp.where(flag, theirs, mine)
            out_ref[:, columns:] = jnp.where(flag, mine, theirs)

        return whole_call(
            kernel, [((rows, 2 * columns), f32)], "join_cols", scalars, mine, theirs
        )[0]

    def fold_sum(scalars, kept, arrived, bit, outer):
        rows, columns = kept.shape[0] // 2, kept.shape[1]
        part = rows // outer

        def kernel(scal, kept_ref, arrived_ref, own_ref, sent_ref):
            flag = is_high(scal, bit)
            for at in range(outer):
                first = pl.ds(2 * at * part, part)
                second = pl.ds((2 * at + 1) * part, part)
                low = kept_ref[first, :].astype(f32) + arrived_ref[first, :].astype(f32)
                high = kept_ref[second, :].astype(f32) + arrived_ref[second, :].astype(f32)
                spot = pl.ds(at * part, part)
                own_ref[spot, :] = jnp.where(flag, high, low).astype(bf16)
                sent_ref[spot, :] = jnp.where(flag, low, high).astype(bf16)

        return whole_call(
            kernel, [((rows, columns), bf16)] * 2, "fold_sum", scalars, kept, arrived
        )

    def fold_fixed(scalars, kept, arrived, keep, give_away):
        many = len(keep) + len(give_away)
        rows, columns = kept.shape[0] // many, kept.shape[1]

        def kernel(scal, kept_ref, arrived_ref, own_ref, sent_ref):
            for blocks, ref in ((keep, own_ref), (give_away, sent_ref)):
                for at, spot in enumerate(blocks):
                    spot = pl.ds(spot * rows, rows)
                    ref[at * rows : (at + 1) * rows, :] = (
                        kept_ref[spot, :].astype(f32) + arrived_ref[spot, :].astype(f32)
                    ).astype(ref.dtype)

        outs = [((len(keep) * rows, columns), f32), ((len(give_away) * rows, columns), bf16)]
        return whole_call(kernel, outs, "fold_fixed", scalars, kept, arrived)

    def norm_two(scalars, rows_in, own, arrived, gain):
        def kernel(scal, in_ref, own_ref, arrived_ref, gain_ref, hidden_ref, out_ref):
            hidden = in_ref[...].astype(f32) + own_ref[...] + arrived_ref[...].astype(f32)
            hidden_ref[...] = hidden
            out_ref[...] = (norm_forward(hidden)[0] * gain_ref[...]).astype(bf16)

        outs = [(rows_in.shape, f32), (rows_in.shape, bf16)]
        return whole_call(kernel, outs, "norm_two", scalars, rows_in, own, arrived, gain)

    def norm_one_back(scalars, rows_in, own, arrived, gain, given):
        def kernel(scal, in_ref, own_ref, arrived_ref, gain_ref, given_ref, out_ref):
            grad_out = own_ref[...] + arrived_ref[...].astype(f32)
            normed, row_scale = norm_forward(in_ref[...].astype(f32))
            grad_normed = grad_out * gain_ref[...]
            grad_in = row_scale * (
                grad_normed - normed * jnp.mean(grad_normed * normed, axis=-1, keepdims=True)
            )
            out_ref[...] = (given_ref[...] + grad_in).astype(bf16)

        return whole_call(
            kernel, [(rows_in.shape, bf16)], "norm_one_back", scalars, rows_in, own, arrived, gain, given
        )[0]

    def join_both(scalars, first, mine, theirs):
        rows, columns = mine.shape[0] // 2, mine.shape[1]

        def kernel(scal, first_ref, mine_ref, theirs_ref, out_ref, both_ref):
            flag = is_high(scal, pair_bit)
            low = jnp.where(flag, theirs_ref[:rows, :], mine_ref[:rows, :])
            high = jnp.where(flag, mine_ref[:rows, :], theirs_ref[:rows, :])
            out_ref[:rows, :] = low
            out_ref[rows:, :] = high
            both_ref[: 2 * rows, :] = first_ref[...]
            both_ref[2 * rows : 3 * rows, :] = low
            both_ref[3 * rows :, :] = high

        return whole_call(
            kernel,
            [((2 * rows, columns), bf16), ((4 * rows, columns), bf16)],
            "join_both", scalars, first, mine, theirs,
        )

    def spread_eight(scalars, kept, arrived):
        rows, model = kept.shape[0] // 4, kept.shape[1]
        half = rows // 2

        def kernel(scal, kept_ref, arrived_ref, own_ref, x_ref, l_ref, far_a_ref, far_b_ref):
            for at, ref in enumerate((own_ref, x_ref, l_ref)):
                spot = pl.ds(at * rows, rows)
                ref[...] = kept_ref[spot, :].astype(f32) + arrived_ref[spot, :].astype(f32)
            for at, ref in enumerate((far_a_ref, far_b_ref)):
                spot = pl.ds(3 * rows + at * half, half)
                ref[...] = (
                    kept_ref[spot, :].astype(f32) + arrived_ref[spot, :].astype(f32)
                ).astype(bf16)

        outs = [((rows, model), f32)] * 3 + [((half, model), bf16)] * 2
        return whole_call(kernel, outs, "spread_eight", scalars, kept, arrived)

    def spread_two(scalars, to_x, to_l, far_x, far_l):
        rows, model = to_x.shape
        half = rows // 2

        def kernel(scal, x_ref, l_ref, far_x_ref, far_l_ref, out_x_ref, out_l_ref):
            out_x_ref[:half, :] = x_ref[:half, :].astype(bf16)
            out_x_ref[half:, :] = (x_ref[half:, :] + far_l_ref[...].astype(f32)).astype(bf16)
            out_l_ref[:half, :] = (l_ref[:half, :] + far_x_ref[...].astype(f32)).astype(bf16)
            out_l_ref[half:, :] = l_ref[half:, :].astype(bf16)

        return whole_call(
            kernel, [((rows, model), bf16)] * 2, "spread_two", scalars, to_x, to_l, far_x, far_l
        )

    def give(total, scal, kept_ref, sent_ref):
        part = total.shape[0] // dp_size
        flag = is_high(scal, 1)
        for at in range(total.shape[0] // (2 * part)):
            low = total[2 * at * part : (2 * at + 1) * part]
            high = total[(2 * at + 1) * part : (2 * at + 2) * part]
            kept_ref[pl.ds(at * part, part), :] = jnp.where(flag, high, low)
            sent_ref[pl.ds(at * part, part), :] = jnp.where(flag, low, high)

    def project(scalars, pair, core, pieces, bias, cosine, sine):
        tokens, model = 2 * pair.shape[0], pair.shape[1]
        columns = pieces[0][0].shape[1]
        width = columns - HD

        def kernel(scal, pair_ref, core_ref, bias_ref, cos_ref, sin_ref, *refs):
            query_ref, kv_ref, acts, held, sems = refs[dp_size:]
            wait_all(
                start_all(
                    attn_jobs(scal[0], refs[:dp_size], pieces, held)
                    + token_jobs(scal[1], pair_ref, core_ref, acts),
                    sems,
                )
            )
            is_value = jnp.bitwise_and(scal[1], 1) == 1
            rows = tokens // 4
            for at in range(4):
                spot = pl.ds(at * rows, rows)
                out = mm(acts[spot, :], held[...]) + bias_ref[...]
                cosine_rows, sine_rows = cos_ref[spot, :], sin_ref[spot, :]
                for head in range(width // HD):
                    query_ref[spot, head * HD : (head + 1) * HD] = turned(
                        out[:, head * HD : (head + 1) * HD], cosine_rows, sine_rows, 1.0
                    ).astype(bf16)
                kv = out[:, width:]
                kv_ref[spot, :] = jnp.where(
                    is_value, kv, turned(kv, cosine_rows, sine_rows, 1.0)
                ).astype(bf16)

        return pl.pallas_call(
            kernel,
            in_specs=[SCALARS, ANY, ANY, WHOLE, WHOLE, WHOLE] + [ANY] * dp_size,
            out_specs=[WHOLE, WHOLE],
            out_shape=[
                jax.ShapeDtypeStruct((tokens, width), bf16),
                jax.ShapeDtypeStruct((tokens, HD), bf16),
            ],
            scratch_shapes=[
                pltpu.VMEM((tokens, model), bf16),
                pltpu.VMEM((model, columns), bf16),
                pltpu.SemaphoreType.DMA((dp_size + 4,)),
            ],
            name="project",
        )(scalars, pair, core, bias, cosine, sine, *arrays_of(pieces))

    def probabilities(query, keys, start_rows, first):
        scores = mm_nt(query, keys) * (1.0 / math.sqrt(HD))
        column = lax.broadcasted_iota(jnp.int32, scores.shape, 1)
        row = lax.broadcasted_iota(jnp.int32, scores.shape, 0) + first
        allowed = (column <= row) & (column >= start_rows)
        scores = jnp.where(allowed, scores, masked_score)
        top = jnp.max(scores, axis=1, keepdims=True)
        raised = jnp.exp(scores - top)
        return raised * (1.0 / jnp.sum(raised, axis=1, keepdims=True))

    def attend(scalars, query, kv_own, kv_other, starts):
        tokens, width = query.shape
        rows = tokens // 4

        def kernel(scal, query_ref, own_ref, other_ref, start_ref, context_ref):
            is_value = jnp.bitwise_and(scal[1], 1) == 1
            own, other = own_ref[...], other_ref[...]
            keys = jnp.where(is_value, other, own)
            values = jnp.where(is_value, own, other)
            for at in range(4):
                end = (at + 1) * rows
                spot = pl.ds(at * rows, rows)
                for head in range(width // HD):
                    lanes = slice(head * HD, (head + 1) * HD)
                    probs = probabilities(
                        query_ref[spot, lanes], keys[:end], start_ref[spot, :], at * rows
                    )
                    context_ref[spot, lanes] = mm(probs.astype(bf16), values[:end]).astype(bf16)

        return whole_call(
            kernel, [((tokens, width), bf16)], "attend", scalars, query, kv_own, kv_other, starts
        )[0]

    def out_rows(scalars, context, pieces, model):
        tokens, width = context.shape
        rows = tokens // 4

        def kernel(scal, context_ref, *refs):
            kept_ref, sent_ref, held, part, sems, out_sems = refs[dp_size:]
            wait_all(start_all(attn_jobs(scal[0], refs[:dp_size], pieces, held), sems))
            for at in range(4):
                spot = pl.ds(at * rows, rows)
                part[spot, :] = mm_nt(context_ref[spot, :], held[...]).astype(bf16)
            wait_all(start_all(back(token_jobs(scal[1], kept_ref, sent_ref, part)), out_sems))

        half = jax.ShapeDtypeStruct((tokens // 2, model), bf16)
        return pl.pallas_call(
            kernel,
            in_specs=[SCALARS, WHOLE] + [ANY] * dp_size,
            out_specs=[ANY, ANY],
            out_shape=[half, half],
            scratch_shapes=[
                pltpu.VMEM((model, width), bf16),
                pltpu.VMEM((tokens, model), bf16),
                pltpu.SemaphoreType.DMA((dp_size,)),
                pltpu.SemaphoreType.DMA((4,)),
            ],
            name="out_rows",
        )(scalars, context, *arrays_of(pieces))

    def attend_back(
        scalars, query, kv_own, kv_other, starts, pieces, pair, core, context, cosine, sine
    ):
        tokens, width = query.shape
        model = pair.shape[1]
        rows = tokens // 4
        scale = 1.0 / math.sqrt(HD)

        def kernel(
            scal, query_ref, own_ref, other_ref, start_ref, pair_ref, core_ref,
            context_ref, cos_ref, sin_ref, *refs,
        ):
            grad_query_ref, kv_kept_ref, kv_sent_ref, bias_ref, wout_ref, wout_sent_ref = refs[
                dp_size : dp_size + 6
            ]
            held, grads, grad_context, grad_key, grad_value, sems = refs[dp_size + 6 :]
            wait_all(
                start_all(
                    attn_jobs(scal[0], refs[:dp_size], pieces, held)
                    + token_jobs(scal[1], pair_ref, core_ref, grads),
                    sems,
                )
            )
            is_value = jnp.bitwise_and(scal[1], 1) == 1
            own, other = own_ref[...], other_ref[...]
            keys = jnp.where(is_value, other, own)
            values = jnp.where(is_value, own, other)
            for at in range(2):
                spot = pl.ds(at * 2 * rows, 2 * rows)
                grad_context[spot, :] = mm(grads[spot, :], held[...]).astype(bf16)
            give(mm_tn(grads[...], context_ref[...]).astype(bf16), scal, wout_ref, wout_sent_ref)
            grad_key[...] = jnp.zeros_like(grad_key)
            grad_value[...] = jnp.zeros_like(grad_value)
            bias_ref[...] = jnp.zeros_like(bias_ref)
            for at in range(4):
                end = (at + 1) * rows
                spot = pl.ds(at * rows, rows)
                upto = pl.ds(0, end)
                for head in range(width // HD):
                    lanes = slice(head * HD, (head + 1) * HD)
                    queries = query_ref[spot, lanes]
                    given = grad_context[spot, lanes]
                    probs = probabilities(queries, keys[:end], start_ref[spot, :], at * rows)
                    low = probs.astype(bf16)
                    grad_probs = mm_nt(given, values[:end])
                    delta = jnp.sum(low.astype(f32) * grad_probs, axis=1, keepdims=True)
                    grad_scores = (probs * (grad_probs - delta)).astype(bf16)
                    grad_query = turned(
                        mm(grad_scores, keys[:end]) * scale, cos_ref[spot, :], sin_ref[spot, :], -1.0
                    )
                    grad_query_ref[spot, lanes] = grad_query.astype(bf16)
                    bias_ref[0:1, lanes] += jnp.sum(grad_query, axis=0, keepdims=True)
                    grad_key[upto, :] += mm_tn(grad_scores, queries)
                    grad_value[upto, :] += mm_tn(low, given)
            grad_keys = turned(grad_key[...] * scale, cos_ref[...], sin_ref[...], -1.0)
            grad_values = grad_value[...]
            bias_ref[0:1, width : width + HD] = jnp.sum(grad_keys, axis=0, keepdims=True)
            bias_ref[0:1, width + HD :] = jnp.sum(grad_values, axis=0, keepdims=True)
            kv_kept_ref[...] = jnp.where(is_value, grad_values, grad_keys)
            kv_sent_ref[...] = jnp.where(is_value, grad_keys, grad_values).astype(bf16)

        return pl.pallas_call(
            kernel,
            in_specs=[SCALARS] + [WHOLE] * 4 + [ANY] * 2 + [WHOLE] * 3 + [ANY] * dp_size,
            out_specs=[WHOLE] * 6,
            out_shape=[
                jax.ShapeDtypeStruct((tokens, width), bf16),
                jax.ShapeDtypeStruct((tokens, HD), f32),
                jax.ShapeDtypeStruct((tokens, HD), bf16),
                jax.ShapeDtypeStruct((8, width + 2 * HD), f32),
                jax.ShapeDtypeStruct((model // 2, width), bf16),
                jax.ShapeDtypeStruct((model // 2, width), bf16),
            ],
            scratch_shapes=[
                pltpu.VMEM((model, width), bf16),
                pltpu.VMEM((tokens, model), bf16),
                pltpu.VMEM((tokens, width), bf16),
                pltpu.VMEM((tokens, HD), f32),
                pltpu.VMEM((tokens, HD), f32),
                pltpu.SemaphoreType.DMA((dp_size + 4,)),
            ],
            name="attend_back",
        )(
            scalars, query, kv_own, kv_other, starts, pair, core, context, cosine, sine,
            *arrays_of(pieces),
        )

    def project_back(scalars, grad_query, kv_kept, kv_arrived, pieces, pair, core):
        tokens, width = grad_query.shape
        model, columns = pair.shape[1], pieces[0][0].shape[1]
        rows = tokens // 4

        def kernel(
            scal, query_ref, kept_kv_ref, arrived_ref, pair_ref, core_ref, *refs
        ):
            (
                grads_ref, kept_ref, sent_ref, gain_ref, held, part, acts, sems, out_sems,
            ) = refs[dp_size:]
            copies = start_all(
                attn_jobs(scal[0], refs[:dp_size], pieces, held)
                + token_jobs(scal[1], pair_ref, core_ref, acts),
                sems,
            )
            grads_ref[:, :width] = query_ref[...]
            grads_ref[:, width:] = (kept_kv_ref[...] + arrived_ref[...].astype(f32)).astype(bf16)
            wait_all(copies)
            for at in range(4):
                spot = pl.ds(at * rows, rows)
                part[spot, :] = mm_nt(grads_ref[spot, :], held[...]).astype(bf16)
            copies = start_all(back(token_jobs(scal[1], kept_ref, sent_ref, part)), out_sems)
            gain_ref[...] = jnp.zeros_like(gain_ref)
            for at in range(8):
                spot = pl.ds(at * rows // 2, rows // 2)
                gain_ref[0:1, :] += jnp.sum(
                    part[spot, :].astype(f32) * acts[spot, :].astype(f32), axis=0, keepdims=True
                )
            wait_all(copies)

        half = jax.ShapeDtypeStruct((tokens // 2, model), bf16)
        return pl.pallas_call(
            kernel,
            in_specs=[SCALARS, WHOLE, WHOLE, WHOLE, ANY, ANY] + [ANY] * dp_size,
            out_specs=[WHOLE, ANY, ANY, WHOLE],
            out_shape=[
                jax.ShapeDtypeStruct((tokens, columns), bf16),
                half,
                half,
                jax.ShapeDtypeStruct((8, model), f32),
            ],
            scratch_shapes=[
                pltpu.VMEM((model, columns), bf16),
                pltpu.VMEM((tokens, model), bf16),
                pltpu.VMEM((tokens, model), bf16),
                pltpu.SemaphoreType.DMA((dp_size + 4,)),
                pltpu.SemaphoreType.DMA((4,)),
            ],
            name="project_back",
        )(scalars, grad_query, kv_kept, kv_arrived, pair, core, *arrays_of(pieces))

    def project_grad(scalars, pair, core, grads):
        tokens, columns = grads.shape
        model = pair.shape[1]

        def kernel(scal, pair_ref, core_ref, grads_ref, kept_ref, sent_ref, acts, sems):
            wait_all(start_all(token_jobs(scal[1], pair_ref, core_ref, acts), sems))
            give(mm_tn(acts[...], grads_ref[...]).astype(bf16), scal, kept_ref, sent_ref)

        return pl.pallas_call(
            kernel,
            in_specs=[SCALARS, ANY, ANY, WHOLE],
            out_specs=[WHOLE] * 2,
            out_shape=[jax.ShapeDtypeStruct((model // 2, columns), bf16)] * 2,
            scratch_shapes=[
                pltpu.VMEM((tokens, model), bf16),
                pltpu.SemaphoreType.DMA((4,)),
            ],
            name="project_grad",
        )(scalars, pair, core, grads)

    def norm_two_back(scalars, own, from_x, from_l, hidden, gain, given):
        rows, model = own.shape

        def kernel(scal, own_ref, x_ref, l_ref, hidden_ref, gain_ref, given_ref, out_ref, low_ref, sum_ref):
            grad_out = own_ref[...] + x_ref[...].astype(f32) + l_ref[...].astype(f32)
            normed, row_scale = norm_forward(hidden_ref[...])
            grad_normed = grad_out * gain_ref[...]
            grad_in = row_scale * (
                grad_normed - normed * jnp.mean(grad_normed * normed, axis=-1, keepdims=True)
            )
            total = given_ref[...].astype(f32) + grad_in
            out_ref[...] = total
            low_ref[...] = total.astype(bf16)
            sum_ref[0:1, :] = jnp.sum(grad_out * normed, axis=0, keepdims=True)

        outs = [((rows, model), f32), ((rows, model), bf16), ((8, model), f32)]
        return whole_call(
            kernel, outs, "norm_two_back", scalars, own, from_x, from_l, hidden, gain, given
        )

    def local(
        block_input,
        segment_ids,
        gain_attn,
        w_query,
        b_query,
        w_keyval,
        b_keyval,
        w_out,
        gain_ffn,
        w_gate,
        w_up,
        w_down,
        cotangent,
    ):
        dp_index = lax.axis_index("dp")
        tensor_index = lax.axis_index("tensor")
        scalars = jnp.stack([dp_index, tensor_index]).astype(jnp.int32)
        local_heads = b_query.shape[0] // HD
        head_kv = tensor_index * local_heads // (HQ // KV)
        is_value = tensor_index % 2
        kv_column = is_value * (KV * HD) + head_kv * HD
        width = local_heads * HD

        groups = dp_size // 4

        def fold_rows(total, bit):
            flag = ((dp_index & bit) != 0).astype(jnp.int32)
            view = total.reshape(2, -1, total.shape[1])
            kept = lax.dynamic_index_in_dim(view, flag, 0, keepdims=False)
            sent = lax.dynamic_index_in_dim(view, 1 - flag, 0, keepdims=False)
            return kept, swap(sent.astype(bf16), "dp", bit)

        def far_rest(kept, sent):
            arrived = swap(sent, "dp", far_bits[0])
            for bit in far_bits[1:]:
                kept, sent = fold_sum(scalars, kept, arrived, bit, 1)
                arrived = swap(sent, "dp", bit)
            return kept, arrived

        keyval_cols = lax.dynamic_slice_in_dim(w_keyval, kv_column, HD, 1)
        qkv_own = jnp.concatenate([w_query, keyval_cols], axis=1)
        shard = qkv_own.shape[0]
        qkv_far = far_pieces(qkv_own)
        qkv_l = swap(qkv_own, "dp", pair_bit)
        qkv_y = swap(qkv_own, "dp", 1)
        rows_float = block_input.astype(f32)
        normed_one, scale_one = norm_forward(rows_float)
        act_own = (normed_one * gain_attn).astype(bf16)
        act_x = swap(act_own, "tensor", 2)
        gate_mine, gate_sent = split_cols(scalars, w_gate)
        gate_theirs = swap(gate_sent, "dp", pair_bit)

        qkv_far_in, qkv_l, qkv_y, out_own, w_up_in, w_down_in, segments = hold(
            [gate_sent, act_own],
            [tuple(qkv_far[1:]), qkv_l, qkv_y, w_out.T, w_up, w_down, segment_ids],
        )
        far_rows = rows_of(*qkv_far_in)
        qkv_y2 = swap(rows_of(qkv_l, far_rows), "dp", 1)
        qkv_l2 = swap(far_rows, "dp", pair_bit)
        out_far = far_pieces(out_own)
        rest_mine, rest_sent = split_cols(scalars, w_up_in, w_down_in.T)
        positions = positions_of(segments[0])
        cosine, sine = rotary(positions)
        sine = jnp.where(jnp.arange(HD)[None, :] < HD // 2, -sine, sine)
        starts = (jnp.arange(positions.shape[0], dtype=jnp.int32) - positions)[:, None]
        qkv_bias = jnp.concatenate([b_query, lax.dynamic_slice_in_dim(b_keyval, kv_column, HD, 0)])[
            None, :
        ]

        qkv_y2, qkv_l2, act_pair, gate_theirs, out_half, cosine, sine, starts, rest_sent, cot_own = (
            hold(
                [],
                [
                    qkv_y2,
                    qkv_l2,
                    rows_of(act_own, act_x),
                    gate_theirs,
                    rows_of(*out_far),
                    cosine,
                    sine,
                    starts,
                    rest_sent,
                    cotangent,
                ],
            )
        )
        gate_piece = join_rows(scalars, gate_mine, gate_theirs, 0, 1)
        gate_far = far_pieces(gate_piece)
        cot_x = swap(cot_own, "tensor", 2)
        (qkv_l2,) = hold([gate_piece], [qkv_l2])

        def gather_attn():
            return (
                swap(qkv_l2, "dp", 1),
                swap(act_pair, "tensor", 1),
                swap(out_half, "dp", pair_bit),
            )

        qkv_y3, act_c, out_l = section(gather_attn)

        qkv_y3, act_c, out_near, rest_sent, cot_core = hold(
            [], [qkv_y3, act_c, rows_of(out_half, out_l), rest_sent, cotangent]
        )
        rest_theirs = swap(rest_sent, "dp", pair_bit)
        out_y = swap(out_near, "dp", 1)
        far_masks = masks_of(far_bits)
        qkv_pieces = [(part, 0, mask) for part, mask in zip(qkv_far, far_masks)]
        qkv_pieces += [(qkv_l, 0, pair_bit), (qkv_y, 0, 1), (qkv_y2, 0, pair_bit ^ 1)]
        for at, mask in enumerate(far_masks[1:]):
            qkv_pieces += [
                (qkv_y2, (at + 1) * shard, mask ^ 1),
                (qkv_l2, at * shard, mask ^ pair_bit),
                (qkv_y3, at * shard, mask ^ pair_bit ^ 1),
            ]

        def attention():
            query_rot, kv_own = project(
                scalars, act_pair, act_c, qkv_pieces, qkv_bias, cosine, sine
            )
            kv_other = swap(kv_own, "tensor", 1)
            kv_other, cot_given = hold([], [kv_other, cot_core])
            cot_own_c = swap(cot_given, "tensor", 1)
            context = attend(scalars, query_rot, kv_own, kv_other, starts)
            context, cot_own_c = hold([], [context, cot_own_c])
            return query_rot, kv_own, kv_other, context, cot_own_c

        def out_pieces(near, far):
            pieces = []
            masks = masks_of(far_bits + [pair_bit])
            for at, mask in enumerate(masks):
                pieces += [(near, at * shard, mask), (far, at * shard, mask ^ 1)]
            return pieces

        query_rot, kv_own, kv_other, context, cot_own_c = section(attention)
        context, out_y = hold([], [context, out_y])
        out_parts = out_pieces(out_near, out_y)
        attn_kept, attn_sent = out_rows(scalars, context, out_parts, act_pair.shape[1])

        attn_sent, rest_theirs, cot_own_l = hold([cot_x], [attn_sent, rest_theirs, cotangent])

        def sum_cores():
            arrived = swap(attn_sent, "tensor", 1)
            return arrived, join_both(scalars, gate_piece, rest_mine, rest_theirs)

        attn_arrived, (up_piece, own_both) = section(sum_cores)
        attn_arrived, up_piece, own_both = hold([], [attn_arrived, up_piece, own_both])
        up_far = far_pieces(up_piece)
        own_y = swap(own_both, "dp", 1)
        cot_l = swap(cot_own_l, "dp", pair_bit)

        def sum_heads():
            own, sent = fold_fixed(scalars, attn_kept, attn_arrived, [0], [1])
            return norm_two(
                scalars, block_input, own, swap(sent, "tensor", 2), gain_ffn[None, :]
            )

        hidden, two_own = section(sum_heads)

        two_own, gate_halves = hold([cot_l], [two_own, tuple(gate_far[1:])])
        gate_y2 = [swap(part, "dp", 1) for part in gate_halves]

        def gather_near():
            two_x = swap(two_own, "tensor", 2)
            two_l = swap(two_own, "dp", pair_bit)
            return two_x, two_l, join_rows(scalars, rest_mine, rest_theirs, 1, 2)

        two_x, two_l, down_piece = section(gather_near)

        rows = two_own.shape[0]
        two_x, two_l, down_piece, up_halves = hold(
            [own_y, gate_y2], [two_x, two_l, down_piece, tuple(up_far[1:])]
        )
        up_y2 = [swap(part, "dp", 1) for part in up_halves]
        down_far = far_pieces(down_piece)

        def gather_rest():
            far_a = swap(two_l[: rows // 2], "tensor", 2)
            far_b = swap(two_x[rows // 2 :], "dp", pair_bit)

            def cores():
                given, arrived = [two_x, two_l, two_own], []
                for at in range(3):
                    part = swap(given[at], "tensor", 1)
                    part, *given = hold([], [part] + given)
                    arrived.append(part)
                return arrived

            arrived = section(cores)
            far_a, far_b, *arrived = hold([], [far_a, far_b] + arrived)
            return far_a, far_b, *arrived, swap(far_a, "tensor", 1), swap(far_b, "tensor", 1)

        far_a, far_b, two_x_c, two_l_c, two_own_c, far_a_c, far_b_c = section(gather_rest)
        two_pieces = [two_own, two_x, two_l]
        two_pieces_c = [two_own_c, two_x_c, two_l_c]

        size = gate_piece.shape[0]
        gate_pieces = [(part, 0) for part in [*gate_far]] + [
            (part, 0) for part in [own_y, *gate_y2]
        ]
        up_pieces = [(part, 0) for part in [*up_far]] + [(own_y, size)] + [
            (part, 0) for part in up_y2
        ]
        far_a, far_b, far_a_c, far_b_c, down_piece_y, cot_x, cot_l = hold(
            up_y2, [far_a, far_b, far_a_c, far_b_c, down_piece, cot_x, cot_l]
        )
        two_pieces += [far_a, far_b]
        two_pieces_c += [far_a_c, far_b_c]

        def feed_own():
            down_y1 = swap(down_piece_y, "dp", 1)
            cot_far = swap(cot_l, "tensor", 2)
            x_c = swap(cot_x, "tensor", 1)
            own = ffn_up(scalars, two_pieces, gate_pieces, up_pieces)
            down_y1, cot_far, x_c = hold([own], [down_y1, cot_far, x_c])
            return down_y1, cot_far, x_c, own

        down_y1, cot_far, cot_x_c, (acts_a, mixed_a, silu_a, back_a) = section(feed_own)

        mixed_a, down_halves, cot_l_in = hold([], [mixed_a, tuple(down_far[1:]), cot_l])

        cots = [cot_own, cot_x, cot_l, cot_far]

        def feed_core():
            down_y2 = tuple(swap(part, "dp", 1) for part in down_halves)

            def core_half():
                l_c = swap(cot_l_in, "tensor", 1)
                far_c = swap(cot_far, "tensor", 1)
                core = ffn_up(scalars, two_pieces_c, gate_pieces, up_pieces)
                l_c, far_c, *core = hold([], [l_c, far_c, *core])
                grads = ffn_grad(
                    scalars, cots, [cot_own_c, cot_x_c, l_c, far_c], mixed_a, core[1], "grad_down"
                )
                return l_c, far_c, core, grads

            outs = section(core_half)
            down_y2, outs = hold([], [down_y2, outs])
            return (down_y2, *outs)

        (
            down_y2, cot_l_c, cot_far_c, (acts_b, mixed_b, silu_b, back_b), (down_kept, down_sent),
        ) = section(feed_core)
        cots_c = [cot_own_c, cot_x_c, cot_l_c, cot_far_c]
        down_pieces = [(part, 0) for part in [*down_far, down_y1, *down_y2]]

        down_sent, silu_b = hold([], [down_sent, silu_b])
        down_sent = swap(down_sent, "dp", 1)

        def back_all():
            gate_b, up_b, two_sent = ffn_back(
                scalars, cots_c, down_pieces, gate_pieces, up_pieces, silu_b, back_b
            )
            (two_sent,) = hold([], [two_sent])
            arrived = swap(two_sent, "tensor", 1)
            gate_a, up_a, kept = ffn_back(
                scalars, cots, down_pieces, gate_pieces, up_pieces, silu_a, back_a
            )
            return (gate_a, up_a, gate_b, up_b, *spread_eight(scalars, kept, arrived))

        gate_a, up_a, gate_b, up_b, own, to_x, to_l, far_a, far_b = section(back_all)

        far_a, far_b, down_sent = hold([], [far_a, far_b, down_sent])

        def backward():
            def spread_far():
                far_x = swap(far_a, "tensor", 2)
                far_l = swap(far_b, "dp", pair_bit)
                gate_grads = ffn_grad(scalars, [acts_a], [acts_b], gate_a, gate_b, "grad_gate")
                far_x, far_l = hold([gate_grads], [far_x, far_l])
                return (*gate_grads, *spread_two(scalars, to_x, to_l, far_x, far_l))

            gate_kept, gate_sent, given_x, given_l = section(spread_far)

            given_x, given_l, gate_sent = hold([], [given_x, given_l, gate_sent])
            gate_sent = swap(gate_sent, "dp", 1)

            def second_norm():
                def spread_near():
                    from_x = swap(given_x, "tensor", 2)
                    from_l = swap(given_l, "dp", pair_bit)
                    up_grads = ffn_grad(scalars, [acts_a], [acts_b], up_a, up_b, "grad_up")
                    down_pair = fold_sum(scalars, down_kept, down_sent, far_bits[0], 1)
                    from_x, from_l = hold([up_grads, down_pair], [from_x, from_l])
                    return (
                        *up_grads,
                        *down_pair,
                        *norm_two_back(
                            scalars, own, from_x, from_l, hidden, gain_ffn[None, :], cotangent
                        ),
                    )

                up_kept, up_sent, down_own, down_given, grad_hidden, attn_own, gain_two = section(
                    spread_near
                )

                attn_own, down_given = hold([], [attn_own, down_given])
                down_own, down_arrived = far_rest(down_own, down_given)

                def gather_back():
                    attn_x = swap(attn_own, "tensor", 2)
                    model = attn_own.shape[1]
                    block_sent = ffn_rows(scalars, mixed_b, down_pieces, model, "block_rows")
                    block_kept = ffn_rows(scalars, mixed_a, down_pieces, model, "block_rows")
                    (attn_x,) = hold([block_kept, block_sent], [attn_x])
                    return rows_of(attn_own, attn_x), block_kept, block_sent

                attn_half, block_kept, block_sent = section(gather_back)
                attn_half, down_arrived = hold([], [attn_half, down_arrived])
                return (
                    up_kept, up_sent, down_own, down_arrived, grad_hidden, gain_two,
                    attn_half, block_kept, block_sent,
                )

            outs = section(second_norm)
            outs, gate_sent = hold([], [outs, gate_sent])
            return (gate_kept, gate_sent, *outs)

        (
            gate_kept, gate_sent, up_kept, up_sent, down_kept, down_sent, grad_hidden, gain_two,
            attn_half, block_kept, block_sent,
        ) = section(backward)

        attn_half, gate_sent, up_sent, down_sent, block_sent = hold(
            [], [attn_half, gate_sent, up_sent, down_sent, block_sent]
        )
        up_sent = swap(up_sent, "dp", 1)

        def gather_back_core():
            attn_c = swap(attn_half, "tensor", 1)
            gate_pair = fold_sum(scalars, gate_kept, gate_sent, far_bits[0], 1)
            attn_c, block_given = hold([gate_pair], [attn_c, block_sent])
            block_arrived = swap(block_given, "tensor", 1)
            down_pair = fold_sum(scalars, down_kept, down_sent, pair_bit, 1)
            (block_arrived,) = hold([down_pair], [block_arrived])
            block_pair = fold_fixed(scalars, block_kept, block_arrived, [0, 2], [1, 3])
            return attn_c, gate_pair, down_pair, block_pair

        attn_c, (gate_kept, gate_sent), (down_mine, down_given), (block_kept, block_sent) = section(
            gather_back_core
        )

        attn_c, block_sent, gate_sent = hold([], [attn_c, block_sent, gate_sent])
        gate_kept, gate_sent = far_rest(gate_kept, gate_sent)
        block_sent = swap(block_sent, "tensor", 2)

        def attention_back():
            outs = attend_back(
                scalars, query_rot, kv_own, kv_other, starts, out_parts, attn_half, attn_c,
                context, cosine, sine,
            )
            grad_query_low, kv_kept, kv_given, bias_rows, wout_kept, wout_sent = outs
            kv_given, wout_sent = hold([], [kv_given, wout_sent])
            wout_arrived = swap(wout_sent, "dp", 1)

            def project_all():
                kv_arrived = swap(kv_given, "tensor", 1)
                grad_qkv, one_kept, one_sent, gain_rows = project_back(
                    scalars, grad_query_low, kv_kept, kv_arrived, qkv_pieces, act_pair, act_c
                )
                arrived = swap(one_sent, "tensor", 1)
                wqkv_pair = project_grad(scalars, act_pair, act_c, grad_qkv)
                (arrived,) = hold([wqkv_pair], [arrived])
                return (
                    *wqkv_pair,
                    *fold_fixed(scalars, one_kept, arrived, [0], [1]),
                    gain_rows,
                )

            outs = section(project_all)
            outs, wout_arrived = hold([], [outs, wout_arrived])
            return (
                *outs, bias_rows, *fold_sum(scalars, wout_kept, wout_arrived, pair_bit, groups)
            )

        (
            wqkv_kept,
            wqkv_sent,
            one_kept,
            one_sent,
            gain_rows,
            bias_rows,
            wout_kept,
            wout_sent,
        ) = section(attention_back)

        up_sent, one_sent, wqkv_sent, wout_sent, down_given, block_sent = hold(
            [], [up_sent, one_sent, wqkv_sent, wout_sent, down_given, block_sent]
        )
        up_kept, up_sent = fold_sum(scalars, up_kept, up_sent, far_bits[0], 1)
        one_sent, wqkv_sent, up_sent, gate_sent = hold(
            [], [one_sent, wqkv_sent, up_sent, gate_sent]
        )
        up_kept, up_sent = far_rest(up_kept, up_sent)
        devices = dp_size * tensor_size

        def first_norm_back():
            arrived = swap(one_sent, "tensor", 2)
            wqkv_arrived = swap(wqkv_sent, "dp", 1)
            wout_arrived = swap(wout_sent, "dp", pair_bit)
            down_arrived = swap(down_given, "dp", pair_bit)
            gate_pair = fold_sum(scalars, gate_kept, gate_sent, pair_bit, 1)
            block_pair = fold_fixed(scalars, block_kept, block_sent, [0], [1])
            bias_keyval = jnp.zeros((2 * KV * HD,), f32)
            bias_keyval = lax.dynamic_update_slice_in_dim(
                bias_keyval, bias_rows[0, width : width + HD], head_kv * HD, 0
            )
            bias_keyval = lax.dynamic_update_slice_in_dim(
                bias_keyval, bias_rows[0, width + HD :], KV * HD + head_kv * HD, 0
            )
            bias_query = lax.dynamic_update_slice_in_dim(
                jnp.zeros((HQ * HD,), f32), bias_rows[0, :width], tensor_index * width, 0
            )
            parts = (gain_rows[0] / gain_attn, gain_two[0], bias_query, bias_keyval)
            small = jnp.concatenate([part.reshape(devices, -1) for part in parts], axis=1)
            (arrived,) = hold([gate_pair, block_pair, small], [arrived])
            grad_rows = norm_one_back(
                scalars, block_input, one_kept, arrived, gain_attn[None, :], grad_hidden
            )
            wqkv_arrived, wout_arrived, down_arrived = hold(
                [grad_rows], [wqkv_arrived, wout_arrived, down_arrived]
            )
            return (
                grad_rows,
                small,
                gate_pair,
                block_pair,
                fold_sum(scalars, wqkv_kept, wqkv_arrived, pair_bit, groups),
                wout_arrived,
                down_arrived,
            )

        (
            grad_rows,
            small,
            (gate_mine, gate_given),
            (block_kept, block_sent),
            (wqkv_kept, wqkv_sent),
            wout_arrived,
            down_theirs,
        ) = section(first_norm_back)

        wqkv_sent, gate_given, block_sent, small = hold(
            [], [wqkv_sent, gate_given, block_sent, small]
        )
        small = lax.all_to_all(small, ("dp", "tensor"), 0, 0, tiled=True)

        def last_rows():
            wqkv_arrived = swap(wqkv_sent, "dp", pair_bit)
            block_arrived = swap(block_sent, "dp", pair_bit)
            wout_total = add(wout_kept, wout_arrived)
            down_share = join_cols(scalars, down_mine, down_theirs, w_down.shape[0] // 2).T
            (wqkv_arrived,) = hold([down_share, wout_total], [wqkv_arrived])
            total = jnp.concatenate([add(wqkv_kept, wqkv_arrived), wout_total], axis=1)
            total, gate_out = hold([], [total, gate_given])
            for bit in far_bits[:-1]:
                total = add(*fold_rows(total, bit))
            kept, sent = fold_rows(total, far_bits[-1])
            gate_theirs = swap(gate_out, "dp", pair_bit)
            (block_arrived,) = hold([kept], [block_arrived])
            block_out = (hidden + add(block_kept, block_arrived)).astype(bf16)
            (sent,) = hold([block_out], [sent])
            share = add(kept, sent)
            kv_rows = share[:, width : width + HD]
            share_rows = kv_rows.shape[0] // tensor_size
            keyval_share = jnp.zeros((share_rows, 2 * KV * HD), f32)
            moved = []
            for mask in range(tensor_size):
                rows_for = lax.dynamic_slice_in_dim(
                    kv_rows, (tensor_index ^ mask) * share_rows, share_rows, 0
                )
                moved.append(swap(rows_for, "tensor", mask) if mask else rows_for)
            query_share, out_share = share[:, :width], share[:, width + HD :].T
            gate_theirs, *moved = hold([query_share, out_share], [gate_theirs] + moved)
            gate_share = join_cols(scalars, gate_mine, gate_theirs, w_gate.shape[1] // 2)
            for mask in range(tensor_size):
                sender = tensor_index ^ mask
                column = (sender % 2) * (KV * HD) + (sender * local_heads // (HQ // KV)) * HD
                keyval_share = lax.dynamic_update_slice_in_dim(
                    keyval_share, moved[mask], column, 1
                )
            return down_share, gate_share, block_out, query_share, out_share, keyval_share

        down_share, gate_share, block_out, query_share, out_share, keyval_share = section(last_rows)

        up_sent, small = hold([block_out, keyval_share], [up_sent, small])
        up_mine, up_given = fold_sum(scalars, up_kept, up_sent, pair_bit, 1)
        up_theirs = swap(up_given, "dp", pair_bit)
        small = jnp.sum(small, axis=0)
        up_share = join_cols(scalars, up_mine, up_theirs, w_up.shape[1] // 2)
        sizes = [HQ * HD // devices, 2 * KV * HD // devices, gain_attn.shape[0] // devices]
        ends = [sizes[2], 2 * sizes[2], 2 * sizes[2] + sizes[0]]
        gain_one_share = small[: ends[0]]
        gain_two_share = small[ends[0] : ends[1]]
        query_bias_share = small[ends[1] : ends[2]]
        keyval_bias_share = small[ends[2] :]
        return (
            block_out,
            grad_rows,
            gain_one_share,
            query_share,
            query_bias_share,
            keyval_share,
            keyval_bias_share,
            out_share,
            gain_two_share,
            gate_share,
            up_share,
            down_share,
        )

    placed = (
        P(("dp", "tensor"), None),
        P("dp", None),
        P(),
        P("dp", "tensor"),
        P("tensor"),
        P("dp", None),
        P(),
        P("tensor", "dp"),
        P(),
        P("dp", "tensor"),
        P("dp", "tensor"),
        P("tensor", "dp"),
        P(("dp", "tensor"), None),
    )
    return jax.shard_map(
        local,
        mesh=mesh,
        in_specs=placed,
        out_specs=(
            P(("dp", "tensor"), None),
            P(("dp", "tensor"), None),
            P(("dp", "tensor")),
            P("dp", "tensor"),
            P(("dp", "tensor")),
            P(("dp", "tensor"), None),
            P(("dp", "tensor")),
            P("tensor", "dp"),
            P(("dp", "tensor")),
            P("dp", "tensor"),
            P("dp", "tensor"),
            P("tensor", "dp"),
        ),
        check_vma=False,
    )
```

```python
import math

import jax
import jax.numpy as jnp
from jax import lax
from jax.experimental import pallas as pl
from jax.experimental.pallas import tpu as pltpu
from jax.sharding import PartitionSpec as P

HQ = 12
KV = 2
HD = 128


epsilon = 1e-06
rope_base = 1000000.0
masked_score = -1e30
bf16 = jnp.bfloat16
f32 = jnp.float32


def positions_of(segment_row):
    index_row = jnp.arange(segment_row.shape[0], dtype=jnp.int32)
    starts = jnp.concatenate(
        [jnp.ones((1,), jnp.int32), (segment_row[1:] != segment_row[:-1]).astype(jnp.int32)]
    )
    first_index = lax.cummax(jnp.where(starts > 0, index_row, 0), axis=0)
    return index_row - first_index


def rotary(positions):
    inverse = rope_base ** (-(jnp.arange(HD // 2, dtype=jnp.float32) * 2.0 / HD))
    angles = positions.astype(jnp.float32)[:, None] * inverse[None, :]
    angles = jnp.concatenate([angles, angles], axis=1)
    return (jnp.cos(angles), jnp.sin(angles))


def norm_forward(values_in):
    row_scale = lax.rsqrt(jnp.mean(values_in * values_in, axis=-1, keepdims=True) + epsilon)
    return (values_in * row_scale, row_scale)


def norm_backward(grad_out, normed, row_scale, gain_vec):
    grad_normed = grad_out * gain_vec
    grad_in = row_scale * (
        grad_normed - normed * jnp.mean(grad_normed * normed, axis=-1, keepdims=True)
    )
    return (grad_in, jnp.sum(grad_out * normed, axis=0))


ANY = pl.BlockSpec(memory_space=pl.ANY)
WHOLE = pl.BlockSpec(memory_space=pltpu.VMEM)
SCALARS = pl.BlockSpec(memory_space=pltpu.SMEM)


def made(jobs, sems, first=0):
    return [
        pltpu.make_async_copy(src, dst, sems.at[first + at]) for at, (src, dst) in enumerate(jobs)
    ]


def start_all(jobs, sems):
    copies = made(jobs, sems)
    for copy in copies:
        copy.start()
    return copies


def wait_all(copies):
    for copy in copies:
        copy.wait()


def block(ref, at, rows):
    return ref.at[pl.ds(pl.multiple_of(at * rows, rows), rows)]


def turned(values, cosine, sine, sign):
    return values * cosine + sign * (pltpu.roll(values, HD // 2, 1) * sine)


def mm(left, right):
    return lax.dot_general(left, right, (((1,), (0,)), ((), ())), preferred_element_type=f32)


def mm_nt(left, right):
    return lax.dot_general(left, right, (((1,), (1,)), ((), ())), preferred_element_type=f32)


def mm_tn(left, right):
    return lax.dot_general(left, right, (((0,), (0,)), ((), ())), preferred_element_type=f32)


def hold(due, release):
    out = lax.optimization_barrier((tuple(due), tuple(release)))
    return out[1]


def section(body):
    outs = jax.eval_shape(body)
    return lax.cond(
        lax.optimization_barrier(jnp.bool_(True)),
        body,
        lambda: jax.tree.map(lambda out: jnp.zeros(out.shape, out.dtype), outs),
    )


def solution(mesh):
    dp_size = mesh.shape["dp"]
    tensor_size = mesh.shape["tensor"]
    pair_bit = 2
    far_bits = []
    bit = dp_size // 2
    while bit > pair_bit:
        far_bits.append(bit)
        bit //= 2
    ring_bits = far_bits + [1]

    def swap(array, axis, bit):
        size = mesh.shape[axis]
        with jax.named_scope(f"swap_{axis}_{bit}"):
            return lax.ppermute(array, axis, [(i, i ^ bit) for i in range(size)])

    def masks_of(bits):
        masks = [0]
        for bit in bits:
            masks = masks + [mask ^ bit for mask in masks]
        return masks

    def rows_of(*pieces):
        return jnp.concatenate(pieces, axis=0)

    def far_pieces(piece):
        pieces = [piece]
        for bit in far_bits:
            pieces = pieces + [swap(part, "dp", bit) for part in pieces]
        return pieces

    def fold(total, axis, bit):
        half = total.shape[0] // 2
        return total[:half], swap(total[half:].astype(bf16), axis, bit)

    def add(kept, arrived):
        return kept.astype(f32) + arrived.astype(f32)

    ring_masks = masks_of(ring_bits)
    ring_mask = sum(ring_bits)
    count = len(ring_masks)


    def ffn_jobs(dp_index, refs, offsets, held):
        rows = held.shape[0] // dp_size
        jobs = []
        for mask, ref, offset in zip(ring_masks, refs, offsets):
            base = jnp.bitwise_xor(jnp.bitwise_and(dp_index, ring_mask), mask)
            for low in (0, 1):
                jobs.append(
                    (
                        ref.at[pl.ds(offset + low * rows, rows)],
                        block(held, base + low * pair_bit, rows),
                    )
                )
        return jobs

    def row_jobs(refs, held):
        jobs, start = [], 0
        for ref in refs:
            jobs.append((ref, held.at[pl.ds(start, ref.shape[0])]))
            start += ref.shape[0]
        return jobs

    def attn_jobs(dp_index, refs, pieces, held):
        rows = held.shape[0] // dp_size
        return [
            (
                ref.at[pl.ds(first, rows)],
                block(held, jnp.bitwise_xor(dp_index, mask), rows),
            )
            for ref, (_, first, mask) in zip(refs, pieces)
        ]

    def arrays_of(pieces):
        return [piece[0] for piece in pieces]

    token_masks = ((0, 2), (1, 3))

    def token_jobs(tensor_index, pair, other, held):
        rows = held.shape[0] // 4
        jobs = []
        for masks, ref in zip(token_masks, (pair, other)):
            for at, mask in enumerate(masks):
                spot = jnp.bitwise_xor(tensor_index, mask)
                jobs.append((ref.at[pl.ds(at * rows, rows)], block(held, spot, rows)))
        return jobs

    def back(jobs):
        return [(dst, src) for src, dst in jobs]

    def ffn_up(scalars, pieces, gate_pieces, up_pieces):
        tokens, model = sum(piece.shape[0] for piece in pieces), pieces[0].shape[1]
        units = gate_pieces[0][0].shape[1]
        rows = tokens // 2
        many = len(pieces)
        early = 2

        def kernel(scal, *refs):
            parts = refs[:many]
            gates = refs[many : many + count]
            ups = refs[many + count : many + 2 * count]
            acts_ref, mixed_ref, silu_ref, back_ref, acts, gate_w, up_w, sems = refs[
                many + 2 * count :
            ]
            jobs = row_jobs(parts, acts)
            gate_jobs = ffn_jobs(scal[0], gates, [at for _, at in gate_pieces], gate_w)
            up_jobs = ffn_jobs(scal[0], ups, [at for _, at in up_pieces], up_w)
            step = pl.program_id(0)

            @pl.when(step == 0)
            def _():
                copies = start_all(jobs[:early] + gate_jobs + jobs[early:] + up_jobs, sems)
                wait_all(copies[: early + 2 * count])

            @pl.when(step == 1)
            def _():
                wait_all(made(jobs[early:], sems, early + 2 * count))

            spot = pl.ds(pl.multiple_of(step * rows, rows), rows)
            rows_in = acts[spot, :]
            acts_ref[...] = rows_in
            gate = mm(rows_in, gate_w[...])

            @pl.when(step == 0)
            def _():
                wait_all(made(up_jobs, sems, many + 2 * count))

            up = mm(rows_in, up_w[...])
            sig = jax.nn.sigmoid(gate)
            silu = gate * sig
            mixed_ref[...] = (silu * up).astype(bf16)
            silu_ref[...] = silu.astype(bf16)
            back_ref[...] = (up * sig * (1.0 + gate * (1.0 - sig))).astype(bf16)

        out = jax.ShapeDtypeStruct((tokens, units), bf16)
        spec = pl.BlockSpec((rows, units), lambda i: (i, 0))
        return pl.pallas_call(
            kernel,
            grid=(2,),
            in_specs=[SCALARS] + [ANY] * (many + 2 * count),
            out_specs=[pl.BlockSpec((rows, model), lambda i: (i, 0))] + [spec] * 3,
            out_shape=[jax.ShapeDtypeStruct((tokens, model), bf16)] + [out] * 3,
            scratch_shapes=[
                pltpu.VMEM((tokens, model), bf16),
                pltpu.VMEM((model, units), bf16),
                pltpu.VMEM((model, units), bf16),
                pltpu.SemaphoreType.DMA((many + 4 * count,)),
            ],
            name="ffn_up",
        )(
            scalars,
            *pieces,
            *[ref for ref, _ in gate_pieces],
            *[ref for ref, _ in up_pieces],
        )

    def ffn_back(scalars, cots, down_pieces, gate_pieces, up_pieces, silu, back_part):
        many = len(cots)
        tokens, model = sum(piece.shape[0] for piece in cots), cots[0].shape[1]
        units = silu.shape[1]
        rows = tokens // 2
        lists = (down_pieces, gate_pieces, up_pieces)

        def kernel(scal, *refs):
            parts = refs[:many]
            pieces = [refs[many + at * count : many + (at + 1) * count] for at in range(3)]
            silu_ref, back_ref, grad_gate_ref, grad_up_ref, out_ref = refs[
                many + 3 * count : many + 3 * count + 5
            ]
            cot, *held = refs[many + 3 * count + 5 : -1]
            sems = refs[-1]
            jobs = row_jobs(parts, cot)
            for at in range(3):
                jobs += ffn_jobs(scal[0], pieces[at], [spot for _, spot in lists[at]], held[at])
            first = pl.program_id(0) == 0
            early = many + 2 * count

            @pl.when(first)
            def _():
                wait_all(start_all(jobs, sems)[:early])

            spot = pl.ds(pl.multiple_of(pl.program_id(0) * rows, rows), rows)
            grad_mixed = mm(cot[spot, :], held[0][...])
            grad_gate = (grad_mixed * back_ref[...].astype(f32)).astype(bf16)
            grad_up = (grad_mixed * silu_ref[...].astype(f32)).astype(bf16)
            grad_gate_ref[...] = grad_gate
            grad_up_ref[...] = grad_up

            @pl.when(first)
            def _():
                wait_all(made(jobs[early:], sems, early))

            out_ref[...] = (
                mm_nt(grad_gate, held[1][...]) + mm_nt(grad_up, held[2][...])
            ).astype(bf16)

        out = jax.ShapeDtypeStruct((tokens, units), bf16)
        spec = pl.BlockSpec((rows, units), lambda i: (i, 0))
        wide = pl.BlockSpec((rows, model), lambda i: (i, 0))
        return pl.pallas_call(
            kernel,
            grid=(2,),
            in_specs=[SCALARS] + [ANY] * (many + 3 * count) + [spec, spec],
            out_specs=[spec, spec, wide],
            out_shape=[out, out, jax.ShapeDtypeStruct((tokens, model), bf16)],
            scratch_shapes=[pltpu.VMEM((tokens, model), bf16)]
            + [pltpu.VMEM((model, units), bf16)] * 3
            + [pltpu.SemaphoreType.DMA((many + 6 * count,))],
            name="ffn_back",
        )(scalars, *cots, *[ref for pieces in lists for ref, _ in pieces], silu, back_part)

    def ffn_rows(scalars, left, pieces, model, name):
        tokens, units = left.shape
        rows = tokens // 2

        def kernel(scal, left_ref, *refs):
            parts = refs[:count]
            out_ref, held, sems = refs[count:]

            @pl.when(pl.program_id(0) == 0)
            def _():
                wait_all(
                    start_all(ffn_jobs(scal[0], parts, [at for _, at in pieces], held), sems)
                )

            out_ref[...] = mm_nt(left_ref[...], held[...]).astype(bf16)

        return pl.pallas_call(
            kernel,
            grid=(2,),
            in_specs=[SCALARS, pl.BlockSpec((rows, units), lambda i: (i, 0))] + [ANY] * count,
            out_specs=pl.BlockSpec((rows, model), lambda i: (i, 0)),
            out_shape=jax.ShapeDtypeStruct((tokens, model), bf16),
            scratch_shapes=[
                pltpu.VMEM((model, units), bf16),
                pltpu.SemaphoreType.DMA((2 * count,)),
            ],
            name=name,
        )(scalars, left, *[ref for ref, _ in pieces])

    def ffn_grad(scalars, own_pieces, core_pieces, low, high, name):
        pieces = [*own_pieces, *core_pieces]
        many = len(own_pieces)
        tokens, model = low.shape[0], pieces[0].shape[1]
        units = low.shape[1]
        shard = model // dp_size
        wide = 384
        groups = wide // (2 * shard)

        def kernel(scal, *refs):
            def stack(parts):
                values = [part[...] for part in parts]
                return values[0] if len(values) == 1 else jnp.concatenate(values, axis=0)

            low_ref, high_ref, kept_ref, sent_ref = refs[2 * many :]
            total = mm_tn(stack(refs[:many]), low_ref[...])
            total = total + mm_tn(stack(refs[many : 2 * many]), high_ref[...])
            total = total.astype(bf16)
            odd = jnp.bitwise_and(scal[0], 1) == 1
            for group in range(groups):
                first = total[group * 2 * shard : group * 2 * shard + shard]
                second = total[group * 2 * shard + shard : (group + 1) * 2 * shard]
                spot = pl.ds(group * shard, shard)
                kept_ref[spot, :] = jnp.where(odd, second, first)
                sent_ref[spot, :] = jnp.where(odd, first, second)

        out = jax.ShapeDtypeStruct((model // 2, units), bf16)
        spec = pl.BlockSpec((wide // 2, units), lambda i: (i, 0))
        whole = pl.BlockSpec((tokens, units), lambda i: (0, 0))
        return pl.pallas_call(
            kernel,
            grid=(model // wide,),
            in_specs=[SCALARS]
            + [pl.BlockSpec((piece.shape[0], wide), lambda i: (0, i)) for piece in pieces]
            + [whole, whole],
            out_specs=[spec] * 2,
            out_shape=[out] * 2,
            name=name,
        )(scalars, *pieces, low, high)

    def is_high(scal, bit):
        return jnp.bitwise_and(scal[0], bit) != 0

    def whole_call(kernel, outs, name, *args):
        return pl.pallas_call(
            kernel,
            in_specs=[SCALARS] + [WHOLE] * (len(args) - 1),
            out_specs=[WHOLE] * len(outs),
            out_shape=[jax.ShapeDtypeStruct(shape, kind) for shape, kind in outs],
            name=name,
        )(*args)

    def split_cols(scalars, *arrays):
        rows, half = arrays[0].shape[0], arrays[0].shape[1] // 2
        wide = -(-half // 128) * 128
        many = len(arrays)

        def kernel(scal, *refs):
            mine_ref, sent_ref = refs[many:]
            flag = is_high(scal, pair_bit)
            mine_ref[...] = jnp.zeros_like(mine_ref)
            sent_ref[...] = jnp.zeros_like(sent_ref)
            for at in range(many):
                low, high = refs[at][:, :half], refs[at][:, half:]
                mine_ref[at * rows : (at + 1) * rows, :half] = jnp.where(flag, high, low)
                sent_ref[at * rows : (at + 1) * rows, :half] = jnp.where(flag, low, high)

        return whole_call(
            kernel, [((many * rows, wide), bf16)] * 2, "split_cols", scalars, *arrays
        )

    def join_rows(scalars, mine, theirs, at, many):
        rows, columns = mine.shape[0] // many, mine.shape[1]
        spot = pl.ds(at * rows, rows)

        def kernel(scal, mine_ref, theirs_ref, out_ref):
            flag = is_high(scal, pair_bit)
            out_ref[:rows, :] = jnp.where(flag, theirs_ref[spot, :], mine_ref[spot, :])
            out_ref[rows:, :] = jnp.where(flag, mine_ref[spot, :], theirs_ref[spot, :])

        return whole_call(
            kernel, [((2 * rows, columns), bf16)], "join_rows", scalars, mine, theirs
        )[0]

    def join_cols(scalars, mine, theirs, columns):
        rows = mine.shape[0]

        def kernel(scal, mine_ref, theirs_ref, out_ref):
            flag = is_high(scal, pair_bit)
            mine = mine_ref[:, :columns].astype(f32)
            theirs = theirs_ref[:, :columns].astype(f32)
            out_ref[:, :columns] = jnp.where(flag, theirs, mine)
            out_ref[:, columns:] = jnp.where(flag, mine, theirs)

        return whole_call(
            kernel, [((rows, 2 * columns), f32)], "join_cols", scalars, mine, theirs
        )[0]

    def fold_sum(scalars, kept, arrived, bit, outer):
        rows, columns = kept.shape[0] // 2, kept.shape[1]
        part = rows // outer

        def kernel(scal, kept_ref, arrived_ref, own_ref, sent_ref):
            flag = is_high(scal, bit)
            for at in range(outer):
                first = pl.ds(2 * at * part, part)
                second = pl.ds((2 * at + 1) * part, part)
                low = kept_ref[first, :].astype(f32) + arrived_ref[first, :].astype(f32)
                high = kept_ref[second, :].astype(f32) + arrived_ref[second, :].astype(f32)
                spot = pl.ds(at * part, part)
                own_ref[spot, :] = jnp.where(flag, high, low).astype(bf16)
                sent_ref[spot, :] = jnp.where(flag, low, high).astype(bf16)

        return whole_call(
            kernel, [((rows, columns), bf16)] * 2, "fold_sum", scalars, kept, arrived
        )

    def fold_fixed(scalars, kept, arrived, keep, give_away):
        many = len(keep) + len(give_away)
        rows, columns = kept.shape[0] // many, kept.shape[1]

        def kernel(scal, kept_ref, arrived_ref, own_ref, sent_ref):
            for blocks, ref in ((keep, own_ref), (give_away, sent_ref)):
                for at, spot in enumerate(blocks):
                    spot = pl.ds(spot * rows, rows)
                    ref[at * rows : (at + 1) * rows, :] = (
                        kept_ref[spot, :].astype(f32) + arrived_ref[spot, :].astype(f32)
                    ).astype(ref.dtype)

        outs = [((len(keep) * rows, columns), f32), ((len(give_away) * rows, columns), bf16)]
        return whole_call(kernel, outs, "fold_fixed", scalars, kept, arrived)

    def norm_two(scalars, rows_in, own, arrived, gain):
        def kernel(scal, in_ref, own_ref, arrived_ref, gain_ref, hidden_ref, out_ref):
            hidden = in_ref[...].astype(f32) + own_ref[...] + arrived_ref[...].astype(f32)
            hidden_ref[...] = hidden
            out_ref[...] = (norm_forward(hidden)[0] * gain_ref[...]).astype(bf16)

        outs = [(rows_in.shape, f32), (rows_in.shape, bf16)]
        return whole_call(kernel, outs, "norm_two", scalars, rows_in, own, arrived, gain)

    def norm_one_back(scalars, rows_in, own, arrived, gain, given):
        def kernel(scal, in_ref, own_ref, arrived_ref, gain_ref, given_ref, out_ref):
            grad_out = own_ref[...] + arrived_ref[...].astype(f32)
            normed, row_scale = norm_forward(in_ref[...].astype(f32))
            grad_normed = grad_out * gain_ref[...]
            grad_in = row_scale * (
                grad_normed - normed * jnp.mean(grad_normed * normed, axis=-1, keepdims=True)
            )
            out_ref[...] = (given_ref[...] + grad_in).astype(bf16)

        return whole_call(
            kernel, [(rows_in.shape, bf16)], "norm_one_back", scalars, rows_in, own, arrived, gain, given
        )[0]

    def join_both(scalars, first, mine, theirs):
        rows, columns = mine.shape[0] // 2, mine.shape[1]

        def kernel(scal, first_ref, mine_ref, theirs_ref, out_ref, both_ref):
            flag = is_high(scal, pair_bit)
            low = jnp.where(flag, theirs_ref[:rows, :], mine_ref[:rows, :])
            high = jnp.where(flag, mine_ref[:rows, :], theirs_ref[:rows, :])
            out_ref[:rows, :] = low
            out_ref[rows:, :] = high
            both_ref[: 2 * rows, :] = first_ref[...]
            both_ref[2 * rows : 3 * rows, :] = low
            both_ref[3 * rows :, :] = high

        return whole_call(
            kernel,
            [((2 * rows, columns), bf16), ((4 * rows, columns), bf16)],
            "join_both", scalars, first, mine, theirs,
        )

    def halves(scalars, first, second):
        rows, columns = first.shape[0] // 2, first.shape[1]

        def kernel(scal, first_ref, second_ref, out_a_ref, out_b_ref):
            out_a_ref[...] = first_ref[:rows, :]
            out_b_ref[...] = second_ref[rows:, :]

        return whole_call(
            kernel, [((rows, columns), bf16)] * 2, "halves", scalars, first, second
        )

    def block_step(scalars, kept, arrived):
        rows, columns = arrived.shape[0] // 2, arrived.shape[1]

        def kernel(scal, kept_ref, arrived_ref, own_ref, sent_ref):
            own_ref[...] = kept_ref[:rows, :] + arrived_ref[:rows, :].astype(f32)
            sent_ref[...] = (kept_ref[rows:, :] + arrived_ref[rows:, :].astype(f32)).astype(bf16)

        outs = [((rows, columns), f32), ((rows, columns), bf16)]
        return whole_call(kernel, outs, "block_step", scalars, kept, arrived)

    def spread_eight(scalars, kept, arrived):
        rows, model = kept.shape[0] // 4, kept.shape[1]
        half = rows // 2

        def kernel(scal, kept_ref, arrived_ref, own_ref, x_ref, l_ref, far_a_ref, far_b_ref):
            for at, ref in enumerate((own_ref, x_ref, l_ref)):
                spot = pl.ds(at * rows, rows)
                ref[...] = kept_ref[spot, :].astype(f32) + arrived_ref[spot, :].astype(f32)
            for at, ref in enumerate((far_a_ref, far_b_ref)):
                spot = pl.ds(3 * rows + at * half, half)
                ref[...] = (
                    kept_ref[spot, :].astype(f32) + arrived_ref[spot, :].astype(f32)
                ).astype(bf16)

        outs = [((rows, model), f32)] * 3 + [((half, model), bf16)] * 2
        return whole_call(kernel, outs, "spread_eight", scalars, kept, arrived)

    def spread_two(scalars, to_x, to_l, far_x, far_l):
        rows, model = to_x.shape
        half = rows // 2

        def kernel(scal, x_ref, l_ref, far_x_ref, far_l_ref, out_x_ref, out_l_ref):
            out_x_ref[:half, :] = x_ref[:half, :].astype(bf16)
            out_x_ref[half:, :] = (x_ref[half:, :] + far_l_ref[...].astype(f32)).astype(bf16)
            out_l_ref[:half, :] = (l_ref[:half, :] + far_x_ref[...].astype(f32)).astype(bf16)
            out_l_ref[half:, :] = l_ref[half:, :].astype(bf16)

        return whole_call(
            kernel, [((rows, model), bf16)] * 2, "spread_two", scalars, to_x, to_l, far_x, far_l
        )

    def give(total, scal, kept_ref, sent_ref):
        part = pair_bit * (total.shape[0] // dp_size)
        flag = is_high(scal, pair_bit)
        for at in range(total.shape[0] // (2 * part)):
            low = total[2 * at * part : (2 * at + 1) * part]
            high = total[(2 * at + 1) * part : (2 * at + 2) * part]
            kept_ref[pl.ds(at * part, part), :] = jnp.where(flag, high, low)
            sent_ref[pl.ds(at * part, part), :] = jnp.where(flag, low, high)

    def project(scalars, pair, core, pieces, bias, cosine, sine):
        tokens, model = 2 * pair.shape[0], pair.shape[1]
        columns = pieces[0][0].shape[1]
        width = columns - HD

        def kernel(scal, pair_ref, core_ref, bias_ref, cos_ref, sin_ref, *refs):
            query_ref, kv_ref, acts, held, sems = refs[dp_size:]
            wait_all(
                start_all(
                    attn_jobs(scal[0], refs[:dp_size], pieces, held)
                    + token_jobs(scal[1], pair_ref, core_ref, acts),
                    sems,
                )
            )
            is_value = jnp.bitwise_and(scal[1], 1) == 1
            rows = tokens // 4
            for at in range(4):
                spot = pl.ds(at * rows, rows)
                out = mm(acts[spot, :], held[...]) + bias_ref[...]
                cosine_rows, sine_rows = cos_ref[spot, :], sin_ref[spot, :]
                for head in range(width // HD):
                    query_ref[spot, head * HD : (head + 1) * HD] = turned(
                        out[:, head * HD : (head + 1) * HD], cosine_rows, sine_rows, 1.0
                    ).astype(bf16)
                kv = out[:, width:]
                kv_ref[spot, :] = jnp.where(
                    is_value, kv, turned(kv, cosine_rows, sine_rows, 1.0)
                ).astype(bf16)

        return pl.pallas_call(
            kernel,
            in_specs=[SCALARS, ANY, ANY, WHOLE, WHOLE, WHOLE] + [ANY] * dp_size,
            out_specs=[WHOLE, WHOLE],
            out_shape=[
                jax.ShapeDtypeStruct((tokens, width), bf16),
                jax.ShapeDtypeStruct((tokens, HD), bf16),
            ],
            scratch_shapes=[
                pltpu.VMEM((tokens, model), bf16),
                pltpu.VMEM((model, columns), bf16),
                pltpu.SemaphoreType.DMA((dp_size + 4,)),
            ],
            name="project",
        )(scalars, pair, core, bias, cosine, sine, *arrays_of(pieces))

    def probabilities(query, keys, start_rows, first):
        scores = mm_nt(query, keys) * (1.0 / math.sqrt(HD))
        column = lax.broadcasted_iota(jnp.int32, scores.shape, 1)
        row = lax.broadcasted_iota(jnp.int32, scores.shape, 0) + first
        allowed = (column <= row) & (column >= start_rows)
        scores = jnp.where(allowed, scores, masked_score)
        top = jnp.max(scores, axis=1, keepdims=True)
        raised = jnp.exp(scores - top)
        return raised * (1.0 / jnp.sum(raised, axis=1, keepdims=True))

    def attend(scalars, query, kv_own, kv_other, starts):
        tokens, width = query.shape
        rows = tokens // 4

        def kernel(scal, query_ref, own_ref, other_ref, start_ref, context_ref):
            is_value = jnp.bitwise_and(scal[1], 1) == 1
            own, other = own_ref[...], other_ref[...]
            keys = jnp.where(is_value, other, own)
            values = jnp.where(is_value, own, other)
            for at in range(4):
                end = (at + 1) * rows
                spot = pl.ds(at * rows, rows)
                for head in range(width // HD):
                    lanes = slice(head * HD, (head + 1) * HD)
                    probs = probabilities(
                        query_ref[spot, lanes], keys[:end], start_ref[spot, :], at * rows
                    )
                    context_ref[spot, lanes] = mm(probs.astype(bf16), values[:end]).astype(bf16)

        return whole_call(
            kernel, [((tokens, width), bf16)], "attend", scalars, query, kv_own, kv_other, starts
        )[0]

    def out_rows(scalars, context, pieces, model):
        tokens, width = context.shape
        rows = tokens // 4

        def kernel(scal, context_ref, *refs):
            kept_ref, sent_ref, held, part, sems, out_sems = refs[dp_size:]
            wait_all(start_all(attn_jobs(scal[0], refs[:dp_size], pieces, held), sems))
            for at in range(4):
                spot = pl.ds(at * rows, rows)
                part[spot, :] = mm_nt(context_ref[spot, :], held[...]).astype(bf16)
            wait_all(start_all(back(token_jobs(scal[1], kept_ref, sent_ref, part)), out_sems))

        half = jax.ShapeDtypeStruct((tokens // 2, model), bf16)
        return pl.pallas_call(
            kernel,
            in_specs=[SCALARS, WHOLE] + [ANY] * dp_size,
            out_specs=[ANY, ANY],
            out_shape=[half, half],
            scratch_shapes=[
                pltpu.VMEM((model, width), bf16),
                pltpu.VMEM((tokens, model), bf16),
                pltpu.SemaphoreType.DMA((dp_size,)),
                pltpu.SemaphoreType.DMA((4,)),
            ],
            name="out_rows",
        )(scalars, context, *arrays_of(pieces))

    def attend_back(
        scalars, query, kv_own, kv_other, starts, pieces, pair, core, context, cosine, sine
    ):
        tokens, width = query.shape
        model = pair.shape[1]
        rows = tokens // 4
        scale = 1.0 / math.sqrt(HD)

        def kernel(
            scal, query_ref, own_ref, other_ref, start_ref, pair_ref, core_ref,
            context_ref, cos_ref, sin_ref, *refs,
        ):
            grad_query_ref, kv_kept_ref, kv_sent_ref, bias_ref, wout_ref, wout_sent_ref = refs[
                dp_size : dp_size + 6
            ]
            held, grads, grad_context, grad_key, grad_value, sems = refs[dp_size + 6 :]
            wait_all(
                start_all(
                    attn_jobs(scal[0], refs[:dp_size], pieces, held)
                    + token_jobs(scal[1], pair_ref, core_ref, grads),
                    sems,
                )
            )
            is_value = jnp.bitwise_and(scal[1], 1) == 1
            own, other = own_ref[...], other_ref[...]
            keys = jnp.where(is_value, other, own)
            values = jnp.where(is_value, own, other)
            for at in range(2):
                spot = pl.ds(at * 2 * rows, 2 * rows)
                grad_context[spot, :] = mm(grads[spot, :], held[...]).astype(bf16)
            give(mm_tn(grads[...], context_ref[...]).astype(bf16), scal, wout_ref, wout_sent_ref)
            grad_key[...] = jnp.zeros_like(grad_key)
            grad_value[...] = jnp.zeros_like(grad_value)
            bias_ref[...] = jnp.zeros_like(bias_ref)
            for at in range(4):
                end = (at + 1) * rows
                spot = pl.ds(at * rows, rows)
                upto = pl.ds(0, end)
                for head in range(width // HD):
                    lanes = slice(head * HD, (head + 1) * HD)
                    queries = query_ref[spot, lanes]
                    given = grad_context[spot, lanes]
                    probs = probabilities(queries, keys[:end], start_ref[spot, :], at * rows)
                    low = probs.astype(bf16)
                    grad_probs = mm_nt(given, values[:end])
                    delta = jnp.sum(low.astype(f32) * grad_probs, axis=1, keepdims=True)
                    grad_scores = (probs * (grad_probs - delta)).astype(bf16)
                    grad_query = turned(
                        mm(grad_scores, keys[:end]) * scale, cos_ref[spot, :], sin_ref[spot, :], -1.0
                    )
                    grad_query_ref[spot, lanes] = grad_query.astype(bf16)
                    bias_ref[0:1, lanes] += jnp.sum(grad_query, axis=0, keepdims=True)
                    grad_key[upto, :] += mm_tn(grad_scores, queries)
                    grad_value[upto, :] += mm_tn(low, given)
            grad_keys = turned(grad_key[...] * scale, cos_ref[...], sin_ref[...], -1.0)
            grad_values = grad_value[...]
            bias_ref[0:1, width : width + HD] = jnp.sum(grad_keys, axis=0, keepdims=True)
            bias_ref[0:1, width + HD :] = jnp.sum(grad_values, axis=0, keepdims=True)
            kv_kept_ref[...] = jnp.where(is_value, grad_values, grad_keys)
            kv_sent_ref[...] = jnp.where(is_value, grad_keys, grad_values).astype(bf16)

        return pl.pallas_call(
            kernel,
            in_specs=[SCALARS] + [WHOLE] * 4 + [ANY] * 2 + [WHOLE] * 3 + [ANY] * dp_size,
            out_specs=[WHOLE] * 6,
            out_shape=[
                jax.ShapeDtypeStruct((tokens, width), bf16),
                jax.ShapeDtypeStruct((tokens, HD), f32),
                jax.ShapeDtypeStruct((tokens, HD), bf16),
                jax.ShapeDtypeStruct((8, width + 2 * HD), f32),
                jax.ShapeDtypeStruct((model // 2, width), bf16),
                jax.ShapeDtypeStruct((model // 2, width), bf16),
            ],
            scratch_shapes=[
                pltpu.VMEM((model, width), bf16),
                pltpu.VMEM((tokens, model), bf16),
                pltpu.VMEM((tokens, width), bf16),
                pltpu.VMEM((tokens, HD), f32),
                pltpu.VMEM((tokens, HD), f32),
                pltpu.SemaphoreType.DMA((dp_size + 4,)),
            ],
            name="attend_back",
        )(
            scalars, query, kv_own, kv_other, starts, pair, core, context, cosine, sine,
            *arrays_of(pieces),
        )

    def project_back(scalars, grad_query, kv_kept, kv_arrived, pieces, pair, core):
        tokens, width = grad_query.shape
        model, columns = pair.shape[1], pieces[0][0].shape[1]
        rows = tokens // 4

        def kernel(
            scal, query_ref, kept_kv_ref, arrived_ref, pair_ref, core_ref, *refs
        ):
            (
                grads_ref, kept_ref, sent_ref, gain_ref, held, part, acts, sems, out_sems,
            ) = refs[dp_size:]
            copies = start_all(
                attn_jobs(scal[0], refs[:dp_size], pieces, held)
                + token_jobs(scal[1], pair_ref, core_ref, acts),
                sems,
            )
            grads_ref[:, :width] = query_ref[...]
            grads_ref[:, width:] = (kept_kv_ref[...] + arrived_ref[...].astype(f32)).astype(bf16)
            wait_all(copies)
            for at in range(4):
                spot = pl.ds(at * rows, rows)
                part[spot, :] = mm_nt(grads_ref[spot, :], held[...]).astype(bf16)
            copies = start_all(back(token_jobs(scal[1], kept_ref, sent_ref, part)), out_sems)
            gain_ref[...] = jnp.zeros_like(gain_ref)
            for at in range(8):
                spot = pl.ds(at * rows // 2, rows // 2)
                gain_ref[0:1, :] += jnp.sum(
                    part[spot, :].astype(f32) * acts[spot, :].astype(f32), axis=0, keepdims=True
                )
            wait_all(copies)

        half = jax.ShapeDtypeStruct((tokens // 2, model), bf16)
        return pl.pallas_call(
            kernel,
            in_specs=[SCALARS, WHOLE, WHOLE, WHOLE, ANY, ANY] + [ANY] * dp_size,
            out_specs=[WHOLE, ANY, ANY, WHOLE],
            out_shape=[
                jax.ShapeDtypeStruct((tokens, columns), bf16),
                half,
                half,
                jax.ShapeDtypeStruct((8, model), f32),
            ],
            scratch_shapes=[
                pltpu.VMEM((model, columns), bf16),
                pltpu.VMEM((tokens, model), bf16),
                pltpu.VMEM((tokens, model), bf16),
                pltpu.SemaphoreType.DMA((dp_size + 4,)),
                pltpu.SemaphoreType.DMA((4,)),
            ],
            name="project_back",
        )(scalars, grad_query, kv_kept, kv_arrived, pair, core, *arrays_of(pieces))

    def project_grad(scalars, pair, core, grads):
        tokens, columns = grads.shape
        model = pair.shape[1]

        def kernel(scal, pair_ref, core_ref, grads_ref, kept_ref, sent_ref, acts, sems):
            wait_all(start_all(token_jobs(scal[1], pair_ref, core_ref, acts), sems))
            give(mm_tn(acts[...], grads_ref[...]).astype(bf16), scal, kept_ref, sent_ref)

        return pl.pallas_call(
            kernel,
            in_specs=[SCALARS, ANY, ANY, WHOLE],
            out_specs=[WHOLE] * 2,
            out_shape=[jax.ShapeDtypeStruct((model // 2, columns), bf16)] * 2,
            scratch_shapes=[
                pltpu.VMEM((tokens, model), bf16),
                pltpu.SemaphoreType.DMA((4,)),
            ],
            name="project_grad",
        )(scalars, pair, core, grads)

    def norm_two_back(scalars, own, from_x, from_l, hidden, gain, given):
        rows, model = own.shape

        def kernel(scal, own_ref, x_ref, l_ref, hidden_ref, gain_ref, given_ref, out_ref, low_ref, sum_ref):
            grad_out = own_ref[...] + x_ref[...].astype(f32) + l_ref[...].astype(f32)
            normed, row_scale = norm_forward(hidden_ref[...])
            grad_normed = grad_out * gain_ref[...]
            grad_in = row_scale * (
                grad_normed - normed * jnp.mean(grad_normed * normed, axis=-1, keepdims=True)
            )
            total = given_ref[...].astype(f32) + grad_in
            out_ref[...] = total
            low_ref[...] = total.astype(bf16)
            sum_ref[0:1, :] = jnp.sum(grad_out * normed, axis=0, keepdims=True)

        outs = [((rows, model), f32), ((rows, model), bf16), ((8, model), f32)]
        return whole_call(
            kernel, outs, "norm_two_back", scalars, own, from_x, from_l, hidden, gain, given
        )

    def local(
        block_input,
        segment_ids,
        gain_attn,
        w_query,
        b_query,
        w_keyval,
        b_keyval,
        w_out,
        gain_ffn,
        w_gate,
        w_up,
        w_down,
        cotangent,
    ):
        dp_index = lax.axis_index("dp")
        tensor_index = lax.axis_index("tensor")
        scalars = jnp.stack([dp_index, tensor_index]).astype(jnp.int32)
        local_heads = b_query.shape[0] // HD
        head_kv = tensor_index * local_heads // (HQ // KV)
        is_value = tensor_index % 2
        kv_column = is_value * (KV * HD) + head_kv * HD
        width = local_heads * HD

        groups = dp_size // 4

        def fold_rows(total, bit):
            flag = ((dp_index & bit) != 0).astype(jnp.int32)
            view = total.reshape(2, -1, total.shape[1])
            kept = lax.dynamic_index_in_dim(view, flag, 0, keepdims=False)
            sent = lax.dynamic_index_in_dim(view, 1 - flag, 0, keepdims=False)
            return kept, swap(sent.astype(bf16), "dp", bit)

        def far_rest(kept, sent):
            arrived = swap(sent, "dp", far_bits[0])
            for bit in far_bits[1:]:
                kept, sent = fold_sum(scalars, kept, arrived, bit, 1)
                arrived = swap(sent, "dp", bit)
            return kept, arrived

        keyval_cols = lax.dynamic_slice_in_dim(w_keyval, kv_column, HD, 1)
        qkv_own = jnp.concatenate([w_query, keyval_cols], axis=1)
        shard = qkv_own.shape[0]
        qkv_far = far_pieces(qkv_own)
        qkv_l = swap(qkv_own, "dp", pair_bit)
        qkv_y = swap(qkv_own, "dp", 1)
        rows_float = block_input.astype(f32)
        normed_one, scale_one = norm_forward(rows_float)
        act_own = (normed_one * gain_attn).astype(bf16)
        act_x = swap(act_own, "tensor", 2)
        gate_mine, gate_sent = split_cols(scalars, w_gate)
        gate_theirs = swap(gate_sent, "dp", pair_bit)

        qkv_far_in, qkv_l, qkv_y, out_own, w_up_in, w_down_in, segments = hold(
            [gate_sent, act_own],
            [tuple(qkv_far[1:]), qkv_l, qkv_y, w_out.T, w_up, w_down, segment_ids],
        )
        far_rows = rows_of(*qkv_far_in)
        qkv_y2 = swap(rows_of(qkv_l, far_rows), "dp", 1)
        qkv_l2 = swap(far_rows, "dp", pair_bit)
        out_far = far_pieces(out_own)
        rest_mine, rest_sent = split_cols(scalars, w_up_in, w_down_in.T)
        positions = positions_of(segments[0])
        cosine, sine = rotary(positions)
        sine = jnp.where(jnp.arange(HD)[None, :] < HD // 2, -sine, sine)
        starts = (jnp.arange(positions.shape[0], dtype=jnp.int32) - positions)[:, None]
        qkv_bias = jnp.concatenate([b_query, lax.dynamic_slice_in_dim(b_keyval, kv_column, HD, 0)])[
            None, :
        ]

        qkv_y2, qkv_l2, act_pair, gate_theirs, out_half, cosine, sine, starts, rest_sent, cot_own = (
            hold(
                [],
                [
                    qkv_y2,
                    qkv_l2,
                    rows_of(act_own, act_x),
                    gate_theirs,
                    rows_of(*out_far),
                    cosine,
                    sine,
                    starts,
                    rest_sent,
                    cotangent,
                ],
            )
        )
        gate_piece = join_rows(scalars, gate_mine, gate_theirs, 0, 1)
        (qkv_l2,) = hold([gate_piece], [qkv_l2])

        def gather_attn():
            return (
                swap(qkv_l2, "dp", 1),
                swap(act_pair, "tensor", 1),
                swap(out_half, "dp", pair_bit),
            )

        qkv_y3, act_c, out_l = section(gather_attn)

        qkv_y3, act_c, out_near, rest_sent, cot_core, gate_piece = hold(
            [], [qkv_y3, act_c, rows_of(out_half, out_l), rest_sent, cotangent, gate_piece]
        )
        gate_far = far_pieces(gate_piece)
        cot_x = swap(cot_core, "tensor", 2)
        rest_theirs = swap(rest_sent, "dp", pair_bit)
        out_y = swap(out_near, "dp", 1)
        far_masks = masks_of(far_bits)
        qkv_pieces = [(part, 0, mask) for part, mask in zip(qkv_far, far_masks)]
        qkv_pieces += [(qkv_l, 0, pair_bit), (qkv_y, 0, 1), (qkv_y2, 0, pair_bit ^ 1)]
        for at, mask in enumerate(far_masks[1:]):
            qkv_pieces += [
                (qkv_y2, (at + 1) * shard, mask ^ 1),
                (qkv_l2, at * shard, mask ^ pair_bit),
                (qkv_y3, at * shard, mask ^ pair_bit ^ 1),
            ]

        def attention():
            query_rot, kv_own = project(
                scalars, act_pair, act_c, qkv_pieces, qkv_bias, cosine, sine
            )
            kv_other = swap(kv_own, "tensor", 1)
            kv_other, cot_given = hold([], [kv_other, cot_core])
            cot_own_c = swap(cot_given, "tensor", 1)
            context = attend(scalars, query_rot, kv_own, kv_other, starts)
            context, cot_own_c = hold([], [context, cot_own_c])
            return query_rot, kv_own, kv_other, context, cot_own_c

        def out_pieces(near, far):
            pieces = []
            masks = masks_of(far_bits + [pair_bit])
            for at, mask in enumerate(masks):
                pieces += [(near, at * shard, mask), (far, at * shard, mask ^ 1)]
            return pieces

        query_rot, kv_own, kv_other, context, cot_own_c = section(attention)
        context, out_y = hold([], [context, out_y])
        out_parts = out_pieces(out_near, out_y)
        attn_kept, attn_sent = out_rows(scalars, context, out_parts, act_pair.shape[1])

        attn_sent, rest_theirs, cot_own_l = hold([cot_x], [attn_sent, rest_theirs, cotangent])

        def sum_cores():
            arrived = swap(attn_sent, "tensor", 1)
            return arrived, join_both(scalars, gate_piece, rest_mine, rest_theirs)

        attn_arrived, (up_piece, own_both) = section(sum_cores)
        attn_arrived, up_piece, own_both = hold([], [attn_arrived, up_piece, own_both])
        up_far = far_pieces(up_piece)
        own_y = swap(own_both, "dp", 1)
        cot_l = swap(cot_own_l, "dp", pair_bit)

        def sum_heads():
            own, sent = fold_fixed(scalars, attn_kept, attn_arrived, [0], [1])
            return norm_two(
                scalars, block_input, own, swap(sent, "tensor", 2), gain_ffn[None, :]
            )

        hidden, two_own = section(sum_heads)

        two_own, gate_halves = hold([cot_l], [two_own, tuple(gate_far[1:])])
        gate_y2 = [swap(part, "dp", 1) for part in gate_halves]

        def gather_near():
            two_x = swap(two_own, "tensor", 2)
            two_l = swap(two_own, "dp", pair_bit)
            return two_x, two_l, join_rows(scalars, rest_mine, rest_theirs, 1, 2)

        two_x, two_l, down_piece = section(gather_near)

        rows = two_own.shape[0]
        two_x, two_l, up_halves = hold([own_y, gate_y2], [two_x, two_l, tuple(up_far[1:])])
        up_y2 = [swap(part, "dp", 1) for part in up_halves]

        def gather_rest():
            given_a, given_b = halves(scalars, two_l, two_x)
            far_a = swap(given_a, "tensor", 2)
            far_b = swap(given_b, "dp", pair_bit)

            def cores():
                given, arrived = [two_x, two_l, two_own], []
                for at in range(3):
                    part = swap(given[at], "tensor", 1)
                    part, *given = hold([], [part] + given)
                    arrived.append(part)
                return arrived

            arrived = section(cores)
            return hold([], [far_a, far_b, *arrived])

        far_a, far_b, two_x_c, two_l_c, two_own_c = section(gather_rest)
        far_a, far_b, down_piece = hold(up_y2, [far_a, far_b, down_piece])
        down_far = far_pieces(down_piece)

        def gather_far():
            return swap(far_a, "tensor", 1), swap(far_b, "tensor", 1)

        far_a_c, far_b_c = section(gather_far)
        two_pieces = [two_own, two_x, two_l]
        two_pieces_c = [two_own_c, two_x_c, two_l_c]

        size = gate_piece.shape[0]
        gate_pieces = [(part, 0) for part in [*gate_far]] + [
            (part, 0) for part in [own_y, *gate_y2]
        ]
        up_pieces = [(part, 0) for part in [*up_far]] + [(own_y, size)] + [
            (part, 0) for part in up_y2
        ]
        far_a, far_b, far_a_c, far_b_c, down_piece_y, cot_x, cot_l = hold(
            [], [far_a, far_b, far_a_c, far_b_c, down_piece, cot_x, cot_l]
        )
        two_pieces += [far_a, far_b]
        two_pieces_c += [far_a_c, far_b_c]

        def feed_own():
            down_y1 = swap(down_piece_y, "dp", 1)
            cot_far = swap(cot_l, "tensor", 2)
            x_c = swap(cot_x, "tensor", 1)
            own = ffn_up(scalars, two_pieces, gate_pieces, up_pieces)
            down_y1, cot_far, x_c = hold([own], [down_y1, cot_far, x_c])
            return down_y1, cot_far, x_c, own

        down_y1, cot_far, cot_x_c, (acts_a, mixed_a, silu_a, back_a) = section(feed_own)

        mixed_a, cot_l_in = hold([], [mixed_a, cot_l])

        def feed_core():
            l_c = swap(cot_l_in, "tensor", 1)
            far_c = swap(cot_far, "tensor", 1)
            core = ffn_up(scalars, two_pieces_c, gate_pieces, up_pieces)
            l_c, far_c = hold([core], [l_c, far_c])
            return l_c, far_c, core

        cot_l_c, cot_far_c, (acts_b, mixed_b, silu_b, back_b) = section(feed_core)

        cots = [cotangent, cot_x, cot_l, cot_far]
        cots_c = [cot_own_c, cot_x_c, cot_l_c, cot_far_c]
        mixed_b, down_halves = hold([down_y1], [mixed_b, tuple(down_far[1:])])
        down_y2 = tuple(swap(part, "dp", 1) for part in down_halves)
        down_kept, down_sent = section(
            lambda: ffn_grad(scalars, cots, cots_c, mixed_a, mixed_b, "grad_down")
        )
        down_sent, down_y2 = hold([], [down_sent, down_y2])
        down_pieces = [(part, 0) for part in [*down_far, down_y1, *down_y2]]

        down_sent, silu_b = hold([], [down_sent, silu_b])
        down_sent = swap(down_sent, "dp", 1)

        def back_all():
            gate_b, up_b, two_sent = ffn_back(
                scalars, cots_c, down_pieces, gate_pieces, up_pieces, silu_b, back_b
            )
            (two_sent,) = hold([], [two_sent])
            arrived = swap(two_sent, "tensor", 1)
            gate_a, up_a, kept = ffn_back(
                scalars, cots, down_pieces, gate_pieces, up_pieces, silu_a, back_a
            )
            return (gate_a, up_a, gate_b, up_b, *spread_eight(scalars, kept, arrived))

        gate_a, up_a, gate_b, up_b, own, to_x, to_l, far_a, far_b = section(back_all)

        far_a, far_b, mixed_b = hold([], [far_a, far_b, mixed_b])
        model = far_a.shape[1]

        def spread_far():
            far_x = swap(far_a, "tensor", 2)
            far_l = swap(far_b, "dp", pair_bit)

            def block_rows():
                sent = ffn_rows(scalars, mixed_b, down_pieces, model, "block_rows")
                (sent,) = hold([], [sent])
                arrived = swap(sent, "tensor", 1)
                kept = ffn_rows(scalars, mixed_a, down_pieces, model, "block_rows")
                return hold([], [kept, arrived])

            outs = section(block_rows)
            outs, far_x, far_l = hold([], [outs, far_x, far_l])
            return (*outs, *spread_two(scalars, to_x, to_l, far_x, far_l))

        block_kept, block_arrived, to_x, to_l = section(spread_far)

        to_x, to_l, down_sent = hold([], [to_x, to_l, down_sent])

        def spread_near():
            from_x = swap(to_x, "tensor", 2)
            from_l = swap(to_l, "dp", pair_bit)
            up_grads = ffn_grad(scalars, [acts_a], [acts_b], up_a, up_b, "grad_up")
            down_pair = fold_sum(scalars, down_kept, down_sent, far_bits[0], 1)
            block_pair = fold_fixed(scalars, block_kept, block_arrived, [0, 1], [2, 3])
            from_x, from_l = hold([up_grads, down_pair, block_pair], [from_x, from_l])
            return (
                *up_grads,
                *down_pair,
                *block_pair,
                *norm_two_back(
                    scalars, own, from_x, from_l, hidden, gain_ffn[None, :], cotangent
                ),
            )

        (
            up_kept, up_sent, down_kept, down_sent, block_kept, block_sent,
            grad_hidden, attn_own, gain_two,
        ) = section(spread_near)

        attn_own, down_sent, up_sent, block_sent, gate_b = hold(
            [], [attn_own, down_sent, up_sent, block_sent, gate_b]
        )
        down_kept, down_sent = far_rest(down_kept, down_sent)
        up_sent = swap(up_sent, "dp", 1)
        block_sent = swap(block_sent, "dp", pair_bit)

        def attention_back():
            def gather_back():
                attn_x = swap(attn_own, "tensor", 2)
                gate_grads = ffn_grad(scalars, [acts_a], [acts_b], gate_a, gate_b, "grad_gate")
                (attn_x,) = hold([gate_grads], [attn_x])
                return (rows_of(attn_own, attn_x), *gate_grads)

            attn_half, gate_kept, gate_sent = section(gather_back)
            attn_half, gate_sent = hold([], [attn_half, gate_sent])
            attn_c = swap(attn_half, "tensor", 1)
            outs = attend_back(
                scalars, query_rot, kv_own, kv_other, starts, out_parts, attn_half, attn_c,
                context, cosine, sine,
            )
            return gate_kept, gate_sent, outs

        gate_kept, gate_sent, outs = section(attention_back)
        grad_query_low, kv_kept, kv_given, bias_rows, wout_kept, wout_sent = outs

        kv_given, wout_sent, gate_sent, down_sent, up_sent, block_sent = hold(
            [], [kv_given, wout_sent, gate_sent, down_sent, up_sent, block_sent]
        )
        wout_arrived = swap(wout_sent, "dp", pair_bit)
        devices = dp_size * tensor_size

        def input_grads():
            up_own, up_given = fold_sum(scalars, up_kept, up_sent, far_bits[0], 1)
            kv_in, gate_in, up_given = hold([], [kv_given, gate_sent, up_given])
            gate_y = swap(gate_in, "dp", 1)
            up_own, up_far_sum = far_rest(up_own, up_given)

            def project_all():
                kv_arrived = swap(kv_in, "tensor", 1)
                down_pair = fold_sum(scalars, down_kept, down_sent, pair_bit, 1)
                (kv_arrived,) = hold([down_pair], [kv_arrived])
                grad_qkv, one_kept, one_sent, gain_rows = project_back(
                    scalars, grad_query_low, kv_kept, kv_arrived, qkv_pieces, act_pair, act_c
                )
                arrived = swap(one_sent, "tensor", 1)
                wqkv_pair = project_grad(scalars, act_pair, act_c, grad_qkv)
                (arrived,) = hold([wqkv_pair], [arrived])
                wqkv_kept, wqkv_sent = wqkv_pair
                one_kept, one_sent = fold_fixed(scalars, one_kept, arrived, [0], [1])

                def first_norm_back():
                    arrived = swap(one_sent, "tensor", 2)
                    wqkv_arrived = swap(wqkv_sent, "dp", pair_bit)
                    block = block_step(scalars, block_kept, block_sent)
                    bias_keyval = jnp.zeros((2 * KV * HD,), f32)
                    bias_keyval = lax.dynamic_update_slice_in_dim(
                        bias_keyval, bias_rows[0, width : width + HD], head_kv * HD, 0
                    )
                    bias_keyval = lax.dynamic_update_slice_in_dim(
                        bias_keyval, bias_rows[0, width + HD :], KV * HD + head_kv * HD, 0
                    )
                    bias_query = lax.dynamic_update_slice_in_dim(
                        jnp.zeros((HQ * HD,), f32), bias_rows[0, :width], tensor_index * width, 0
                    )
                    parts = (gain_rows[0] / gain_attn, gain_two[0], bias_query, bias_keyval)
                    small = jnp.concatenate([part.reshape(devices, -1) for part in parts], axis=1)
                    (arrived,) = hold([block, small], [arrived])
                    grad_rows = norm_one_back(
                        scalars, block_input, one_kept, arrived, gain_attn[None, :], grad_hidden
                    )
                    (wqkv_arrived,) = hold([grad_rows], [wqkv_arrived])
                    return grad_rows, small, *block, wqkv_arrived

                return (*down_pair, wqkv_kept, *section(first_norm_back))

            outs = section(project_all)
            outs, gate_y, up_far_sum = hold([], [outs, gate_y, up_far_sum])
            return (up_own, up_far_sum, gate_y, *outs)

        (
            up_kept, up_sent, gate_sent, down_mine, down_given, wqkv_kept, grad_rows, small,
            block_own, block_sent, wqkv_arrived,
        ) = section(input_grads)

        wqkv_arrived, wout_arrived, gate_sent, small, down_given = hold(
            [], [wqkv_arrived, wout_arrived, gate_sent, small, down_given]
        )
        gate_kept, gate_sent = fold_sum(scalars, gate_kept, gate_sent, far_bits[0], 1)
        wqkv_arrived, gate_sent, small = hold([], [wqkv_arrived, gate_sent, small])
        gate_kept, gate_sent = far_rest(gate_kept, gate_sent)
        small = lax.all_to_all(small, ("dp", "tensor"), 0, 0, tiled=True)

        def last_rows():
            down_theirs = swap(down_given, "dp", pair_bit)
            block_x = swap(block_sent, "tensor", 2)

            def attn_step():
                wqkv_own, wqkv_sent = fold_sum(scalars, wqkv_kept, wqkv_arrived, 1, groups)
                wout_own, wout_sent = fold_sum(scalars, wout_kept, wout_arrived, 1, groups)
                wqkv_y = swap(wqkv_sent, "dp", 1)
                wout_y = swap(wout_sent, "dp", 1)
                up_pair = fold_sum(scalars, up_kept, up_sent, pair_bit, 1)
                wqkv_y, wout_y = hold([up_pair], [wqkv_y, wout_y])
                total = jnp.concatenate([add(wqkv_own, wqkv_y), add(wout_own, wout_y)], axis=1)
                return total, up_pair

            total, up_pair = section(attn_step)
            total, down_theirs, block_x, up_given = hold(
                [], [total, down_theirs, block_x, up_pair[1]]
            )
            up_theirs = swap(up_given, "dp", pair_bit)
            for bit in far_bits[:-1]:
                total = add(*fold_rows(total, bit))
            flag = ((dp_index & far_bits[-1]) != 0).astype(jnp.int32)
            view = total.reshape(2, -1, total.shape[1])
            kept = lax.dynamic_index_in_dim(view, flag, 0, keepdims=False)
            sent = lax.dynamic_index_in_dim(view, 1 - flag, 0, keepdims=False).astype(bf16)
            block_out = (hidden + add(block_own, block_x)).astype(bf16)
            down_share = join_cols(scalars, down_mine, down_theirs, w_down.shape[0] // 2).T
            (up_theirs,) = hold([kept, sent, block_out, down_share], [up_theirs])
            return kept, sent, up_pair[0], up_theirs, block_out, down_share

        attn_kept, attn_sent, up_mine, up_theirs, block_out, down_share = section(last_rows)

        gate_sent, attn_sent, up_theirs, small = hold(
            [block_out, down_share], [gate_sent, attn_sent, up_theirs, small]
        )
        small = jnp.sum(small, axis=0)
        attn_sent = swap(attn_sent, "dp", far_bits[-1])
        gate_mine, gate_given = fold_sum(scalars, gate_kept, gate_sent, pair_bit, 1)
        gate_theirs = swap(gate_given, "dp", pair_bit)
        (up_theirs,) = hold([gate_given], [up_theirs])
        up_share = join_cols(scalars, up_mine, up_theirs, w_up.shape[1] // 2)
        (attn_sent,) = hold([up_share], [attn_sent])
        share = add(attn_kept, attn_sent)
        kv_rows = share[:, width : width + HD]
        share_rows = kv_rows.shape[0] // tensor_size
        moved = []
        for mask in range(tensor_size):
            rows_for = lax.dynamic_slice_in_dim(
                kv_rows, (tensor_index ^ mask) * share_rows, share_rows, 0
            )
            moved.append(swap(rows_for, "tensor", mask) if mask else rows_for)
        query_share, out_share = share[:, :width], share[:, width + HD :].T
        gate_theirs, *moved = hold([query_share, out_share], [gate_theirs] + moved)
        gate_share = join_cols(scalars, gate_mine, gate_theirs, w_gate.shape[1] // 2)
        keyval_share = jnp.zeros((share_rows, 2 * KV * HD), f32)
        for mask in range(tensor_size):
            sender = tensor_index ^ mask
            column = (sender % 2) * (KV * HD) + (sender * local_heads // (HQ // KV)) * HD
            keyval_share = lax.dynamic_update_slice_in_dim(keyval_share, moved[mask], column, 1)
        sizes = [HQ * HD // devices, 2 * KV * HD // devices, gain_attn.shape[0] // devices]
        ends = [sizes[2], 2 * sizes[2], 2 * sizes[2] + sizes[0]]
        gain_one_share = small[: ends[0]]
        gain_two_share = small[ends[0] : ends[1]]
        query_bias_share = small[ends[1] : ends[2]]
        keyval_bias_share = small[ends[2] :]
        return (
            block_out,
            grad_rows,
            gain_one_share,
            query_share,
            query_bias_share,
            keyval_share,
            keyval_bias_share,
            out_share,
            gain_two_share,
            gate_share,
            up_share,
            down_share,
        )

    placed = (
        P(("dp", "tensor"), None),
        P("dp", None),
        P(),
        P("dp", "tensor"),
        P("tensor"),
        P("dp", None),
        P(),
        P("tensor", "dp"),
        P(),
        P("dp", "tensor"),
        P("dp", "tensor"),
        P("tensor", "dp"),
        P(("dp", "tensor"), None),
    )
    return jax.shard_map(
        local,
        mesh=mesh,
        in_specs=placed,
        out_specs=(
            P(("dp", "tensor"), None),
            P(("dp", "tensor"), None),
            P(("dp", "tensor")),
            P("dp", "tensor"),
            P(("dp", "tensor")),
            P(("dp", "tensor"), None),
            P(("dp", "tensor")),
            P("tensor", "dp"),
            P(("dp", "tensor")),
            P("dp", "tensor"),
            P("dp", "tensor"),
            P("tensor", "dp"),
        ),
        check_vma=False,
    )
```

```python
import math

import jax
import jax.numpy as jnp
from jax import lax
from jax.experimental import pallas as pl
from jax.experimental.pallas import tpu as pltpu
from jax.sharding import PartitionSpec as P

HQ = 12
KV = 2
HD = 128


epsilon = 1e-06
rope_base = 1000000.0
masked_score = -1e30
bf16 = jnp.bfloat16
f32 = jnp.float32


def positions_of(segment_row):
    index_row = jnp.arange(segment_row.shape[0], dtype=jnp.int32)
    starts = jnp.concatenate(
        [jnp.ones((1,), jnp.int32), (segment_row[1:] != segment_row[:-1]).astype(jnp.int32)]
    )
    first_index = lax.cummax(jnp.where(starts > 0, index_row, 0), axis=0)
    return index_row - first_index


def rotary(positions):
    inverse = rope_base ** (-(jnp.arange(HD // 2, dtype=jnp.float32) * 2.0 / HD))
    angles = positions.astype(jnp.float32)[:, None] * inverse[None, :]
    angles = jnp.concatenate([angles, angles], axis=1)
    return (jnp.cos(angles), jnp.sin(angles))


def norm_forward(values_in):
    row_scale = lax.rsqrt(jnp.mean(values_in * values_in, axis=-1, keepdims=True) + epsilon)
    return (values_in * row_scale, row_scale)


def norm_backward(grad_out, normed, row_scale, gain_vec):
    grad_normed = grad_out * gain_vec
    grad_in = row_scale * (
        grad_normed - normed * jnp.mean(grad_normed * normed, axis=-1, keepdims=True)
    )
    return (grad_in, jnp.sum(grad_out * normed, axis=0))


ANY = pl.BlockSpec(memory_space=pl.ANY)
WHOLE = pl.BlockSpec(memory_space=pltpu.VMEM)
SCALARS = pl.BlockSpec(memory_space=pltpu.SMEM)


def made(jobs, sems, first=0):
    return [
        pltpu.make_async_copy(src, dst, sems.at[first + at]) for at, (src, dst) in enumerate(jobs)
    ]


def start_all(jobs, sems):
    copies = made(jobs, sems)
    for copy in copies:
        copy.start()
    return copies


def wait_all(copies):
    for copy in copies:
        copy.wait()


def block(ref, at, rows):
    return ref.at[pl.ds(pl.multiple_of(at * rows, rows), rows)]


def turned(values, cosine, sine, sign):
    return values * cosine + sign * (pltpu.roll(values, HD // 2, 1) * sine)


def mm(left, right):
    return lax.dot_general(left, right, (((1,), (0,)), ((), ())), preferred_element_type=f32)


def mm_nt(left, right):
    return lax.dot_general(left, right, (((1,), (1,)), ((), ())), preferred_element_type=f32)


def mm_tn(left, right):
    return lax.dot_general(left, right, (((0,), (0,)), ((), ())), preferred_element_type=f32)


def hold(due, release):
    out = lax.optimization_barrier((tuple(due), tuple(release)))
    return out[1]


def section(body):
    outs = jax.eval_shape(body)
    return lax.cond(
        lax.optimization_barrier(jnp.bool_(True)),
        body,
        lambda: jax.tree.map(lambda out: jnp.zeros(out.shape, out.dtype), outs),
    )


def solution(mesh):
    dp_size = mesh.shape["dp"]
    tensor_size = mesh.shape["tensor"]
    pair_bit = 2
    far_bits = []
    bit = dp_size // 2
    while bit > pair_bit:
        far_bits.append(bit)
        bit //= 2
    ring_bits = far_bits + [1]

    def swap(array, axis, bit):
        size = mesh.shape[axis]
        with jax.named_scope(f"swap_{axis}_{bit}"):
            return lax.ppermute(array, axis, [(i, i ^ bit) for i in range(size)])

    def masks_of(bits):
        masks = [0]
        for bit in bits:
            masks = masks + [mask ^ bit for mask in masks]
        return masks

    def rows_of(*pieces):
        return jnp.concatenate(pieces, axis=0)

    def far_pieces(piece):
        pieces = [piece]
        for bit in far_bits:
            pieces = pieces + [swap(part, "dp", bit) for part in pieces]
        return pieces

    def fold(total, axis, bit):
        half = total.shape[0] // 2
        return total[:half], swap(total[half:].astype(bf16), axis, bit)

    def add(kept, arrived):
        return kept.astype(f32) + arrived.astype(f32)

    ring_masks = masks_of(ring_bits)
    ring_mask = sum(ring_bits)
    count = len(ring_masks)


    def ffn_jobs(dp_index, refs, offsets, held):
        rows = held.shape[0] // dp_size
        jobs = []
        for mask, ref, offset in zip(ring_masks, refs, offsets):
            base = jnp.bitwise_xor(jnp.bitwise_and(dp_index, ring_mask), mask)
            for low in (0, 1):
                jobs.append(
                    (
                        ref.at[pl.ds(offset + low * rows, rows)],
                        block(held, base + low * pair_bit, rows),
                    )
                )
        return jobs

    def row_jobs(refs, held):
        jobs, start = [], 0
        for ref in refs:
            jobs.append((ref, held.at[pl.ds(start, ref.shape[0])]))
            start += ref.shape[0]
        return jobs

    def attn_jobs(dp_index, refs, pieces, held):
        rows = held.shape[0] // dp_size
        return [
            (
                ref.at[pl.ds(first, rows)],
                block(held, jnp.bitwise_xor(dp_index, mask), rows),
            )
            for ref, (_, first, mask) in zip(refs, pieces)
        ]

    def arrays_of(pieces):
        return [piece[0] for piece in pieces]

    token_masks = ((0, 2), (1, 3))

    def token_jobs(tensor_index, pair, other, held):
        rows = held.shape[0] // 4
        jobs = []
        for masks, ref in zip(token_masks, (pair, other)):
            for at, mask in enumerate(masks):
                spot = jnp.bitwise_xor(tensor_index, mask)
                jobs.append((ref.at[pl.ds(at * rows, rows)], block(held, spot, rows)))
        return jobs

    def quarter_jobs(tensor_index, refs, held):
        rows = held.shape[0] // 4
        return [
            (ref, block(held, jnp.bitwise_xor(tensor_index, mask), rows))
            for ref, mask in zip(refs, (0, 2, 1, 3))
        ]

    def back(jobs):
        return [(dst, src) for src, dst in jobs]

    def ffn_up(scalars, pieces, gate_pieces, up_pieces):
        tokens, model = sum(piece.shape[0] for piece in pieces), pieces[0].shape[1]
        units = gate_pieces[0][0].shape[1]
        rows = tokens // 2
        many = len(pieces)
        early = 2

        def kernel(scal, *refs):
            parts = refs[:many]
            gates = refs[many : many + count]
            ups = refs[many + count : many + 2 * count]
            acts_ref, mixed_ref, silu_ref, back_ref, acts, gate_w, up_w, sems = refs[
                many + 2 * count :
            ]
            jobs = row_jobs(parts, acts)
            gate_jobs = ffn_jobs(scal[0], gates, [at for _, at in gate_pieces], gate_w)
            up_jobs = ffn_jobs(scal[0], ups, [at for _, at in up_pieces], up_w)
            step = pl.program_id(0)

            @pl.when(step == 0)
            def _():
                copies = start_all(jobs[:early] + gate_jobs + jobs[early:] + up_jobs, sems)
                wait_all(copies[: early + 2 * count])

            @pl.when(step == 1)
            def _():
                wait_all(made(jobs[early:], sems, early + 2 * count))

            spot = pl.ds(pl.multiple_of(step * rows, rows), rows)
            rows_in = acts[spot, :]
            acts_ref[...] = rows_in
            gate = mm(rows_in, gate_w[...])

            @pl.when(step == 0)
            def _():
                wait_all(made(up_jobs, sems, many + 2 * count))

            up = mm(rows_in, up_w[...])
            sig = jax.nn.sigmoid(gate)
            silu = gate * sig
            mixed_ref[...] = (silu * up).astype(bf16)
            silu_ref[...] = silu.astype(bf16)
            back_ref[...] = (up * sig * (1.0 + gate * (1.0 - sig))).astype(bf16)

        out = jax.ShapeDtypeStruct((tokens, units), bf16)
        spec = pl.BlockSpec((rows, units), lambda i: (i, 0))
        return pl.pallas_call(
            kernel,
            grid=(2,),
            in_specs=[SCALARS] + [ANY] * (many + 2 * count),
            out_specs=[pl.BlockSpec((rows, model), lambda i: (i, 0))] + [spec] * 3,
            out_shape=[jax.ShapeDtypeStruct((tokens, model), bf16)] + [out] * 3,
            scratch_shapes=[
                pltpu.VMEM((tokens, model), bf16),
                pltpu.VMEM((model, units), bf16),
                pltpu.VMEM((model, units), bf16),
                pltpu.SemaphoreType.DMA((many + 4 * count,)),
            ],
            name="ffn_up",
        )(
            scalars,
            *pieces,
            *[ref for ref, _ in gate_pieces],
            *[ref for ref, _ in up_pieces],
        )

    def ffn_back(scalars, cots, down_pieces, gate_pieces, up_pieces, silu, back_part):
        many = len(cots)
        tokens, model = sum(piece.shape[0] for piece in cots), cots[0].shape[1]
        units = silu.shape[1]
        rows = tokens // 2
        lists = (down_pieces, gate_pieces, up_pieces)

        def kernel(scal, *refs):
            parts = refs[:many]
            pieces = [refs[many + at * count : many + (at + 1) * count] for at in range(3)]
            silu_ref, back_ref, grad_gate_ref, grad_up_ref, out_ref = refs[
                many + 3 * count : many + 3 * count + 5
            ]
            cot, *held = refs[many + 3 * count + 5 : -1]
            sems = refs[-1]
            jobs = row_jobs(parts, cot)
            for at in range(3):
                jobs += ffn_jobs(scal[0], pieces[at], [spot for _, spot in lists[at]], held[at])
            first = pl.program_id(0) == 0
            early = many + 2 * count

            @pl.when(first)
            def _():
                wait_all(start_all(jobs, sems)[:early])

            spot = pl.ds(pl.multiple_of(pl.program_id(0) * rows, rows), rows)
            grad_mixed = mm(cot[spot, :], held[0][...])
            grad_gate = (grad_mixed * back_ref[...].astype(f32)).astype(bf16)
            grad_up = (grad_mixed * silu_ref[...].astype(f32)).astype(bf16)
            grad_gate_ref[...] = grad_gate
            grad_up_ref[...] = grad_up

            @pl.when(first)
            def _():
                wait_all(made(jobs[early:], sems, early))

            out_ref[...] = (
                mm_nt(grad_gate, held[1][...]) + mm_nt(grad_up, held[2][...])
            ).astype(bf16)

        out = jax.ShapeDtypeStruct((tokens, units), bf16)
        spec = pl.BlockSpec((rows, units), lambda i: (i, 0))
        wide = pl.BlockSpec((rows, model), lambda i: (i, 0))
        return pl.pallas_call(
            kernel,
            grid=(2,),
            in_specs=[SCALARS] + [ANY] * (many + 3 * count) + [spec, spec],
            out_specs=[spec, spec, wide],
            out_shape=[out, out, jax.ShapeDtypeStruct((tokens, model), bf16)],
            scratch_shapes=[pltpu.VMEM((tokens, model), bf16)]
            + [pltpu.VMEM((model, units), bf16)] * 3
            + [pltpu.SemaphoreType.DMA((many + 6 * count,))],
            name="ffn_back",
        )(scalars, *cots, *[ref for pieces in lists for ref, _ in pieces], silu, back_part)

    def ffn_rows(scalars, left, pieces, model, name):
        tokens, units = left.shape
        rows = tokens // 2

        def kernel(scal, left_ref, *refs):
            parts = refs[:count]
            out_ref, held, sems = refs[count:]

            @pl.when(pl.program_id(0) == 0)
            def _():
                wait_all(
                    start_all(ffn_jobs(scal[0], parts, [at for _, at in pieces], held), sems)
                )

            out_ref[...] = mm_nt(left_ref[...], held[...]).astype(bf16)

        return pl.pallas_call(
            kernel,
            grid=(2,),
            in_specs=[SCALARS, pl.BlockSpec((rows, units), lambda i: (i, 0))] + [ANY] * count,
            out_specs=pl.BlockSpec((rows, model), lambda i: (i, 0)),
            out_shape=jax.ShapeDtypeStruct((tokens, model), bf16),
            scratch_shapes=[
                pltpu.VMEM((model, units), bf16),
                pltpu.SemaphoreType.DMA((2 * count,)),
            ],
            name=name,
        )(scalars, left, *[ref for ref, _ in pieces])

    def ffn_grad(scalars, own_pieces, core_pieces, low, high, name):
        pieces = [*own_pieces, *core_pieces]
        many = len(own_pieces)
        tokens, model = low.shape[0], pieces[0].shape[1]
        units = low.shape[1]
        shard = model // dp_size
        wide = 384
        groups = wide // (2 * shard)

        def kernel(scal, *refs):
            def stack(parts):
                values = [part[...] for part in parts]
                return values[0] if len(values) == 1 else jnp.concatenate(values, axis=0)

            low_ref, high_ref, kept_ref, sent_ref = refs[2 * many :]
            total = mm_tn(stack(refs[:many]), low_ref[...])
            total = total + mm_tn(stack(refs[many : 2 * many]), high_ref[...])
            total = total.astype(bf16)
            odd = jnp.bitwise_and(scal[0], 1) == 1
            for group in range(groups):
                first = total[group * 2 * shard : group * 2 * shard + shard]
                second = total[group * 2 * shard + shard : (group + 1) * 2 * shard]
                spot = pl.ds(group * shard, shard)
                kept_ref[spot, :] = jnp.where(odd, second, first)
                sent_ref[spot, :] = jnp.where(odd, first, second)

        out = jax.ShapeDtypeStruct((model // 2, units), bf16)
        spec = pl.BlockSpec((wide // 2, units), lambda i: (i, 0))
        whole = pl.BlockSpec((tokens, units), lambda i: (0, 0))
        return pl.pallas_call(
            kernel,
            grid=(model // wide,),
            in_specs=[SCALARS]
            + [pl.BlockSpec((piece.shape[0], wide), lambda i: (0, i)) for piece in pieces]
            + [whole, whole],
            out_specs=[spec] * 2,
            out_shape=[out] * 2,
            name=name,
        )(scalars, *pieces, low, high)

    def is_high(scal, bit):
        return jnp.bitwise_and(scal[0], bit) != 0

    def whole_call(kernel, outs, name, *args):
        return pl.pallas_call(
            kernel,
            in_specs=[SCALARS] + [WHOLE] * (len(args) - 1),
            out_specs=[WHOLE] * len(outs),
            out_shape=[jax.ShapeDtypeStruct(shape, kind) for shape, kind in outs],
            name=name,
        )(*args)

    def split_cols(scalars, *arrays):
        rows, half = arrays[0].shape[0], arrays[0].shape[1] // 2
        wide = -(-half // 128) * 128
        many = len(arrays)

        def kernel(scal, *refs):
            mine_ref, sent_ref = refs[many:]
            flag = is_high(scal, pair_bit)
            mine_ref[...] = jnp.zeros_like(mine_ref)
            sent_ref[...] = jnp.zeros_like(sent_ref)
            for at in range(many):
                low, high = refs[at][:, :half], refs[at][:, half:]
                mine_ref[at * rows : (at + 1) * rows, :half] = jnp.where(flag, high, low)
                sent_ref[at * rows : (at + 1) * rows, :half] = jnp.where(flag, low, high)

        return whole_call(
            kernel, [((many * rows, wide), bf16)] * 2, "split_cols", scalars, *arrays
        )

    def join_rows(scalars, mine, theirs, at, many):
        rows, columns = mine.shape[0] // many, mine.shape[1]
        spot = pl.ds(at * rows, rows)

        def kernel(scal, mine_ref, theirs_ref, out_ref):
            flag = is_high(scal, pair_bit)
            out_ref[:rows, :] = jnp.where(flag, theirs_ref[spot, :], mine_ref[spot, :])
            out_ref[rows:, :] = jnp.where(flag, mine_ref[spot, :], theirs_ref[spot, :])

        return whole_call(
            kernel, [((2 * rows, columns), bf16)], "join_rows", scalars, mine, theirs
        )[0]

    def join_cols(scalars, mine, theirs, columns):
        rows = mine.shape[0]

        def kernel(scal, mine_ref, theirs_ref, out_ref):
            flag = is_high(scal, pair_bit)
            mine = mine_ref[:, :columns].astype(f32)
            theirs = theirs_ref[:, :columns].astype(f32)
            out_ref[:, :columns] = jnp.where(flag, theirs, mine)
            out_ref[:, columns:] = jnp.where(flag, mine, theirs)

        return whole_call(
            kernel, [((rows, 2 * columns), f32)], "join_cols", scalars, mine, theirs
        )[0]

    def fold_sum(scalars, kept, arrived, bit, outer):
        rows, columns = kept.shape[0] // 2, kept.shape[1]
        part = rows // outer

        def kernel(scal, kept_ref, arrived_ref, own_ref, sent_ref):
            flag = is_high(scal, bit)
            for at in range(outer):
                first = pl.ds(2 * at * part, part)
                second = pl.ds((2 * at + 1) * part, part)
                low = kept_ref[first, :].astype(f32) + arrived_ref[first, :].astype(f32)
                high = kept_ref[second, :].astype(f32) + arrived_ref[second, :].astype(f32)
                spot = pl.ds(at * part, part)
                own_ref[spot, :] = jnp.where(flag, high, low).astype(bf16)
                sent_ref[spot, :] = jnp.where(flag, low, high).astype(bf16)

        return whole_call(
            kernel, [((rows, columns), bf16)] * 2, "fold_sum", scalars, kept, arrived
        )

    def norm_two(scalars, rows_in, kept, sums, arrived, gain):
        rows, columns = rows_in.shape

        def kernel(scal, kept_ref, sums_ref, in_ref, arrived_ref, gain_ref, hidden_ref, out_ref):
            hidden = in_ref[...].astype(f32) + kept_ref[...].astype(f32)
            hidden = hidden + sums_ref[...].astype(f32) + arrived_ref[...].astype(f32)
            hidden_ref[...] = hidden
            out_ref[...] = (norm_forward(hidden)[0] * gain_ref[...]).astype(bf16)

        return part_call(
            kernel, [((rows, columns), f32), ((rows, columns), bf16)], "norm_two", scalars,
            [(kept, rows, 0), (sums, rows, 0)], [rows_in, arrived, gain],
        )

    def norm_one_back(scalars, rows_in, kept, sums, arrived, gain, given):
        rows, columns = rows_in.shape

        def kernel(scal, kept_ref, sums_ref, in_ref, arrived_ref, gain_ref, given_ref, out_ref):
            grad_out = kept_ref[...].astype(f32) + sums_ref[...].astype(f32)
            grad_out = grad_out + arrived_ref[...].astype(f32)
            normed, row_scale = norm_forward(in_ref[...].astype(f32))
            grad_normed = grad_out * gain_ref[...]
            grad_in = row_scale * (
                grad_normed - normed * jnp.mean(grad_normed * normed, axis=-1, keepdims=True)
            )
            out_ref[...] = (given_ref[...] + grad_in).astype(bf16)

        return part_call(
            kernel, [((rows, columns), bf16)], "norm_one_back", scalars,
            [(kept, rows, 0), (sums, rows, 0)], [rows_in, arrived, gain, given],
        )[0]

    def join_both(scalars, first, mine, theirs):
        rows, columns = mine.shape[0] // 2, mine.shape[1]

        def kernel(scal, first_ref, mine_ref, theirs_ref, out_ref, both_ref):
            flag = is_high(scal, pair_bit)
            low = jnp.where(flag, theirs_ref[:rows, :], mine_ref[:rows, :])
            high = jnp.where(flag, mine_ref[:rows, :], theirs_ref[:rows, :])
            out_ref[:rows, :] = low
            out_ref[rows:, :] = high
            both_ref[: 2 * rows, :] = first_ref[...]
            both_ref[2 * rows : 3 * rows, :] = low
            both_ref[3 * rows :, :] = high

        return whole_call(
            kernel,
            [((2 * rows, columns), bf16), ((4 * rows, columns), bf16)],
            "join_both", scalars, first, mine, theirs,
        )

    def halves(scalars, first, second):
        rows, columns = first.shape[0] // 2, first.shape[1]

        def kernel(scal, first_ref, second_ref, out_a_ref, out_b_ref):
            out_a_ref[...] = first_ref[:rows, :]
            out_b_ref[...] = second_ref[rows:, :]

        return whole_call(
            kernel, [((rows, columns), bf16)] * 2, "halves", scalars, first, second
        )

    def fold_both(scalars, first, first_arrived, second, second_arrived, bit, outer):
        rows = first.shape[0] // 2
        columns = (first.shape[1], second.shape[1])
        part = rows // outer

        def kernel(scal, first_ref, first_in_ref, second_ref, second_in_ref, own_ref, sent_ref):
            flag = is_high(scal, bit)
            for lanes, kept_ref, arrived_ref in (
                (slice(0, columns[0]), first_ref, first_in_ref),
                (slice(columns[0], columns[0] + columns[1]), second_ref, second_in_ref),
            ):
                for at in range(outer):
                    low_spot = pl.ds(2 * at * part, part)
                    high_spot = pl.ds((2 * at + 1) * part, part)
                    low = kept_ref[low_spot, :].astype(f32) + arrived_ref[low_spot, :].astype(f32)
                    high = kept_ref[high_spot, :].astype(f32) + arrived_ref[high_spot, :].astype(f32)
                    spot = pl.ds(at * part, part)
                    own_ref[spot, lanes] = jnp.where(flag, high, low)
                    sent_ref[spot, lanes] = jnp.where(flag, low, high).astype(bf16)

        outs = [((rows, sum(columns)), f32), ((rows, sum(columns)), bf16)]
        return whole_call(
            kernel, outs, "fold_both", scalars, first, first_arrived, second, second_arrived
        )

    def rows_block(rows, columns, at):
        return pl.BlockSpec((rows, columns), lambda i: (at, 0))

    def part_call(kernel, outs, name, scalars, parts, rest):
        return pl.pallas_call(
            kernel,
            grid=(1,),
            in_specs=[SCALARS]
            + [rows_block(rows, array.shape[1], at) for array, rows, at in parts]
            + [WHOLE] * len(rest),
            out_specs=[WHOLE] * len(outs),
            out_shape=[jax.ShapeDtypeStruct(shape, kind) for shape, kind in outs],
            name=name,
        )(scalars, *[array for array, _, _ in parts], *rest)

    def part_sum(scalars, kept, arrived, rows, at, pieces):
        columns, size = kept.shape[1], rows // pieces

        def kernel(scal, kept_ref, arrived_ref, *out_refs):
            for piece, ref in enumerate(out_refs):
                spot = pl.ds(piece * size, size)
                ref[...] = (
                    kept_ref[spot, :].astype(f32) + arrived_ref[spot, :].astype(f32)
                ).astype(bf16)

        return part_call(
            kernel, [((size, columns), bf16)] * pieces, "part_sum", scalars,
            [(kept, rows, at), (arrived, rows, at)], [],
        )

    def spread_rest(scalars, kept, arrived, far_x, far_l):
        rows, columns = kept.shape[0] // 4, kept.shape[1]
        half = rows // 2

        def kernel(scal, *refs):
            keeps, arrives = refs[:3], refs[3:6]
            far_x_ref, far_l_ref, own_ref, x_ref, l_ref = refs[6:]
            own_ref[...] = keeps[0][...].astype(f32) + arrives[0][...].astype(f32)
            to_x = keeps[1][...].astype(f32) + arrives[1][...].astype(f32)
            x_ref[:half, :] = to_x[:half].astype(bf16)
            x_ref[half:, :] = (to_x[half:] + far_l_ref[...].astype(f32)).astype(bf16)
            to_l = keeps[2][...].astype(f32) + arrives[2][...].astype(f32)
            l_ref[:half, :] = (to_l[:half] + far_x_ref[...].astype(f32)).astype(bf16)
            l_ref[half:, :] = to_l[half:].astype(bf16)

        outs = [((rows, columns), f32), ((rows, columns), bf16), ((rows, columns), bf16)]
        return part_call(
            kernel, outs, "spread_rest", scalars,
            [(array, rows, at) for array in (kept, arrived) for at in range(3)], [far_x, far_l],
        )

    def block_x_sum(scalars, kept, arrived, from_l):
        rows, columns = kept.shape[0] // 4, kept.shape[1]

        def kernel(scal, kept_ref, arrived_ref, from_ref, out_ref):
            out_ref[...] = (
                kept_ref[...].astype(f32)
                + arrived_ref[...].astype(f32)
                + from_ref[...].astype(f32)
            ).astype(bf16)

        return part_call(
            kernel, [((rows, columns), bf16)], "block_x_sum", scalars,
            [(kept, rows, 1), (arrived, rows, 1), (from_l, rows, 1)], [],
        )[0]

    def block_final(scalars, kept, arrived, from_l, hidden, from_x):
        rows, columns = hidden.shape

        def kernel(scal, kept_ref, arrived_ref, from_ref, hidden_ref, x_ref, out_ref):
            total = hidden_ref[...] + kept_ref[...].astype(f32) + arrived_ref[...].astype(f32)
            out_ref[...] = (total + from_ref[...].astype(f32) + x_ref[...].astype(f32)).astype(bf16)

        return part_call(
            kernel, [((rows, columns), bf16)], "block_final", scalars,
            [(kept, rows, 0), (arrived, rows, 0), (from_l, rows, 0)], [hidden, from_x],
        )[0]

    def give(total, scal, kept_ref, sent_ref):
        part = pair_bit * (total.shape[0] // dp_size)
        flag = is_high(scal, pair_bit)
        for at in range(total.shape[0] // (2 * part)):
            low = total[2 * at * part : (2 * at + 1) * part]
            high = total[(2 * at + 1) * part : (2 * at + 2) * part]
            kept_ref[pl.ds(at * part, part), :] = jnp.where(flag, high, low)
            sent_ref[pl.ds(at * part, part), :] = jnp.where(flag, low, high)

    def project(scalars, pair, core, pieces, bias, cosine, sine):
        tokens, model = 2 * pair.shape[0], pair.shape[1]
        columns = pieces[0][0].shape[1]
        width = columns - HD

        def kernel(scal, pair_ref, core_ref, bias_ref, cos_ref, sin_ref, *refs):
            query_ref, kv_ref, acts, held, sems = refs[dp_size:]
            wait_all(
                start_all(
                    attn_jobs(scal[0], refs[:dp_size], pieces, held)
                    + token_jobs(scal[1], pair_ref, core_ref, acts),
                    sems,
                )
            )
            is_value = jnp.bitwise_and(scal[1], 1) == 1
            rows = tokens // 4
            for at in range(4):
                spot = pl.ds(at * rows, rows)
                out = mm(acts[spot, :], held[...]) + bias_ref[...]
                cosine_rows, sine_rows = cos_ref[spot, :], sin_ref[spot, :]
                for head in range(width // HD):
                    query_ref[spot, head * HD : (head + 1) * HD] = turned(
                        out[:, head * HD : (head + 1) * HD], cosine_rows, sine_rows, 1.0
                    ).astype(bf16)
                kv = out[:, width:]
                kv_ref[spot, :] = jnp.where(
                    is_value, kv, turned(kv, cosine_rows, sine_rows, 1.0)
                ).astype(bf16)

        return pl.pallas_call(
            kernel,
            in_specs=[SCALARS, ANY, ANY, WHOLE, WHOLE, WHOLE] + [ANY] * dp_size,
            out_specs=[WHOLE, WHOLE],
            out_shape=[
                jax.ShapeDtypeStruct((tokens, width), bf16),
                jax.ShapeDtypeStruct((tokens, HD), bf16),
            ],
            scratch_shapes=[
                pltpu.VMEM((tokens, model), bf16),
                pltpu.VMEM((model, columns), bf16),
                pltpu.SemaphoreType.DMA((dp_size + 4,)),
            ],
            name="project",
        )(scalars, pair, core, bias, cosine, sine, *arrays_of(pieces))

    def probabilities(query, keys, start_rows, first):
        scores = mm_nt(query, keys) * (1.0 / math.sqrt(HD))
        column = lax.broadcasted_iota(jnp.int32, scores.shape, 1)
        row = lax.broadcasted_iota(jnp.int32, scores.shape, 0) + first
        allowed = (column <= row) & (column >= start_rows)
        scores = jnp.where(allowed, scores, masked_score)
        top = jnp.max(scores, axis=1, keepdims=True)
        raised = jnp.exp(scores - top)
        return raised * (1.0 / jnp.sum(raised, axis=1, keepdims=True))

    def attend(scalars, query, kv_own, kv_other, starts):
        tokens, width = query.shape
        rows = tokens // 4

        def kernel(scal, query_ref, own_ref, other_ref, start_ref, context_ref):
            is_value = jnp.bitwise_and(scal[1], 1) == 1
            own, other = own_ref[...], other_ref[...]
            keys = jnp.where(is_value, other, own)
            values = jnp.where(is_value, own, other)
            for at in range(4):
                end = (at + 1) * rows
                spot = pl.ds(at * rows, rows)
                for head in range(width // HD):
                    lanes = slice(head * HD, (head + 1) * HD)
                    probs = probabilities(
                        query_ref[spot, lanes], keys[:end], start_ref[spot, :], at * rows
                    )
                    context_ref[spot, lanes] = mm(probs.astype(bf16), values[:end]).astype(bf16)

        return whole_call(
            kernel, [((tokens, width), bf16)], "attend", scalars, query, kv_own, kv_other, starts
        )[0]

    def out_rows(scalars, context, pieces, model):
        tokens, width = context.shape
        rows = tokens // 4

        def kernel(scal, context_ref, *refs):
            kept_ref, sent_ref, held, part, sems, out_sems = refs[dp_size:]
            wait_all(start_all(attn_jobs(scal[0], refs[:dp_size], pieces, held), sems))
            for at in range(4):
                spot = pl.ds(at * rows, rows)
                part[spot, :] = mm_nt(context_ref[spot, :], held[...]).astype(bf16)
            wait_all(start_all(back(token_jobs(scal[1], kept_ref, sent_ref, part)), out_sems))

        half = jax.ShapeDtypeStruct((tokens // 2, model), bf16)
        return pl.pallas_call(
            kernel,
            in_specs=[SCALARS, WHOLE] + [ANY] * dp_size,
            out_specs=[ANY, ANY],
            out_shape=[half, half],
            scratch_shapes=[
                pltpu.VMEM((model, width), bf16),
                pltpu.VMEM((tokens, model), bf16),
                pltpu.SemaphoreType.DMA((dp_size,)),
                pltpu.SemaphoreType.DMA((4,)),
            ],
            name="out_rows",
        )(scalars, context, *arrays_of(pieces))

    def attend_back(
        scalars, query, kv_own, kv_other, starts, pieces, attn, context, cosine, sine
    ):
        tokens, width = query.shape
        model = attn[0].shape[1]
        rows = tokens // 4
        scale = 1.0 / math.sqrt(HD)

        def kernel(
            scal, query_ref, own_ref, other_ref, start_ref, attn_a, attn_b, attn_c, attn_d,
            context_ref, cos_ref, sin_ref, *refs,
        ):
            grad_query_ref, kv_kept_ref, kv_sent_ref, bias_ref, wout_ref, wout_sent_ref = refs[
                dp_size : dp_size + 6
            ]
            held, grads, grad_context, grad_key, grad_value, sems = refs[dp_size + 6 :]
            wait_all(
                start_all(
                    attn_jobs(scal[0], refs[:dp_size], pieces, held)
                    + quarter_jobs(scal[1], (attn_a, attn_b, attn_c, attn_d), grads),
                    sems,
                )
            )
            is_value = jnp.bitwise_and(scal[1], 1) == 1
            own, other = own_ref[...], other_ref[...]
            keys = jnp.where(is_value, other, own)
            values = jnp.where(is_value, own, other)
            for at in range(2):
                spot = pl.ds(at * 2 * rows, 2 * rows)
                grad_context[spot, :] = mm(grads[spot, :], held[...]).astype(bf16)
            give(mm_tn(grads[...], context_ref[...]).astype(bf16), scal, wout_ref, wout_sent_ref)
            grad_key[...] = jnp.zeros_like(grad_key)
            grad_value[...] = jnp.zeros_like(grad_value)
            bias_ref[...] = jnp.zeros_like(bias_ref)
            for at in range(4):
                end = (at + 1) * rows
                spot = pl.ds(at * rows, rows)
                upto = pl.ds(0, end)
                for head in range(width // HD):
                    lanes = slice(head * HD, (head + 1) * HD)
                    queries = query_ref[spot, lanes]
                    given = grad_context[spot, lanes]
                    probs = probabilities(queries, keys[:end], start_ref[spot, :], at * rows)
                    low = probs.astype(bf16)
                    grad_probs = mm_nt(given, values[:end])
                    delta = jnp.sum(low.astype(f32) * grad_probs, axis=1, keepdims=True)
                    grad_scores = (probs * (grad_probs - delta)).astype(bf16)
                    grad_query = turned(
                        mm(grad_scores, keys[:end]) * scale, cos_ref[spot, :], sin_ref[spot, :], -1.0
                    )
                    grad_query_ref[spot, lanes] = grad_query.astype(bf16)
                    bias_ref[0:1, lanes] += jnp.sum(grad_query, axis=0, keepdims=True)
                    grad_key[upto, :] += mm_tn(grad_scores, queries)
                    grad_value[upto, :] += mm_tn(low, given)
            grad_keys = turned(grad_key[...] * scale, cos_ref[...], sin_ref[...], -1.0)
            grad_values = grad_value[...]
            bias_ref[0:1, width : width + HD] = jnp.sum(grad_keys, axis=0, keepdims=True)
            bias_ref[0:1, width + HD :] = jnp.sum(grad_values, axis=0, keepdims=True)
            kv_kept_ref[...] = jnp.where(is_value, grad_values, grad_keys)
            kv_sent_ref[...] = jnp.where(is_value, grad_keys, grad_values).astype(bf16)

        return pl.pallas_call(
            kernel,
            in_specs=[SCALARS] + [WHOLE] * 4 + [ANY] * 4 + [WHOLE] * 3 + [ANY] * dp_size,
            out_specs=[WHOLE] * 6,
            out_shape=[
                jax.ShapeDtypeStruct((tokens, width), bf16),
                jax.ShapeDtypeStruct((tokens, HD), f32),
                jax.ShapeDtypeStruct((tokens, HD), bf16),
                jax.ShapeDtypeStruct((8, width + 2 * HD), f32),
                jax.ShapeDtypeStruct((model // 2, width), bf16),
                jax.ShapeDtypeStruct((model // 2, width), bf16),
            ],
            scratch_shapes=[
                pltpu.VMEM((model, width), bf16),
                pltpu.VMEM((tokens, model), bf16),
                pltpu.VMEM((tokens, width), bf16),
                pltpu.VMEM((tokens, HD), f32),
                pltpu.VMEM((tokens, HD), f32),
                pltpu.SemaphoreType.DMA((dp_size + 4,)),
            ],
            name="attend_back",
        )(
            scalars, query, kv_own, kv_other, starts, *attn, context, cosine, sine,
            *arrays_of(pieces),
        )

    def project_back(scalars, grad_query, kv_kept, kv_arrived, pieces, pair, core):
        tokens, width = grad_query.shape
        model, columns = pair.shape[1], pieces[0][0].shape[1]
        rows = tokens // 4

        def kernel(
            scal, query_ref, kept_kv_ref, arrived_ref, pair_ref, core_ref, *refs
        ):
            (
                grads_ref, kept_ref, sent_ref, gain_ref, held, part, acts, sems, out_sems,
            ) = refs[dp_size:]
            copies = start_all(
                attn_jobs(scal[0], refs[:dp_size], pieces, held)
                + token_jobs(scal[1], pair_ref, core_ref, acts),
                sems,
            )
            grads_ref[:, :width] = query_ref[...]
            grads_ref[:, width:] = (kept_kv_ref[...] + arrived_ref[...].astype(f32)).astype(bf16)
            wait_all(copies)
            for at in range(4):
                spot = pl.ds(at * rows, rows)
                part[spot, :] = mm_nt(grads_ref[spot, :], held[...]).astype(bf16)
            copies = start_all(back(token_jobs(scal[1], kept_ref, sent_ref, part)), out_sems)
            gain_ref[...] = jnp.zeros_like(gain_ref)
            for at in range(8):
                spot = pl.ds(at * rows // 2, rows // 2)
                gain_ref[0:1, :] += jnp.sum(
                    part[spot, :].astype(f32) * acts[spot, :].astype(f32), axis=0, keepdims=True
                )
            wait_all(copies)

        half = jax.ShapeDtypeStruct((tokens // 2, model), bf16)
        return pl.pallas_call(
            kernel,
            in_specs=[SCALARS, WHOLE, WHOLE, WHOLE, ANY, ANY] + [ANY] * dp_size,
            out_specs=[WHOLE, ANY, ANY, WHOLE],
            out_shape=[
                jax.ShapeDtypeStruct((tokens, columns), bf16),
                half,
                half,
                jax.ShapeDtypeStruct((8, model), f32),
            ],
            scratch_shapes=[
                pltpu.VMEM((model, columns), bf16),
                pltpu.VMEM((tokens, model), bf16),
                pltpu.VMEM((tokens, model), bf16),
                pltpu.SemaphoreType.DMA((dp_size + 4,)),
                pltpu.SemaphoreType.DMA((4,)),
            ],
            name="project_back",
        )(scalars, grad_query, kv_kept, kv_arrived, pair, core, *arrays_of(pieces))

    def project_grad(scalars, pair, core, grads):
        tokens, columns = grads.shape
        model = pair.shape[1]

        def kernel(scal, pair_ref, core_ref, grads_ref, kept_ref, sent_ref, acts, sems):
            wait_all(start_all(token_jobs(scal[1], pair_ref, core_ref, acts), sems))
            give(mm_tn(acts[...], grads_ref[...]).astype(bf16), scal, kept_ref, sent_ref)

        return pl.pallas_call(
            kernel,
            in_specs=[SCALARS, ANY, ANY, WHOLE],
            out_specs=[WHOLE] * 2,
            out_shape=[jax.ShapeDtypeStruct((model // 2, columns), bf16)] * 2,
            scratch_shapes=[
                pltpu.VMEM((tokens, model), bf16),
                pltpu.SemaphoreType.DMA((4,)),
            ],
            name="project_grad",
        )(scalars, pair, core, grads)

    def norm_two_back(scalars, own, from_x, from_l, hidden, gain, given):
        rows, model = own.shape

        def kernel(scal, own_ref, x_ref, l_ref, hidden_ref, gain_ref, given_ref, out_ref, low_ref, sum_ref):
            grad_out = own_ref[...] + x_ref[...].astype(f32) + l_ref[...].astype(f32)
            normed, row_scale = norm_forward(hidden_ref[...])
            grad_normed = grad_out * gain_ref[...]
            grad_in = row_scale * (
                grad_normed - normed * jnp.mean(grad_normed * normed, axis=-1, keepdims=True)
            )
            total = given_ref[...].astype(f32) + grad_in
            out_ref[...] = total
            low_ref[...] = total.astype(bf16)
            sum_ref[0:1, :] = jnp.sum(grad_out * normed, axis=0, keepdims=True)

        outs = [((rows, model), f32), ((rows, model), bf16), ((8, model), f32)]
        return whole_call(
            kernel, outs, "norm_two_back", scalars, own, from_x, from_l, hidden, gain, given
        )

    def local(
        block_input,
        segment_ids,
        gain_attn,
        w_query,
        b_query,
        w_keyval,
        b_keyval,
        w_out,
        gain_ffn,
        w_gate,
        w_up,
        w_down,
        cotangent,
    ):
        dp_index = lax.axis_index("dp")
        tensor_index = lax.axis_index("tensor")
        scalars = jnp.stack([dp_index, tensor_index]).astype(jnp.int32)
        local_heads = b_query.shape[0] // HD
        head_kv = tensor_index * local_heads // (HQ // KV)
        is_value = tensor_index % 2
        kv_column = is_value * (KV * HD) + head_kv * HD
        width = local_heads * HD

        groups = dp_size // 4

        def far_rest(kept, sent):
            arrived = swap(sent, "dp", far_bits[0])
            for bit in far_bits[1:]:
                kept, sent = fold_sum(scalars, kept, arrived, bit, 1)
                arrived = swap(sent, "dp", bit)
            return kept, arrived

        keyval_cols = lax.dynamic_slice_in_dim(w_keyval, kv_column, HD, 1)
        qkv_own = jnp.concatenate([w_query, keyval_cols], axis=1)
        shard = qkv_own.shape[0]
        qkv_far = far_pieces(qkv_own)
        qkv_l = swap(qkv_own, "dp", pair_bit)
        qkv_y = swap(qkv_own, "dp", 1)
        rows_float = block_input.astype(f32)
        normed_one, scale_one = norm_forward(rows_float)
        act_own = (normed_one * gain_attn).astype(bf16)
        act_x = swap(act_own, "tensor", 2)
        gate_mine, gate_sent = split_cols(scalars, w_gate)
        gate_theirs = swap(gate_sent, "dp", pair_bit)

        qkv_far_in, qkv_l, qkv_y, out_own, w_up_in, w_down_in, segments = hold(
            [gate_sent, act_own],
            [tuple(qkv_far[1:]), qkv_l, qkv_y, w_out.T, w_up, w_down, segment_ids],
        )
        far_rows = rows_of(*qkv_far_in)
        qkv_y2 = swap(rows_of(qkv_l, far_rows), "dp", 1)
        qkv_l2 = swap(far_rows, "dp", pair_bit)
        out_far = far_pieces(out_own)
        rest_mine, rest_sent = split_cols(scalars, w_up_in, w_down_in.T)
        positions = positions_of(segments[0])
        cosine, sine = rotary(positions)
        sine = jnp.where(jnp.arange(HD)[None, :] < HD // 2, -sine, sine)
        starts = (jnp.arange(positions.shape[0], dtype=jnp.int32) - positions)[:, None]
        qkv_bias = jnp.concatenate([b_query, lax.dynamic_slice_in_dim(b_keyval, kv_column, HD, 0)])[
            None, :
        ]

        qkv_y2, qkv_l2, act_pair, gate_theirs, out_half, cosine, sine, starts, rest_sent, cot_own = (
            hold(
                [],
                [
                    qkv_y2,
                    qkv_l2,
                    rows_of(act_own, act_x),
                    gate_theirs,
                    rows_of(*out_far),
                    cosine,
                    sine,
                    starts,
                    rest_sent,
                    cotangent,
                ],
            )
        )

        def gather_attn():
            return (
                swap(qkv_l2, "dp", 1),
                swap(act_pair, "tensor", 1),
                swap(out_half, "dp", pair_bit),
                join_rows(scalars, gate_mine, gate_theirs, 0, 1),
            )

        qkv_y3, act_c, out_l, gate_piece = section(gather_attn)

        qkv_y3, act_c, out_near, rest_sent, cot_core, gate_piece = hold(
            [], [qkv_y3, act_c, rows_of(out_half, out_l), rest_sent, cotangent, gate_piece]
        )
        gate_far = far_pieces(gate_piece)
        cot_x = swap(cot_core, "tensor", 2)
        rest_theirs = swap(rest_sent, "dp", pair_bit)
        out_y = swap(out_near, "dp", 1)
        far_masks = masks_of(far_bits)
        qkv_pieces = [(part, 0, mask) for part, mask in zip(qkv_far, far_masks)]
        qkv_pieces += [(qkv_l, 0, pair_bit), (qkv_y, 0, 1), (qkv_y2, 0, pair_bit ^ 1)]
        for at, mask in enumerate(far_masks[1:]):
            qkv_pieces += [
                (qkv_y2, (at + 1) * shard, mask ^ 1),
                (qkv_l2, at * shard, mask ^ pair_bit),
                (qkv_y3, at * shard, mask ^ pair_bit ^ 1),
            ]

        def attention():
            query_rot, kv_own = project(
                scalars, act_pair, act_c, qkv_pieces, qkv_bias, cosine, sine
            )
            kv_other = swap(kv_own, "tensor", 1)
            kv_other, cot_given = hold([], [kv_other, cot_core])
            cot_own_c = swap(cot_given, "tensor", 1)
            context = attend(scalars, query_rot, kv_own, kv_other, starts)
            context, cot_own_c = hold([], [context, cot_own_c])
            return query_rot, kv_own, kv_other, context, cot_own_c

        def out_pieces(near, far):
            pieces = []
            masks = masks_of(far_bits + [pair_bit])
            for at, mask in enumerate(masks):
                pieces += [(near, at * shard, mask), (far, at * shard, mask ^ 1)]
            return pieces

        query_rot, kv_own, kv_other, context, cot_own_c = section(attention)
        context, out_y = hold([], [context, out_y])
        out_parts = out_pieces(out_near, out_y)
        attn_kept, attn_sent = out_rows(scalars, context, out_parts, act_pair.shape[1])

        attn_sent, rest_theirs, cot_own_l = hold([cot_x], [attn_sent, rest_theirs, cotangent])

        def sum_cores():
            arrived = swap(attn_sent, "tensor", 1)
            return arrived, join_both(scalars, gate_piece, rest_mine, rest_theirs)

        attn_arrived, (up_piece, own_both) = section(sum_cores)
        attn_arrived, up_piece, own_both = hold([], [attn_arrived, up_piece, own_both])
        up_far = far_pieces(up_piece)
        own_y = swap(own_both, "dp", 1)
        cot_l = swap(cot_own_l, "dp", pair_bit)

        def sum_heads():
            (sent,) = part_sum(scalars, attn_kept, attn_arrived, block_input.shape[0], 1, 1)
            return norm_two(
                scalars, block_input, attn_kept, attn_arrived, swap(sent, "tensor", 2),
                gain_ffn[None, :],
            )

        hidden, two_own = section(sum_heads)

        two_own, gate_halves = hold([cot_l], [two_own, tuple(gate_far[1:])])
        gate_y2 = [swap(part, "dp", 1) for part in gate_halves]

        def gather_near():
            two_x = swap(two_own, "tensor", 2)
            two_l = swap(two_own, "dp", pair_bit)
            return two_x, two_l, join_rows(scalars, rest_mine, rest_theirs, 1, 2)

        two_x, two_l, down_piece = section(gather_near)

        rows = two_own.shape[0]
        two_x, two_l, up_halves = hold([own_y, gate_y2], [two_x, two_l, tuple(up_far[1:])])
        up_y2 = [swap(part, "dp", 1) for part in up_halves]

        def gather_rest():
            given_a, given_b = halves(scalars, two_l, two_x)
            far_a = swap(given_a, "tensor", 2)
            far_b = swap(given_b, "dp", pair_bit)

            def cores():
                given, arrived = [two_x, two_l, two_own], []
                for at in range(3):
                    part = swap(given[at], "tensor", 1)
                    part, *given = hold([], [part] + given)
                    arrived.append(part)
                return arrived

            arrived = section(cores)
            return hold([], [far_a, far_b, *arrived])

        far_a, far_b, two_x_c, two_l_c, two_own_c = section(gather_rest)
        far_a, far_b, down_piece = hold(up_y2, [far_a, far_b, down_piece])
        down_far = far_pieces(down_piece)

        def gather_far():
            return swap(far_a, "tensor", 1), swap(far_b, "tensor", 1)

        far_a_c, far_b_c = section(gather_far)
        two_pieces = [two_own, two_x, two_l]
        two_pieces_c = [two_own_c, two_x_c, two_l_c]

        size = gate_piece.shape[0]
        gate_pieces = [(part, 0) for part in [*gate_far]] + [
            (part, 0) for part in [own_y, *gate_y2]
        ]
        up_pieces = [(part, 0) for part in [*up_far]] + [(own_y, size)] + [
            (part, 0) for part in up_y2
        ]
        far_a, far_b, far_a_c, far_b_c, down_piece_y, cot_x, cot_l = hold(
            [], [far_a, far_b, far_a_c, far_b_c, down_piece, cot_x, cot_l]
        )
        two_pieces += [far_a, far_b]
        two_pieces_c += [far_a_c, far_b_c]

        def feed_own():
            down_y1 = swap(down_piece_y, "dp", 1)
            cot_far = swap(cot_l, "tensor", 2)
            x_c = swap(cot_x, "tensor", 1)
            own = ffn_up(scalars, two_pieces, gate_pieces, up_pieces)
            down_y1, cot_far, x_c = hold([own], [down_y1, cot_far, x_c])
            return down_y1, cot_far, x_c, own

        down_y1, cot_far, cot_x_c, (acts_a, mixed_a, silu_a, back_a) = section(feed_own)

        mixed_a, cot_l_in = hold([], [mixed_a, cot_l])

        def feed_core():
            l_c = swap(cot_l_in, "tensor", 1)
            far_c = swap(cot_far, "tensor", 1)
            core = ffn_up(scalars, two_pieces_c, gate_pieces, up_pieces)
            l_c, far_c = hold([core], [l_c, far_c])
            return l_c, far_c, core

        cot_l_c, cot_far_c, (acts_b, mixed_b, silu_b, back_b) = section(feed_core)

        cots = [cotangent, cot_x, cot_l, cot_far]
        cots_c = [cot_own_c, cot_x_c, cot_l_c, cot_far_c]
        mixed_b, down_halves = hold([down_y1], [mixed_b, tuple(down_far[1:])])
        down_y2 = tuple(swap(part, "dp", 1) for part in down_halves)
        down_kept, down_sent = section(
            lambda: ffn_grad(scalars, cots, cots_c, mixed_a, mixed_b, "grad_down")
        )
        down_sent, down_y2 = hold([], [down_sent, down_y2])
        down_pieces = [(part, 0) for part in [*down_far, down_y1, *down_y2]]

        down_sent, silu_b = hold([], [down_sent, silu_b])
        down_sent = swap(down_sent, "dp", 1)

        def back_all():
            gate_b, up_b, two_sent = ffn_back(
                scalars, cots_c, down_pieces, gate_pieces, up_pieces, silu_b, back_b
            )
            (two_sent,) = hold([], [two_sent])
            arrived = swap(two_sent, "tensor", 1)
            gate_a, up_a, kept = ffn_back(
                scalars, cots, down_pieces, gate_pieces, up_pieces, silu_a, back_a
            )
            (kept,) = hold([], [kept])
            far = part_sum(scalars, kept, arrived, kept.shape[0] // 4, 3, 2)
            return gate_a, up_a, gate_b, up_b, kept, arrived, *far

        gate_a, up_a, gate_b, up_b, two_kept, two_arrived, far_a, far_b = section(back_all)

        far_a, far_b, mixed_b = hold([], [far_a, far_b, mixed_b])
        model = far_a.shape[1]

        def spread_far():
            far_x = swap(far_a, "tensor", 2)
            far_l = swap(far_b, "dp", pair_bit)

            def block_rows():
                sent = ffn_rows(scalars, mixed_b, down_pieces, model, "block_rows")
                (sent,) = hold([], [sent])
                arrived = swap(sent, "tensor", 1)
                kept = ffn_rows(scalars, mixed_a, down_pieces, model, "block_rows")
                return hold([], [kept, arrived])

            outs = section(block_rows)
            outs, far_x, far_l = hold([], [outs, far_x, far_l])
            return (*outs, *spread_rest(scalars, two_kept, two_arrived, far_x, far_l))

        block_kept, block_arrived, own, to_x, to_l = section(spread_far)

        to_x, to_l, down_sent = hold([], [to_x, to_l, down_sent])

        def spread_near():
            from_x = swap(to_x, "tensor", 2)
            from_l = swap(to_l, "dp", pair_bit)
            up_grads = ffn_grad(scalars, [acts_a], [acts_b], up_a, up_b, "grad_up")
            down_pair = fold_sum(scalars, down_kept, down_sent, far_bits[0], 1)
            block_rows = 2 * own.shape[0]
            block_pair = part_sum(scalars, block_kept, block_arrived, block_rows, 1, 1)
            from_x, from_l = hold([up_grads, down_pair, block_pair], [from_x, from_l])
            return (
                *up_grads,
                *down_pair,
                *block_pair,
                *norm_two_back(
                    scalars, own, from_x, from_l, hidden, gain_ffn[None, :], cotangent
                ),
            )

        (
            up_kept, up_sent, down_kept, down_sent, block_sent, grad_hidden, attn_own, gain_two,
        ) = section(spread_near)

        attn_own, down_sent, up_sent, gate_b, block_sent = hold(
            [], [attn_own, down_sent, up_sent, gate_b, block_sent]
        )
        down_kept, down_sent = far_rest(down_kept, down_sent)
        up_sent = swap(up_sent, "dp", 1)
        block_from_l = swap(block_sent, "dp", pair_bit)

        def attention_back():
            def gather_back():
                attn_x = swap(attn_own, "tensor", 2)
                own_c = swap(attn_own, "tensor", 1)
                gate_grads = ffn_grad(scalars, [acts_a], [acts_b], gate_a, gate_b, "grad_gate")
                attn_x, own_c = hold([gate_grads], [attn_x, own_c])
                return (attn_x, own_c, *gate_grads)

            attn_x, own_c, gate_kept, gate_sent = section(gather_back)
            attn_x, own_c, gate_sent = hold([], [attn_x, own_c, gate_sent])
            x_c = swap(attn_x, "tensor", 1)
            outs = attend_back(
                scalars, query_rot, kv_own, kv_other, starts, out_parts,
                [attn_own, attn_x, own_c, x_c], context, cosine, sine,
            )
            return gate_kept, gate_sent, outs

        gate_kept, gate_sent, outs = section(attention_back)
        grad_query_low, kv_kept, kv_given, bias_rows, wout_kept, wout_sent = outs

        kv_given, wout_sent, gate_sent, down_sent, up_sent, block_from_l = hold(
            [], [kv_given, wout_sent, gate_sent, down_sent, up_sent, block_from_l]
        )
        wout_arrived = swap(wout_sent, "dp", pair_bit)
        devices = dp_size * tensor_size

        def input_grads():
            up_own, up_given = fold_sum(scalars, up_kept, up_sent, far_bits[0], 1)
            kv_in, gate_in, up_given = hold([], [kv_given, gate_sent, up_given])
            gate_y = swap(gate_in, "dp", 1)
            up_own, up_far_sum = far_rest(up_own, up_given)

            def project_all():
                kv_arrived = swap(kv_in, "tensor", 1)
                down_pair = fold_sum(scalars, down_kept, down_sent, pair_bit, 1)
                (kv_arrived,) = hold([down_pair], [kv_arrived])
                grad_qkv, one_kept, one_sent, gain_rows = project_back(
                    scalars, grad_query_low, kv_kept, kv_arrived, qkv_pieces, act_pair, act_c
                )
                arrived = swap(one_sent, "tensor", 1)
                wqkv_pair = project_grad(scalars, act_pair, act_c, grad_qkv)
                (arrived,) = hold([wqkv_pair], [arrived])
                wqkv_kept, wqkv_sent = wqkv_pair
                (one_given,) = part_sum(scalars, one_kept, arrived, block_input.shape[0], 1, 1)
                one_arrived = arrived

                def first_norm_back():
                    arrived = swap(one_given, "tensor", 2)
                    wqkv_arrived = swap(wqkv_sent, "dp", pair_bit)
                    block = block_x_sum(scalars, block_kept, block_arrived, block_from_l)
                    bias_keyval = jnp.zeros((2 * KV * HD,), f32)
                    bias_keyval = lax.dynamic_update_slice_in_dim(
                        bias_keyval, bias_rows[0, width : width + HD], head_kv * HD, 0
                    )
                    bias_keyval = lax.dynamic_update_slice_in_dim(
                        bias_keyval, bias_rows[0, width + HD :], KV * HD + head_kv * HD, 0
                    )
                    bias_query = lax.dynamic_update_slice_in_dim(
                        jnp.zeros((HQ * HD,), f32), bias_rows[0, :width], tensor_index * width, 0
                    )
                    parts = (gain_rows[0] / gain_attn, gain_two[0], bias_query, bias_keyval)
                    small = jnp.concatenate([part.reshape(devices, -1) for part in parts], axis=1)
                    (arrived,) = hold([block, small], [arrived])
                    grad_rows = norm_one_back(
                        scalars, block_input, one_kept, one_arrived, arrived, gain_attn[None, :],
                        grad_hidden,
                    )
                    (wqkv_arrived,) = hold([grad_rows], [wqkv_arrived])
                    return grad_rows, small, block, wqkv_arrived

                return (*down_pair, wqkv_kept, *section(first_norm_back))

            outs = section(project_all)
            outs, gate_y, up_far_sum = hold([], [outs, gate_y, up_far_sum])
            return (up_own, up_far_sum, gate_y, *outs)

        (
            up_kept, up_sent, gate_sent, down_mine, down_given, wqkv_kept, grad_rows, small,
            block_to_x, wqkv_arrived,
        ) = section(input_grads)

        wqkv_arrived, wout_arrived, gate_sent, small, down_given = hold(
            [], [wqkv_arrived, wout_arrived, gate_sent, small, down_given]
        )
        gate_kept, gate_sent = fold_sum(scalars, gate_kept, gate_sent, far_bits[0], 1)
        wqkv_arrived, gate_sent, small = hold([], [wqkv_arrived, gate_sent, small])
        gate_kept, gate_sent = far_rest(gate_kept, gate_sent)
        small = lax.all_to_all(small, ("dp", "tensor"), 0, 0, tiled=True)

        def last_rows():
            block_x = swap(block_to_x, "tensor", 2)
            down_theirs = swap(down_given, "dp", pair_bit)

            def attn_step():
                own, sent = fold_both(
                    scalars, wqkv_kept, wqkv_arrived, wout_kept, wout_arrived, 1, groups
                )
                arrived = swap(sent, "dp", 1)
                up_pair = fold_sum(scalars, up_kept, up_sent, pair_bit, 1)
                (arrived,) = hold([up_pair], [arrived])
                return (*fold_sum(scalars, own, arrived, far_bits[0], 1), *up_pair)

            *attn_outs, block_x, down_theirs = hold(
                [], [*section(attn_step), block_x, down_theirs]
            )
            block_out = block_final(
                scalars, block_kept, block_arrived, block_from_l, hidden, block_x
            )
            down_share = join_cols(scalars, down_mine, down_theirs, w_down.shape[0] // 2).T
            return *attn_outs, block_out, down_share

        attn_kept, attn_sent, up_mine, up_given, block_out, down_share = section(last_rows)

        gate_sent, attn_sent, up_given, small = hold(
            [block_out, down_share], [gate_sent, attn_sent, up_given, small]
        )
        attn_kept, attn_sent = far_rest(attn_kept, attn_sent)
        up_theirs = swap(up_given, "dp", pair_bit)
        gate_mine, gate_given = fold_sum(scalars, gate_kept, gate_sent, pair_bit, 1)
        gate_theirs = swap(gate_given, "dp", pair_bit)
        small = jnp.sum(small, axis=0)
        up_theirs = hold([gate_given, small], [up_theirs])[0]
        up_share = join_cols(scalars, up_mine, up_theirs, w_up.shape[1] // 2)
        (attn_sent,) = hold([up_share], [attn_sent])
        share = add(attn_kept, attn_sent)
        kv_rows = share[:, width : width + HD]
        share_rows = kv_rows.shape[0] // tensor_size
        moved = []
        for mask in range(tensor_size):
            rows_for = lax.dynamic_slice_in_dim(
                kv_rows, (tensor_index ^ mask) * share_rows, share_rows, 0
            )
            moved.append(swap(rows_for, "tensor", mask) if mask else rows_for)
        query_share, out_share = share[:, :width], share[:, width + HD :].T
        gate_theirs, *moved = hold([query_share, out_share], [gate_theirs] + moved)
        gate_share = join_cols(scalars, gate_mine, gate_theirs, w_gate.shape[1] // 2)
        keyval_share = jnp.zeros((share_rows, 2 * KV * HD), f32)
        for mask in range(tensor_size):
            sender = tensor_index ^ mask
            column = (sender % 2) * (KV * HD) + (sender * local_heads // (HQ // KV)) * HD
            keyval_share = lax.dynamic_update_slice_in_dim(keyval_share, moved[mask], column, 1)
        sizes = [HQ * HD // devices, 2 * KV * HD // devices, gain_attn.shape[0] // devices]
        ends = [sizes[2], 2 * sizes[2], 2 * sizes[2] + sizes[0]]
        gain_one_share = small[: ends[0]]
        gain_two_share = small[ends[0] : ends[1]]
        query_bias_share = small[ends[1] : ends[2]]
        keyval_bias_share = small[ends[2] :]
        return (
            block_out,
            grad_rows,
            gain_one_share,
            query_share,
            query_bias_share,
            keyval_share,
            keyval_bias_share,
            out_share,
            gain_two_share,
            gate_share,
            up_share,
            down_share,
        )

    placed = (
        P(("dp", "tensor"), None),
        P("dp", None),
        P(),
        P("dp", "tensor"),
        P("tensor"),
        P("dp", None),
        P(),
        P("tensor", "dp"),
        P(),
        P("dp", "tensor"),
        P("dp", "tensor"),
        P("tensor", "dp"),
        P(("dp", "tensor"), None),
    )
    return jax.shard_map(
        local,
        mesh=mesh,
        in_specs=placed,
        out_specs=(
            P(("dp", "tensor"), None),
            P(("dp", "tensor"), None),
            P(("dp", "tensor")),
            P("dp", "tensor"),
            P(("dp", "tensor")),
            P(("dp", "tensor"), None),
            P(("dp", "tensor")),
            P("tensor", "dp"),
            P(("dp", "tensor")),
            P("dp", "tensor"),
            P("dp", "tensor"),
            P("tensor", "dp"),
        ),
        check_vma=False,
    )
```

```python
import math

import jax
import jax.numpy as jnp
from jax import lax
from jax.experimental import pallas as pl
from jax.experimental.pallas import tpu as pltpu
from jax.sharding import PartitionSpec as P

HQ = 12
KV = 2
HD = 128


epsilon = 1e-06
rope_base = 1000000.0
masked_score = -1e30
bf16 = jnp.bfloat16
f32 = jnp.float32


def positions_of(segment_row):
    index_row = jnp.arange(segment_row.shape[0], dtype=jnp.int32)
    starts = jnp.concatenate(
        [jnp.ones((1,), jnp.int32), (segment_row[1:] != segment_row[:-1]).astype(jnp.int32)]
    )
    first_index = lax.cummax(jnp.where(starts > 0, index_row, 0), axis=0)
    return index_row - first_index


def rotary(positions):
    inverse = rope_base ** (-(jnp.arange(HD // 2, dtype=jnp.float32) * 2.0 / HD))
    angles = positions.astype(jnp.float32)[:, None] * inverse[None, :]
    angles = jnp.concatenate([angles, angles], axis=1)
    return (jnp.cos(angles), jnp.sin(angles))


def norm_forward(values_in):
    row_scale = lax.rsqrt(jnp.mean(values_in * values_in, axis=-1, keepdims=True) + epsilon)
    return (values_in * row_scale, row_scale)


def norm_backward(grad_out, normed, row_scale, gain_vec):
    grad_normed = grad_out * gain_vec
    grad_in = row_scale * (
        grad_normed - normed * jnp.mean(grad_normed * normed, axis=-1, keepdims=True)
    )
    return (grad_in, jnp.sum(grad_out * normed, axis=0))


ANY = pl.BlockSpec(memory_space=pl.ANY)
WHOLE = pl.BlockSpec(memory_space=pltpu.VMEM)
SCALARS = pl.BlockSpec(memory_space=pltpu.SMEM)


def made(jobs, sems, first=0):
    return [
        pltpu.make_async_copy(src, dst, sems.at[first + at]) for at, (src, dst) in enumerate(jobs)
    ]


def start_all(jobs, sems):
    copies = made(jobs, sems)
    for copy in copies:
        copy.start()
    return copies


def wait_all(copies):
    for copy in copies:
        copy.wait()


def block(ref, at, rows):
    return ref.at[pl.ds(pl.multiple_of(at * rows, rows), rows)]


def turned(values, cosine, sine, sign):
    return values * cosine + sign * (pltpu.roll(values, HD // 2, 1) * sine)


def mm(left, right):
    return lax.dot_general(left, right, (((1,), (0,)), ((), ())), preferred_element_type=f32)


def mm_nt(left, right):
    return lax.dot_general(left, right, (((1,), (1,)), ((), ())), preferred_element_type=f32)


def mm_tn(left, right):
    return lax.dot_general(left, right, (((0,), (0,)), ((), ())), preferred_element_type=f32)


def hold(due, release):
    out = lax.optimization_barrier((tuple(due), tuple(release)))
    return out[1]


def section(body):
    outs = jax.eval_shape(body)
    return lax.cond(
        lax.optimization_barrier(jnp.bool_(True)),
        body,
        lambda: jax.tree.map(lambda out: jnp.zeros(out.shape, out.dtype), outs),
    )


def solution(mesh):
    dp_size = mesh.shape["dp"]
    tensor_size = mesh.shape["tensor"]
    pair_bit = 2
    far_bits = []
    bit = dp_size // 2
    while bit > pair_bit:
        far_bits.append(bit)
        bit //= 2
    ring_bits = far_bits + [1]

    def swap(array, axis, bit):
        size = mesh.shape[axis]
        with jax.named_scope(f"swap_{axis}_{bit}"):
            return lax.ppermute(array, axis, [(i, i ^ bit) for i in range(size)])

    def masks_of(bits):
        masks = [0]
        for bit in bits:
            masks = masks + [mask ^ bit for mask in masks]
        return masks

    def rows_of(*pieces):
        return jnp.concatenate(pieces, axis=0)

    def far_pieces(piece):
        pieces = [piece]
        for bit in far_bits:
            pieces = pieces + [swap(part, "dp", bit) for part in pieces]
        return pieces

    def fold(total, axis, bit):
        half = total.shape[0] // 2
        return total[:half], swap(total[half:].astype(bf16), axis, bit)

    def add(kept, arrived):
        return kept.astype(f32) + arrived.astype(f32)

    ring_masks = masks_of(ring_bits)
    ring_mask = sum(ring_bits)
    count = len(ring_masks)


    def ffn_jobs(dp_index, refs, offsets, held):
        rows = held.shape[0] // dp_size
        jobs = []
        for mask, ref, offset in zip(ring_masks, refs, offsets):
            base = jnp.bitwise_xor(jnp.bitwise_and(dp_index, ring_mask), mask)
            for low in (0, 1):
                jobs.append(
                    (
                        ref.at[pl.ds(offset + low * rows, rows)],
                        block(held, base + low * pair_bit, rows),
                    )
                )
        return jobs

    def row_jobs(refs, held):
        jobs, start = [], 0
        for ref in refs:
            jobs.append((ref, held.at[pl.ds(start, ref.shape[0])]))
            start += ref.shape[0]
        return jobs

    def attn_jobs(dp_index, refs, pieces, held):
        rows = held.shape[0] // dp_size
        return [
            (
                ref.at[pl.ds(first, rows)],
                block(held, jnp.bitwise_xor(dp_index, mask), rows),
            )
            for ref, (_, first, mask) in zip(refs, pieces)
        ]

    def arrays_of(pieces):
        return [piece[0] for piece in pieces]

    token_masks = ((0, 2), (1, 3))

    def token_jobs(tensor_index, pair, other, held):
        rows = held.shape[0] // 4
        jobs = []
        for masks, ref in zip(token_masks, (pair, other)):
            for at, mask in enumerate(masks):
                spot = jnp.bitwise_xor(tensor_index, mask)
                jobs.append((ref.at[pl.ds(at * rows, rows)], block(held, spot, rows)))
        return jobs

    def quarter_jobs(tensor_index, refs, held):
        rows = held.shape[0] // 4
        return [
            (ref, block(held, jnp.bitwise_xor(tensor_index, mask), rows))
            for ref, mask in zip(refs, (0, 2, 1, 3))
        ]

    def back(jobs):
        return [(dst, src) for src, dst in jobs]

    def ffn_up(scalars, pieces, gate_pieces, up_pieces):
        tokens, model = sum(piece.shape[0] for piece in pieces), pieces[0].shape[1]
        units = gate_pieces[0][0].shape[1]
        rows = tokens // 2
        many = len(pieces)
        early = 2

        def kernel(scal, *refs):
            parts = refs[:many]
            gates = refs[many : many + count]
            ups = refs[many + count : many + 2 * count]
            acts_ref, mixed_ref, silu_ref, back_ref, acts, gate_w, up_w, sems = refs[
                many + 2 * count :
            ]
            jobs = row_jobs(parts, acts)
            gate_jobs = ffn_jobs(scal[0], gates, [at for _, at in gate_pieces], gate_w)
            up_jobs = ffn_jobs(scal[0], ups, [at for _, at in up_pieces], up_w)
            step = pl.program_id(0)

            @pl.when(step == 0)
            def _():
                copies = start_all(jobs[:early] + gate_jobs + jobs[early:] + up_jobs, sems)
                wait_all(copies[: early + 2 * count])

            @pl.when(step == 1)
            def _():
                wait_all(made(jobs[early:], sems, early + 2 * count))

            spot = pl.ds(pl.multiple_of(step * rows, rows), rows)
            rows_in = acts[spot, :]
            acts_ref[...] = rows_in
            gate = mm(rows_in, gate_w[...])

            @pl.when(step == 0)
            def _():
                wait_all(made(up_jobs, sems, many + 2 * count))

            up = mm(rows_in, up_w[...])
            sig = jax.nn.sigmoid(gate)
            silu = gate * sig
            mixed_ref[...] = (silu * up).astype(bf16)
            silu_ref[...] = silu.astype(bf16)
            back_ref[...] = (up * sig * (1.0 + gate * (1.0 - sig))).astype(bf16)

        out = jax.ShapeDtypeStruct((tokens, units), bf16)
        spec = pl.BlockSpec((rows, units), lambda i: (i, 0))
        return pl.pallas_call(
            kernel,
            grid=(2,),
            in_specs=[SCALARS] + [ANY] * (many + 2 * count),
            out_specs=[pl.BlockSpec((rows, model), lambda i: (i, 0))] + [spec] * 3,
            out_shape=[jax.ShapeDtypeStruct((tokens, model), bf16)] + [out] * 3,
            scratch_shapes=[
                pltpu.VMEM((tokens, model), bf16),
                pltpu.VMEM((model, units), bf16),
                pltpu.VMEM((model, units), bf16),
                pltpu.SemaphoreType.DMA((many + 4 * count,)),
            ],
            name="ffn_up",
        )(
            scalars,
            *pieces,
            *[ref for ref, _ in gate_pieces],
            *[ref for ref, _ in up_pieces],
        )

    def ffn_back(scalars, cots, down_pieces, gate_pieces, up_pieces, silu, back_part):
        many = len(cots)
        tokens, model = sum(piece.shape[0] for piece in cots), cots[0].shape[1]
        units = silu.shape[1]
        rows = tokens // 2
        lists = (down_pieces, gate_pieces, up_pieces)

        def kernel(scal, *refs):
            parts = refs[:many]
            pieces = [refs[many + at * count : many + (at + 1) * count] for at in range(3)]
            silu_ref, back_ref, grad_gate_ref, grad_up_ref, out_ref = refs[
                many + 3 * count : many + 3 * count + 5
            ]
            cot, *held = refs[many + 3 * count + 5 : -1]
            sems = refs[-1]
            jobs = row_jobs(parts, cot)
            for at in range(3):
                jobs += ffn_jobs(scal[0], pieces[at], [spot for _, spot in lists[at]], held[at])
            first = pl.program_id(0) == 0
            early = many + 2 * count

            @pl.when(first)
            def _():
                wait_all(start_all(jobs, sems)[:early])

            spot = pl.ds(pl.multiple_of(pl.program_id(0) * rows, rows), rows)
            grad_mixed = mm(cot[spot, :], held[0][...])
            grad_gate = (grad_mixed * back_ref[...].astype(f32)).astype(bf16)
            grad_up = (grad_mixed * silu_ref[...].astype(f32)).astype(bf16)
            grad_gate_ref[...] = grad_gate
            grad_up_ref[...] = grad_up

            @pl.when(first)
            def _():
                wait_all(made(jobs[early:], sems, early))

            out_ref[...] = (
                mm_nt(grad_gate, held[1][...]) + mm_nt(grad_up, held[2][...])
            ).astype(bf16)

        out = jax.ShapeDtypeStruct((tokens, units), bf16)
        spec = pl.BlockSpec((rows, units), lambda i: (i, 0))
        wide = pl.BlockSpec((rows, model), lambda i: (i, 0))
        return pl.pallas_call(
            kernel,
            grid=(2,),
            in_specs=[SCALARS] + [ANY] * (many + 3 * count) + [spec, spec],
            out_specs=[spec, spec, wide],
            out_shape=[out, out, jax.ShapeDtypeStruct((tokens, model), bf16)],
            scratch_shapes=[pltpu.VMEM((tokens, model), bf16)]
            + [pltpu.VMEM((model, units), bf16)] * 3
            + [pltpu.SemaphoreType.DMA((many + 6 * count,))],
            name="ffn_back",
        )(scalars, *cots, *[ref for pieces in lists for ref, _ in pieces], silu, back_part)

    def ffn_rows(scalars, left, pieces, model, name):
        tokens, units = left.shape
        rows = tokens // 2

        def kernel(scal, left_ref, *refs):
            parts = refs[:count]
            out_ref, held, sems = refs[count:]

            @pl.when(pl.program_id(0) == 0)
            def _():
                wait_all(
                    start_all(ffn_jobs(scal[0], parts, [at for _, at in pieces], held), sems)
                )

            out_ref[...] = mm_nt(left_ref[...], held[...]).astype(bf16)

        return pl.pallas_call(
            kernel,
            grid=(2,),
            in_specs=[SCALARS, pl.BlockSpec((rows, units), lambda i: (i, 0))] + [ANY] * count,
            out_specs=pl.BlockSpec((rows, model), lambda i: (i, 0)),
            out_shape=jax.ShapeDtypeStruct((tokens, model), bf16),
            scratch_shapes=[
                pltpu.VMEM((model, units), bf16),
                pltpu.SemaphoreType.DMA((2 * count,)),
            ],
            name=name,
        )(scalars, left, *[ref for ref, _ in pieces])

    def ffn_grad(scalars, own_pieces, core_pieces, low, high, name):
        pieces = [*own_pieces, *core_pieces]
        many = len(own_pieces)
        tokens, model = low.shape[0], pieces[0].shape[1]
        units = low.shape[1]
        shard = model // dp_size
        wide = 384
        groups = wide // (2 * shard)

        def kernel(scal, *refs):
            def stack(parts):
                values = [part[...] for part in parts]
                return values[0] if len(values) == 1 else jnp.concatenate(values, axis=0)

            low_ref, high_ref, kept_ref, sent_ref = refs[2 * many :]
            total = mm_tn(stack(refs[:many]), low_ref[...])
            total = total + mm_tn(stack(refs[many : 2 * many]), high_ref[...])
            total = total.astype(bf16)
            odd = jnp.bitwise_and(scal[0], 1) == 1
            for group in range(groups):
                first = total[group * 2 * shard : group * 2 * shard + shard]
                second = total[group * 2 * shard + shard : (group + 1) * 2 * shard]
                spot = pl.ds(group * shard, shard)
                kept_ref[spot, :] = jnp.where(odd, second, first)
                sent_ref[spot, :] = jnp.where(odd, first, second)

        out = jax.ShapeDtypeStruct((model // 2, units), bf16)
        spec = pl.BlockSpec((wide // 2, units), lambda i: (i, 0))
        whole = pl.BlockSpec((tokens, units), lambda i: (0, 0))
        return pl.pallas_call(
            kernel,
            grid=(model // wide,),
            in_specs=[SCALARS]
            + [pl.BlockSpec((piece.shape[0], wide), lambda i: (0, i)) for piece in pieces]
            + [whole, whole],
            out_specs=[spec] * 2,
            out_shape=[out] * 2,
            name=name,
        )(scalars, *pieces, low, high)

    def is_high(scal, bit):
        return jnp.bitwise_and(scal[0], bit) != 0

    def whole_call(kernel, outs, name, *args):
        return pl.pallas_call(
            kernel,
            in_specs=[SCALARS] + [WHOLE] * (len(args) - 1),
            out_specs=[WHOLE] * len(outs),
            out_shape=[jax.ShapeDtypeStruct(shape, kind) for shape, kind in outs],
            name=name,
        )(*args)

    def split_cols(scalars, *arrays):
        rows, half = arrays[0].shape[0], arrays[0].shape[1] // 2
        wide = -(-half // 128) * 128
        many = len(arrays)

        def kernel(scal, *refs):
            mine_ref, sent_ref = refs[many:]
            flag = is_high(scal, pair_bit)
            mine_ref[...] = jnp.zeros_like(mine_ref)
            sent_ref[...] = jnp.zeros_like(sent_ref)
            for at in range(many):
                low, high = refs[at][:, :half], refs[at][:, half:]
                mine_ref[at * rows : (at + 1) * rows, :half] = jnp.where(flag, high, low)
                sent_ref[at * rows : (at + 1) * rows, :half] = jnp.where(flag, low, high)

        return whole_call(
            kernel, [((many * rows, wide), bf16)] * 2, "split_cols", scalars, *arrays
        )

    def join_rows(scalars, mine, theirs, at, many):
        rows, columns = mine.shape[0] // many, mine.shape[1]
        spot = pl.ds(at * rows, rows)

        def kernel(scal, mine_ref, theirs_ref, out_ref):
            flag = is_high(scal, pair_bit)
            out_ref[:rows, :] = jnp.where(flag, theirs_ref[spot, :], mine_ref[spot, :])
            out_ref[rows:, :] = jnp.where(flag, mine_ref[spot, :], theirs_ref[spot, :])

        return whole_call(
            kernel, [((2 * rows, columns), bf16)], "join_rows", scalars, mine, theirs
        )[0]

    def join_cols(scalars, mine, theirs, columns):
        rows = mine.shape[0]

        def kernel(scal, mine_ref, theirs_ref, out_ref):
            flag = is_high(scal, pair_bit)
            mine = mine_ref[:, :columns].astype(f32)
            theirs = theirs_ref[:, :columns].astype(f32)
            out_ref[:, :columns] = jnp.where(flag, theirs, mine)
            out_ref[:, columns:] = jnp.where(flag, mine, theirs)

        return whole_call(
            kernel, [((rows, 2 * columns), f32)], "join_cols", scalars, mine, theirs
        )[0]

    def fold_sum(scalars, kept, arrived, bit, outer):
        rows, columns = kept.shape[0] // 2, kept.shape[1]
        part = rows // outer

        def kernel(scal, kept_ref, arrived_ref, own_ref, sent_ref):
            flag = is_high(scal, bit)
            for at in range(outer):
                first = pl.ds(2 * at * part, part)
                second = pl.ds((2 * at + 1) * part, part)
                low = kept_ref[first, :].astype(f32) + arrived_ref[first, :].astype(f32)
                high = kept_ref[second, :].astype(f32) + arrived_ref[second, :].astype(f32)
                spot = pl.ds(at * part, part)
                own_ref[spot, :] = jnp.where(flag, high, low).astype(bf16)
                sent_ref[spot, :] = jnp.where(flag, low, high).astype(bf16)

        return whole_call(
            kernel, [((rows, columns), bf16)] * 2, "fold_sum", scalars, kept, arrived
        )

    def norm_two(scalars, rows_in, kept, sums, arrived, gain):
        rows, columns = rows_in.shape

        def kernel(scal, kept_ref, sums_ref, in_ref, arrived_ref, gain_ref, hidden_ref, out_ref):
            hidden = in_ref[...].astype(f32) + kept_ref[...].astype(f32)
            hidden = hidden + sums_ref[...].astype(f32) + arrived_ref[...].astype(f32)
            hidden_ref[...] = hidden
            out_ref[...] = (norm_forward(hidden)[0] * gain_ref[...]).astype(bf16)

        return part_call(
            kernel, [((rows, columns), f32), ((rows, columns), bf16)], "norm_two", scalars,
            [(kept, rows, 0), (sums, rows, 0)], [rows_in, arrived, gain],
        )

    def norm_one_back(scalars, rows_in, kept, sums, arrived, gain, given):
        rows, columns = rows_in.shape

        def kernel(scal, kept_ref, sums_ref, in_ref, arrived_ref, gain_ref, given_ref, out_ref):
            grad_out = kept_ref[...].astype(f32) + sums_ref[...].astype(f32)
            grad_out = grad_out + arrived_ref[...].astype(f32)
            normed, row_scale = norm_forward(in_ref[...].astype(f32))
            grad_normed = grad_out * gain_ref[...]
            grad_in = row_scale * (
                grad_normed - normed * jnp.mean(grad_normed * normed, axis=-1, keepdims=True)
            )
            out_ref[...] = (given_ref[...] + grad_in).astype(bf16)

        return part_call(
            kernel, [((rows, columns), bf16)], "norm_one_back", scalars,
            [(kept, rows, 0), (sums, rows, 0)], [rows_in, arrived, gain, given],
        )[0]

    def join_both(scalars, first, mine, theirs):
        rows, columns = mine.shape[0] // 2, mine.shape[1]

        def kernel(scal, first_ref, mine_ref, theirs_ref, out_ref, both_ref):
            flag = is_high(scal, pair_bit)
            low = jnp.where(flag, theirs_ref[:rows, :], mine_ref[:rows, :])
            high = jnp.where(flag, mine_ref[:rows, :], theirs_ref[:rows, :])
            out_ref[:rows, :] = low
            out_ref[rows:, :] = high
            both_ref[: 2 * rows, :] = first_ref[...]
            both_ref[2 * rows : 3 * rows, :] = low
            both_ref[3 * rows :, :] = high

        return whole_call(
            kernel,
            [((2 * rows, columns), bf16), ((4 * rows, columns), bf16)],
            "join_both", scalars, first, mine, theirs,
        )

    def halves(scalars, first, second):
        rows, columns = first.shape[0] // 2, first.shape[1]

        def kernel(scal, first_ref, second_ref, out_a_ref, out_b_ref):
            out_a_ref[...] = first_ref[:rows, :]
            out_b_ref[...] = second_ref[rows:, :]

        return whole_call(
            kernel, [((rows, columns), bf16)] * 2, "halves", scalars, first, second
        )

    def fold_both(scalars, first, first_arrived, second, second_arrived, bit, outer):
        rows = first.shape[0] // 2
        columns = (first.shape[1], second.shape[1])
        part = rows // outer

        def kernel(scal, first_ref, first_in_ref, second_ref, second_in_ref, own_ref, sent_ref):
            flag = is_high(scal, bit)
            for lanes, kept_ref, arrived_ref in (
                (slice(0, columns[0]), first_ref, first_in_ref),
                (slice(columns[0], columns[0] + columns[1]), second_ref, second_in_ref),
            ):
                for at in range(outer):
                    low_spot = pl.ds(2 * at * part, part)
                    high_spot = pl.ds((2 * at + 1) * part, part)
                    low = kept_ref[low_spot, :].astype(f32) + arrived_ref[low_spot, :].astype(f32)
                    high = kept_ref[high_spot, :].astype(f32) + arrived_ref[high_spot, :].astype(f32)
                    spot = pl.ds(at * part, part)
                    own_ref[spot, lanes] = jnp.where(flag, high, low)
                    sent_ref[spot, lanes] = jnp.where(flag, low, high).astype(bf16)

        outs = [((rows, sum(columns)), f32), ((rows, sum(columns)), bf16)]
        return whole_call(
            kernel, outs, "fold_both", scalars, first, first_arrived, second, second_arrived
        )

    def rows_block(rows, columns, at):
        return pl.BlockSpec((rows, columns), lambda i: (at, 0))

    def part_call(kernel, outs, name, scalars, parts, rest):
        return pl.pallas_call(
            kernel,
            grid=(1,),
            in_specs=[SCALARS]
            + [rows_block(rows, array.shape[1], at) for array, rows, at in parts]
            + [WHOLE] * len(rest),
            out_specs=[WHOLE] * len(outs),
            out_shape=[jax.ShapeDtypeStruct(shape, kind) for shape, kind in outs],
            name=name,
        )(scalars, *[array for array, _, _ in parts], *rest)

    def part_sum(scalars, kept, arrived, rows, at, pieces):
        columns, size = kept.shape[1], rows // pieces

        def kernel(scal, kept_ref, arrived_ref, *out_refs):
            for piece, ref in enumerate(out_refs):
                spot = pl.ds(piece * size, size)
                ref[...] = (
                    kept_ref[spot, :].astype(f32) + arrived_ref[spot, :].astype(f32)
                ).astype(bf16)

        return part_call(
            kernel, [((size, columns), bf16)] * pieces, "part_sum", scalars,
            [(kept, rows, at), (arrived, rows, at)], [],
        )

    def spread_rest(scalars, kept, arrived, far_x, far_l):
        rows, columns = kept.shape[0] // 4, kept.shape[1]
        half = rows // 2

        def kernel(scal, *refs):
            keeps, arrives = refs[:3], refs[3:6]
            far_x_ref, far_l_ref, own_ref, x_ref, l_ref = refs[6:]
            own_ref[...] = keeps[0][...].astype(f32) + arrives[0][...].astype(f32)
            to_x = keeps[1][...].astype(f32) + arrives[1][...].astype(f32)
            x_ref[:half, :] = to_x[:half].astype(bf16)
            x_ref[half:, :] = (to_x[half:] + far_l_ref[...].astype(f32)).astype(bf16)
            to_l = keeps[2][...].astype(f32) + arrives[2][...].astype(f32)
            l_ref[:half, :] = (to_l[:half] + far_x_ref[...].astype(f32)).astype(bf16)
            l_ref[half:, :] = to_l[half:].astype(bf16)

        outs = [((rows, columns), f32), ((rows, columns), bf16), ((rows, columns), bf16)]
        return part_call(
            kernel, outs, "spread_rest", scalars,
            [(array, rows, at) for array in (kept, arrived) for at in range(3)], [far_x, far_l],
        )

    def block_x_sum(scalars, kept, arrived, from_l):
        rows, columns = kept.shape[0] // 4, kept.shape[1]

        def kernel(scal, kept_ref, arrived_ref, from_ref, out_ref):
            out_ref[...] = (
                kept_ref[...].astype(f32)
                + arrived_ref[...].astype(f32)
                + from_ref[...].astype(f32)
            ).astype(bf16)

        return part_call(
            kernel, [((rows, columns), bf16)], "block_x_sum", scalars,
            [(kept, rows, 1), (arrived, rows, 1), (from_l, rows, 1)], [],
        )[0]

    def block_final(scalars, kept, arrived, from_l, hidden, from_x):
        rows, columns = hidden.shape

        def kernel(scal, kept_ref, arrived_ref, from_ref, hidden_ref, x_ref, out_ref):
            total = hidden_ref[...] + kept_ref[...].astype(f32) + arrived_ref[...].astype(f32)
            out_ref[...] = (total + from_ref[...].astype(f32) + x_ref[...].astype(f32)).astype(bf16)

        return part_call(
            kernel, [((rows, columns), bf16)], "block_final", scalars,
            [(kept, rows, 0), (arrived, rows, 0), (from_l, rows, 0)], [hidden, from_x],
        )[0]

    def give(total, scal, kept_ref, sent_ref):
        part = pair_bit * (total.shape[0] // dp_size)
        flag = is_high(scal, pair_bit)
        for at in range(total.shape[0] // (2 * part)):
            low = total[2 * at * part : (2 * at + 1) * part]
            high = total[(2 * at + 1) * part : (2 * at + 2) * part]
            kept_ref[pl.ds(at * part, part), :] = jnp.where(flag, high, low)
            sent_ref[pl.ds(at * part, part), :] = jnp.where(flag, low, high)

    def project(scalars, pair, core, pieces, bias, cosine, sine):
        tokens, model = 2 * pair.shape[0], pair.shape[1]
        columns = pieces[0][0].shape[1]
        width = columns - HD

        def kernel(scal, pair_ref, core_ref, bias_ref, cos_ref, sin_ref, *refs):
            query_ref, kv_ref, acts, held, sems = refs[dp_size:]
            wait_all(
                start_all(
                    attn_jobs(scal[0], refs[:dp_size], pieces, held)
                    + token_jobs(scal[1], pair_ref, core_ref, acts),
                    sems,
                )
            )
            is_value = jnp.bitwise_and(scal[1], 1) == 1
            rows = tokens // 4
            for at in range(4):
                spot = pl.ds(at * rows, rows)
                out = mm(acts[spot, :], held[...]) + bias_ref[...]
                cosine_rows, sine_rows = cos_ref[spot, :], sin_ref[spot, :]
                for head in range(width // HD):
                    query_ref[spot, head * HD : (head + 1) * HD] = turned(
                        out[:, head * HD : (head + 1) * HD], cosine_rows, sine_rows, 1.0
                    ).astype(bf16)
                kv = out[:, width:]
                kv_ref[spot, :] = jnp.where(
                    is_value, kv, turned(kv, cosine_rows, sine_rows, 1.0)
                ).astype(bf16)

        return pl.pallas_call(
            kernel,
            in_specs=[SCALARS, ANY, ANY, WHOLE, WHOLE, WHOLE] + [ANY] * dp_size,
            out_specs=[WHOLE, WHOLE],
            out_shape=[
                jax.ShapeDtypeStruct((tokens, width), bf16),
                jax.ShapeDtypeStruct((tokens, HD), bf16),
            ],
            scratch_shapes=[
                pltpu.VMEM((tokens, model), bf16),
                pltpu.VMEM((model, columns), bf16),
                pltpu.SemaphoreType.DMA((dp_size + 4,)),
            ],
            name="project",
        )(scalars, pair, core, bias, cosine, sine, *arrays_of(pieces))

    def probabilities(query, keys, start_rows, first):
        scores = mm_nt(query, keys) * (1.0 / math.sqrt(HD))
        column = lax.broadcasted_iota(jnp.int32, scores.shape, 1)
        row = lax.broadcasted_iota(jnp.int32, scores.shape, 0) + first
        allowed = (column <= row) & (column >= start_rows)
        scores = jnp.where(allowed, scores, masked_score)
        top = jnp.max(scores, axis=1, keepdims=True)
        raised = jnp.exp(scores - top)
        return raised * (1.0 / jnp.sum(raised, axis=1, keepdims=True))

    def attend(scalars, query, kv_own, kv_other, starts):
        tokens, width = query.shape
        rows = tokens // 4

        def kernel(scal, query_ref, own_ref, other_ref, start_ref, context_ref):
            is_value = jnp.bitwise_and(scal[1], 1) == 1
            own, other = own_ref[...], other_ref[...]
            keys = jnp.where(is_value, other, own)
            values = jnp.where(is_value, own, other)
            for at in range(4):
                end = (at + 1) * rows
                spot = pl.ds(at * rows, rows)
                for head in range(width // HD):
                    lanes = slice(head * HD, (head + 1) * HD)
                    probs = probabilities(
                        query_ref[spot, lanes], keys[:end], start_ref[spot, :], at * rows
                    )
                    context_ref[spot, lanes] = mm(probs.astype(bf16), values[:end]).astype(bf16)

        return whole_call(
            kernel, [((tokens, width), bf16)], "attend", scalars, query, kv_own, kv_other, starts
        )[0]

    def out_rows(scalars, context, pieces, model):
        tokens, width = context.shape
        rows = tokens // 4

        def kernel(scal, context_ref, *refs):
            kept_ref, sent_ref, held, part, sems, out_sems = refs[dp_size:]
            wait_all(start_all(attn_jobs(scal[0], refs[:dp_size], pieces, held), sems))
            for at in range(4):
                spot = pl.ds(at * rows, rows)
                part[spot, :] = mm_nt(context_ref[spot, :], held[...]).astype(bf16)
            wait_all(start_all(back(token_jobs(scal[1], kept_ref, sent_ref, part)), out_sems))

        half = jax.ShapeDtypeStruct((tokens // 2, model), bf16)
        return pl.pallas_call(
            kernel,
            in_specs=[SCALARS, WHOLE] + [ANY] * dp_size,
            out_specs=[ANY, ANY],
            out_shape=[half, half],
            scratch_shapes=[
                pltpu.VMEM((model, width), bf16),
                pltpu.VMEM((tokens, model), bf16),
                pltpu.SemaphoreType.DMA((dp_size,)),
                pltpu.SemaphoreType.DMA((4,)),
            ],
            name="out_rows",
        )(scalars, context, *arrays_of(pieces))

    def attend_back(
        scalars, query, kv_own, kv_other, starts, pieces, attn, context, cosine, sine
    ):
        tokens, width = query.shape
        model = attn[0].shape[1]
        rows = tokens // 4
        scale = 1.0 / math.sqrt(HD)

        def kernel(
            scal, query_ref, own_ref, other_ref, start_ref, attn_a, attn_b, attn_c, attn_d,
            context_ref, cos_ref, sin_ref, *refs,
        ):
            grad_query_ref, kv_kept_ref, kv_sent_ref, bias_ref, wout_ref, wout_sent_ref = refs[
                dp_size : dp_size + 6
            ]
            held, grads, grad_context, grad_key, grad_value, sems = refs[dp_size + 6 :]
            wait_all(
                start_all(
                    attn_jobs(scal[0], refs[:dp_size], pieces, held)
                    + quarter_jobs(scal[1], (attn_a, attn_b, attn_c, attn_d), grads),
                    sems,
                )
            )
            is_value = jnp.bitwise_and(scal[1], 1) == 1
            own, other = own_ref[...], other_ref[...]
            keys = jnp.where(is_value, other, own)
            values = jnp.where(is_value, own, other)
            for at in range(2):
                spot = pl.ds(at * 2 * rows, 2 * rows)
                grad_context[spot, :] = mm(grads[spot, :], held[...]).astype(bf16)
            give(mm_tn(grads[...], context_ref[...]).astype(bf16), scal, wout_ref, wout_sent_ref)
            grad_key[...] = jnp.zeros_like(grad_key)
            grad_value[...] = jnp.zeros_like(grad_value)
            bias_ref[...] = jnp.zeros_like(bias_ref)
            for at in range(4):
                end = (at + 1) * rows
                spot = pl.ds(at * rows, rows)
                upto = pl.ds(0, end)
                for head in range(width // HD):
                    lanes = slice(head * HD, (head + 1) * HD)
                    queries = query_ref[spot, lanes]
                    given = grad_context[spot, lanes]
                    probs = probabilities(queries, keys[:end], start_ref[spot, :], at * rows)
                    low = probs.astype(bf16)
                    grad_probs = mm_nt(given, values[:end])
                    delta = jnp.sum(low.astype(f32) * grad_probs, axis=1, keepdims=True)
                    grad_scores = (probs * (grad_probs - delta)).astype(bf16)
                    grad_query = turned(
                        mm(grad_scores, keys[:end]) * scale, cos_ref[spot, :], sin_ref[spot, :], -1.0
                    )
                    grad_query_ref[spot, lanes] = grad_query.astype(bf16)
                    bias_ref[0:1, lanes] += jnp.sum(grad_query, axis=0, keepdims=True)
                    grad_key[upto, :] += mm_tn(grad_scores, queries)
                    grad_value[upto, :] += mm_tn(low, given)
            grad_keys = turned(grad_key[...] * scale, cos_ref[...], sin_ref[...], -1.0)
            grad_values = grad_value[...]
            bias_ref[0:1, width : width + HD] = jnp.sum(grad_keys, axis=0, keepdims=True)
            bias_ref[0:1, width + HD :] = jnp.sum(grad_values, axis=0, keepdims=True)
            kv_kept_ref[...] = jnp.where(is_value, grad_values, grad_keys)
            kv_sent_ref[...] = jnp.where(is_value, grad_keys, grad_values).astype(bf16)

        return pl.pallas_call(
            kernel,
            in_specs=[SCALARS] + [WHOLE] * 4 + [ANY] * 4 + [WHOLE] * 3 + [ANY] * dp_size,
            out_specs=[WHOLE] * 6,
            out_shape=[
                jax.ShapeDtypeStruct((tokens, width), bf16),
                jax.ShapeDtypeStruct((tokens, HD), f32),
                jax.ShapeDtypeStruct((tokens, HD), bf16),
                jax.ShapeDtypeStruct((8, width + 2 * HD), f32),
                jax.ShapeDtypeStruct((model // 2, width), bf16),
                jax.ShapeDtypeStruct((model // 2, width), bf16),
            ],
            scratch_shapes=[
                pltpu.VMEM((model, width), bf16),
                pltpu.VMEM((tokens, model), bf16),
                pltpu.VMEM((tokens, width), bf16),
                pltpu.VMEM((tokens, HD), f32),
                pltpu.VMEM((tokens, HD), f32),
                pltpu.SemaphoreType.DMA((dp_size + 4,)),
            ],
            name="attend_back",
        )(
            scalars, query, kv_own, kv_other, starts, *attn, context, cosine, sine,
            *arrays_of(pieces),
        )

    def project_back(scalars, grad_query, kv_kept, kv_arrived, pieces):
        tokens, width = grad_query.shape
        columns = pieces[0][0].shape[1]
        model = dp_size * shard_rows(pieces)
        rows = tokens // 4

        def kernel(scal, query_ref, kept_kv_ref, arrived_ref, *refs):
            grads_ref, kept_ref, sent_ref, held, part, sems, out_sems = refs[dp_size:]
            copies = start_all(attn_jobs(scal[0], refs[:dp_size], pieces, held), sems)
            grads_ref[:, :width] = query_ref[...]
            grads_ref[:, width:] = (kept_kv_ref[...] + arrived_ref[...].astype(f32)).astype(bf16)
            wait_all(copies)
            for at in range(4):
                spot = pl.ds(at * rows, rows)
                part[spot, :] = mm_nt(grads_ref[spot, :], held[...]).astype(bf16)
            wait_all(start_all(back(token_jobs(scal[1], kept_ref, sent_ref, part)), out_sems))

        half = jax.ShapeDtypeStruct((tokens // 2, model), bf16)
        return pl.pallas_call(
            kernel,
            in_specs=[SCALARS, WHOLE, WHOLE, WHOLE] + [ANY] * dp_size,
            out_specs=[WHOLE, ANY, ANY],
            out_shape=[jax.ShapeDtypeStruct((tokens, columns), bf16), half, half],
            scratch_shapes=[
                pltpu.VMEM((model, columns), bf16),
                pltpu.VMEM((tokens, model), bf16),
                pltpu.SemaphoreType.DMA((dp_size,)),
                pltpu.SemaphoreType.DMA((4,)),
            ],
            name="project_back",
        )(scalars, grad_query, kv_kept, kv_arrived, *arrays_of(pieces))

    def shard_rows(pieces):
        return min(piece[0].shape[0] for piece in pieces)

    def gain_rows_of(scalars, kept, sent, pair, core):
        rows, model = kept.shape[0] // 4, kept.shape[1]

        def kernel(scal, kept_ref, sent_ref, pair_ref, core_ref, gain_ref):
            @pl.when(pl.program_id(0) == 0)
            def _():
                gain_ref[...] = jnp.zeros_like(gain_ref)

            total = kept_ref[...].astype(f32) * pair_ref[...].astype(f32)
            total = total + sent_ref[...].astype(f32) * core_ref[...].astype(f32)
            gain_ref[0:1, :] += jnp.sum(total, axis=0, keepdims=True)

        return pl.pallas_call(
            kernel,
            grid=(4,),
            in_specs=[SCALARS] + [pl.BlockSpec((rows, model), lambda i: (i, 0))] * 4,
            out_specs=pl.BlockSpec((8, model), lambda i: (0, 0)),
            out_shape=jax.ShapeDtypeStruct((8, model), f32),
            name="gain_rows",
        )(scalars, kept, sent, pair, core)

    def project_grad(scalars, pair, core, grads):
        tokens, columns = grads.shape
        model = pair.shape[1]

        def kernel(scal, pair_ref, core_ref, grads_ref, kept_ref, sent_ref, acts, sems):
            wait_all(start_all(token_jobs(scal[1], pair_ref, core_ref, acts), sems))
            give(mm_tn(acts[...], grads_ref[...]).astype(bf16), scal, kept_ref, sent_ref)

        return pl.pallas_call(
            kernel,
            in_specs=[SCALARS, ANY, ANY, WHOLE],
            out_specs=[WHOLE] * 2,
            out_shape=[jax.ShapeDtypeStruct((model // 2, columns), bf16)] * 2,
            scratch_shapes=[
                pltpu.VMEM((tokens, model), bf16),
                pltpu.SemaphoreType.DMA((4,)),
            ],
            name="project_grad",
        )(scalars, pair, core, grads)

    def norm_two_back(scalars, own, from_x, from_l, hidden, gain, given):
        rows, model = own.shape

        def kernel(scal, own_ref, x_ref, l_ref, hidden_ref, gain_ref, given_ref, out_ref, low_ref, sum_ref):
            grad_out = own_ref[...] + x_ref[...].astype(f32) + l_ref[...].astype(f32)
            normed, row_scale = norm_forward(hidden_ref[...])
            grad_normed = grad_out * gain_ref[...]
            grad_in = row_scale * (
                grad_normed - normed * jnp.mean(grad_normed * normed, axis=-1, keepdims=True)
            )
            total = given_ref[...].astype(f32) + grad_in
            out_ref[...] = total
            low_ref[...] = total.astype(bf16)
            sum_ref[0:1, :] = jnp.sum(grad_out * normed, axis=0, keepdims=True)

        outs = [((rows, model), f32), ((rows, model), bf16), ((8, model), f32)]
        return whole_call(
            kernel, outs, "norm_two_back", scalars, own, from_x, from_l, hidden, gain, given
        )

    def local(
        block_input,
        segment_ids,
        gain_attn,
        w_query,
        b_query,
        w_keyval,
        b_keyval,
        w_out,
        gain_ffn,
        w_gate,
        w_up,
        w_down,
        cotangent,
    ):
        dp_index = lax.axis_index("dp")
        tensor_index = lax.axis_index("tensor")
        scalars = jnp.stack([dp_index, tensor_index]).astype(jnp.int32)
        local_heads = b_query.shape[0] // HD
        head_kv = tensor_index * local_heads // (HQ // KV)
        is_value = tensor_index % 2
        kv_column = is_value * (KV * HD) + head_kv * HD
        width = local_heads * HD

        groups = dp_size // 4

        def far_rest(kept, sent):
            arrived = swap(sent, "dp", far_bits[0])
            for bit in far_bits[1:]:
                kept, sent = fold_sum(scalars, kept, arrived, bit, 1)
                arrived = swap(sent, "dp", bit)
            return kept, arrived

        keyval_cols = lax.dynamic_slice_in_dim(w_keyval, kv_column, HD, 1)
        qkv_own = jnp.concatenate([w_query, keyval_cols], axis=1)
        shard = qkv_own.shape[0]
        qkv_far = far_pieces(qkv_own)
        qkv_l = swap(qkv_own, "dp", pair_bit)
        qkv_y = swap(qkv_own, "dp", 1)
        rows_float = block_input.astype(f32)
        normed_one, scale_one = norm_forward(rows_float)
        act_own = (normed_one * gain_attn).astype(bf16)
        act_x = swap(act_own, "tensor", 2)
        gate_mine, gate_sent = split_cols(scalars, w_gate)
        gate_theirs = swap(gate_sent, "dp", pair_bit)

        qkv_far_in, qkv_l, qkv_y, out_own, w_up_in, w_down_in, segments = hold(
            [gate_sent, act_own],
            [tuple(qkv_far[1:]), qkv_l, qkv_y, w_out.T, w_up, w_down, segment_ids],
        )
        far_rows = rows_of(*qkv_far_in)
        qkv_y2 = swap(rows_of(qkv_l, far_rows), "dp", 1)
        qkv_l2 = swap(far_rows, "dp", pair_bit)
        out_far = far_pieces(out_own)
        rest_mine, rest_sent = split_cols(scalars, w_up_in, w_down_in.T)
        positions = positions_of(segments[0])
        cosine, sine = rotary(positions)
        sine = jnp.where(jnp.arange(HD)[None, :] < HD // 2, -sine, sine)
        starts = (jnp.arange(positions.shape[0], dtype=jnp.int32) - positions)[:, None]
        qkv_bias = jnp.concatenate([b_query, lax.dynamic_slice_in_dim(b_keyval, kv_column, HD, 0)])[
            None, :
        ]

        qkv_y2, qkv_l2, act_pair, gate_theirs, out_half, cosine, sine, starts, rest_sent, cot_own = (
            hold(
                [],
                [
                    qkv_y2,
                    qkv_l2,
                    rows_of(act_own, act_x),
                    gate_theirs,
                    rows_of(*out_far),
                    cosine,
                    sine,
                    starts,
                    rest_sent,
                    cotangent,
                ],
            )
        )

        def gather_attn():
            return (
                swap(qkv_l2, "dp", 1),
                swap(act_pair, "tensor", 1),
                swap(out_half, "dp", pair_bit),
                join_rows(scalars, gate_mine, gate_theirs, 0, 1),
            )

        qkv_y3, act_c, out_l, gate_piece = section(gather_attn)

        qkv_y3, act_c, out_near, rest_sent, cot_core, gate_piece = hold(
            [], [qkv_y3, act_c, rows_of(out_half, out_l), rest_sent, cotangent, gate_piece]
        )
        gate_far = far_pieces(gate_piece)
        cot_x = swap(cot_core, "tensor", 2)
        rest_theirs = swap(rest_sent, "dp", pair_bit)
        out_y = swap(out_near, "dp", 1)
        far_masks = masks_of(far_bits)
        qkv_pieces = [(part, 0, mask) for part, mask in zip(qkv_far, far_masks)]
        qkv_pieces += [(qkv_l, 0, pair_bit), (qkv_y, 0, 1), (qkv_y2, 0, pair_bit ^ 1)]
        for at, mask in enumerate(far_masks[1:]):
            qkv_pieces += [
                (qkv_y2, (at + 1) * shard, mask ^ 1),
                (qkv_l2, at * shard, mask ^ pair_bit),
                (qkv_y3, at * shard, mask ^ pair_bit ^ 1),
            ]

        def attention():
            query_rot, kv_own = project(
                scalars, act_pair, act_c, qkv_pieces, qkv_bias, cosine, sine
            )
            kv_other = swap(kv_own, "tensor", 1)
            kv_other, cot_given = hold([], [kv_other, cot_core])
            cot_own_c = swap(cot_given, "tensor", 1)
            context = attend(scalars, query_rot, kv_own, kv_other, starts)
            context, cot_own_c = hold([], [context, cot_own_c])
            return query_rot, kv_own, kv_other, context, cot_own_c

        def out_pieces(near, far):
            pieces = []
            masks = masks_of(far_bits + [pair_bit])
            for at, mask in enumerate(masks):
                pieces += [(near, at * shard, mask), (far, at * shard, mask ^ 1)]
            return pieces

        query_rot, kv_own, kv_other, context, cot_own_c = section(attention)
        context, out_y = hold([], [context, out_y])
        out_parts = out_pieces(out_near, out_y)
        attn_kept, attn_sent = out_rows(scalars, context, out_parts, act_pair.shape[1])

        attn_sent, rest_theirs, cot_own_l = hold([cot_x], [attn_sent, rest_theirs, cotangent])

        def sum_cores():
            arrived = swap(attn_sent, "tensor", 1)
            return arrived, join_both(scalars, gate_piece, rest_mine, rest_theirs)

        attn_arrived, (up_piece, own_both) = section(sum_cores)
        attn_arrived, up_piece, own_both = hold([], [attn_arrived, up_piece, own_both])
        up_far = far_pieces(up_piece)
        own_y = swap(own_both, "dp", 1)
        cot_l = swap(cot_own_l, "dp", pair_bit)

        def sum_heads():
            (sent,) = part_sum(scalars, attn_kept, attn_arrived, block_input.shape[0], 1, 1)
            return norm_two(
                scalars, block_input, attn_kept, attn_arrived, swap(sent, "tensor", 2),
                gain_ffn[None, :],
            )

        hidden, two_own = section(sum_heads)

        two_own, gate_halves = hold([cot_l], [two_own, tuple(gate_far[1:])])
        gate_y2 = [swap(part, "dp", 1) for part in gate_halves]

        def gather_near():
            two_x = swap(two_own, "tensor", 2)
            two_l = swap(two_own, "dp", pair_bit)
            return two_x, two_l, join_rows(scalars, rest_mine, rest_theirs, 1, 2)

        two_x, two_l, down_piece = section(gather_near)

        rows = two_own.shape[0]
        two_x, two_l, up_halves = hold([own_y, gate_y2], [two_x, two_l, tuple(up_far[1:])])
        up_y2 = [swap(part, "dp", 1) for part in up_halves]

        def gather_rest():
            given_a, given_b = halves(scalars, two_l, two_x)
            far_a = swap(given_a, "tensor", 2)
            far_b = swap(given_b, "dp", pair_bit)

            def cores():
                given, arrived = [two_x, two_l, two_own], []
                for at in range(3):
                    part = swap(given[at], "tensor", 1)
                    part, *given = hold([], [part] + given)
                    arrived.append(part)
                return arrived

            arrived = section(cores)
            return hold([], [far_a, far_b, *arrived])

        far_a, far_b, two_x_c, two_l_c, two_own_c = section(gather_rest)
        far_a, far_b, down_piece = hold(up_y2, [far_a, far_b, down_piece])
        down_far = far_pieces(down_piece)

        def gather_far():
            return swap(far_a, "tensor", 1), swap(far_b, "tensor", 1)

        far_a_c, far_b_c = section(gather_far)
        two_pieces = [two_own, two_x, two_l]
        two_pieces_c = [two_own_c, two_x_c, two_l_c]

        size = gate_piece.shape[0]
        gate_pieces = [(part, 0) for part in [*gate_far]] + [
            (part, 0) for part in [own_y, *gate_y2]
        ]
        up_pieces = [(part, 0) for part in [*up_far]] + [(own_y, size)] + [
            (part, 0) for part in up_y2
        ]
        far_a, far_b, far_a_c, far_b_c, down_piece_y, cot_x, cot_l = hold(
            [], [far_a, far_b, far_a_c, far_b_c, down_piece, cot_x, cot_l]
        )
        two_pieces += [far_a, far_b]
        two_pieces_c += [far_a_c, far_b_c]

        def feed_own():
            down_y1 = swap(down_piece_y, "dp", 1)
            cot_far = swap(cot_l, "tensor", 2)
            x_c = swap(cot_x, "tensor", 1)
            own = ffn_up(scalars, two_pieces, gate_pieces, up_pieces)
            down_y1, cot_far, x_c = hold([own], [down_y1, cot_far, x_c])
            return down_y1, cot_far, x_c, own

        down_y1, cot_far, cot_x_c, (acts_a, mixed_a, silu_a, back_a) = section(feed_own)

        mixed_a, cot_l_in = hold([], [mixed_a, cot_l])

        def feed_core():
            l_c = swap(cot_l_in, "tensor", 1)
            far_c = swap(cot_far, "tensor", 1)
            core = ffn_up(scalars, two_pieces_c, gate_pieces, up_pieces)
            l_c, far_c = hold([core], [l_c, far_c])
            return l_c, far_c, core

        cot_l_c, cot_far_c, (acts_b, mixed_b, silu_b, back_b) = section(feed_core)

        cots = [cotangent, cot_x, cot_l, cot_far]
        cots_c = [cot_own_c, cot_x_c, cot_l_c, cot_far_c]
        mixed_b, down_halves = hold([down_y1], [mixed_b, tuple(down_far[1:])])
        down_y2 = tuple(swap(part, "dp", 1) for part in down_halves)
        down_kept, down_sent = section(
            lambda: ffn_grad(scalars, cots, cots_c, mixed_a, mixed_b, "grad_down")
        )
        down_sent, down_y2 = hold([], [down_sent, down_y2])
        down_pieces = [(part, 0) for part in [*down_far, down_y1, *down_y2]]

        down_sent, silu_b = hold([], [down_sent, silu_b])
        down_sent = swap(down_sent, "dp", 1)

        def back_all():
            gate_b, up_b, two_sent = ffn_back(
                scalars, cots_c, down_pieces, gate_pieces, up_pieces, silu_b, back_b
            )
            (two_sent,) = hold([], [two_sent])
            arrived = swap(two_sent, "tensor", 1)
            gate_a, up_a, kept = ffn_back(
                scalars, cots, down_pieces, gate_pieces, up_pieces, silu_a, back_a
            )
            (kept,) = hold([], [kept])
            far = part_sum(scalars, kept, arrived, kept.shape[0] // 4, 3, 2)
            return gate_a, up_a, gate_b, up_b, kept, arrived, *far

        gate_a, up_a, gate_b, up_b, two_kept, two_arrived, far_a, far_b = section(back_all)

        far_a, far_b, mixed_b = hold([], [far_a, far_b, mixed_b])
        model = far_a.shape[1]

        def spread_far():
            far_x = swap(far_a, "tensor", 2)
            far_l = swap(far_b, "dp", pair_bit)

            def block_rows():
                sent = ffn_rows(scalars, mixed_b, down_pieces, model, "block_rows")
                (sent,) = hold([], [sent])
                arrived = swap(sent, "tensor", 1)
                kept = ffn_rows(scalars, mixed_a, down_pieces, model, "block_rows")
                return hold([], [kept, arrived])

            outs = section(block_rows)
            outs, far_x, far_l = hold([], [outs, far_x, far_l])
            return (*outs, *spread_rest(scalars, two_kept, two_arrived, far_x, far_l))

        block_kept, block_arrived, own, to_x, to_l = section(spread_far)

        to_x, to_l, down_sent = hold([], [to_x, to_l, down_sent])

        def spread_near():
            from_x = swap(to_x, "tensor", 2)
            from_l = swap(to_l, "dp", pair_bit)
            up_grads = ffn_grad(scalars, [acts_a], [acts_b], up_a, up_b, "grad_up")
            down_pair = fold_sum(scalars, down_kept, down_sent, far_bits[0], 1)
            block_rows = 2 * own.shape[0]
            block_pair = part_sum(scalars, block_kept, block_arrived, block_rows, 1, 1)
            from_x, from_l = hold([up_grads, down_pair, block_pair], [from_x, from_l])
            return (
                *up_grads,
                *down_pair,
                *block_pair,
                *norm_two_back(
                    scalars, own, from_x, from_l, hidden, gain_ffn[None, :], cotangent
                ),
            )

        (
            up_kept, up_sent, down_kept, down_sent, block_sent, grad_hidden, attn_own, gain_two,
        ) = section(spread_near)

        attn_own, down_sent, up_sent, gate_b, block_sent = hold(
            [], [attn_own, down_sent, up_sent, gate_b, block_sent]
        )
        down_kept, down_sent = far_rest(down_kept, down_sent)
        up_sent = swap(up_sent, "dp", 1)
        block_from_l = swap(block_sent, "dp", pair_bit)

        def attention_back():
            def gather_back():
                attn_x = swap(attn_own, "tensor", 2)
                own_c = swap(attn_own, "tensor", 1)
                gate_grads = ffn_grad(scalars, [acts_a], [acts_b], gate_a, gate_b, "grad_gate")
                attn_x, own_c = hold([gate_grads], [attn_x, own_c])
                return (attn_x, own_c, *gate_grads)

            attn_x, own_c, gate_kept, gate_sent = section(gather_back)
            attn_x, own_c, gate_sent = hold([], [attn_x, own_c, gate_sent])
            x_c = swap(attn_x, "tensor", 1)
            outs = attend_back(
                scalars, query_rot, kv_own, kv_other, starts, out_parts,
                [attn_own, attn_x, own_c, x_c], context, cosine, sine,
            )
            return gate_kept, gate_sent, outs

        gate_kept, gate_sent, outs = section(attention_back)
        grad_query_low, kv_kept, kv_given, bias_rows, wout_kept, wout_sent = outs

        kv_given, up_sent = hold([], [kv_given, up_sent])

        def pass_keys():
            kv_arrived = swap(kv_given, "tensor", 1)
            up_pair = fold_sum(scalars, up_kept, up_sent, far_bits[0], 1)
            (kv_arrived,) = hold([up_pair], [kv_arrived])
            return kv_arrived, *up_pair

        kv_arrived, up_own, up_given = section(pass_keys)
        kv_arrived, up_given, wout_sent, gate_sent, down_sent, block_from_l = hold(
            [], [kv_arrived, up_given, wout_sent, gate_sent, down_sent, block_from_l]
        )
        wout_arrived = swap(wout_sent, "dp", pair_bit)
        devices = dp_size * tensor_size

        def input_grads():
            kv_in, gate_in, up_in = hold([], [kv_arrived, gate_sent, up_given])
            gate_y = swap(gate_in, "dp", 1)
            up_sum, up_far_sum = far_rest(up_own, up_in)

            def project_all():
                grad_qkv, one_kept, one_sent = project_back(
                    scalars, grad_query_low, kv_kept, kv_in, qkv_pieces
                )
                one_sent, grad_qkv = hold([], [one_sent, grad_qkv])
                arrived = swap(one_sent, "tensor", 1)
                wqkv_pair = project_grad(scalars, act_pair, act_c, grad_qkv)
                (arrived,) = hold([wqkv_pair], [arrived])
                wqkv_kept, wqkv_sent = wqkv_pair
                one_partner = one_sent
                (one_given,) = part_sum(scalars, one_kept, arrived, block_input.shape[0], 1, 1)
                one_arrived = arrived

                def first_norm_back():
                    arrived = swap(one_given, "tensor", 2)
                    wqkv_arrived = swap(wqkv_sent, "dp", pair_bit)
                    block = block_x_sum(scalars, block_kept, block_arrived, block_from_l)
                    down_pair = fold_sum(scalars, down_kept, down_sent, pair_bit, 1)
                    gain_rows = gain_rows_of(scalars, one_kept, one_partner, act_pair, act_c)
                    bias_keyval = jnp.zeros((2 * KV * HD,), f32)
                    bias_keyval = lax.dynamic_update_slice_in_dim(
                        bias_keyval, bias_rows[0, width : width + HD], head_kv * HD, 0
                    )
                    bias_keyval = lax.dynamic_update_slice_in_dim(
                        bias_keyval, bias_rows[0, width + HD :], KV * HD + head_kv * HD, 0
                    )
                    bias_query = lax.dynamic_update_slice_in_dim(
                        jnp.zeros((HQ * HD,), f32), bias_rows[0, :width], tensor_index * width, 0
                    )
                    parts = (gain_rows[0] / gain_attn, gain_two[0], bias_query, bias_keyval)
                    small = jnp.concatenate([part.reshape(devices, -1) for part in parts], axis=1)
                    (arrived,) = hold([block, small, down_pair], [arrived])
                    grad_rows = norm_one_back(
                        scalars, block_input, one_kept, one_arrived, arrived, gain_attn[None, :],
                        grad_hidden,
                    )
                    (wqkv_arrived,) = hold([grad_rows], [wqkv_arrived])
                    return (*down_pair, wqkv_kept, grad_rows, small, block, wqkv_arrived)

                return section(first_norm_back)

            outs = section(project_all)
            outs, gate_y, up_far_sum = hold([], [outs, gate_y, up_far_sum])
            return (up_sum, up_far_sum, gate_y, *outs)

        (
            up_kept, up_sent, gate_sent, down_mine, down_given, wqkv_kept, grad_rows, small,
            block_to_x, wqkv_arrived,
        ) = section(input_grads)

        wqkv_arrived, wout_arrived, gate_sent, small, down_given = hold(
            [], [wqkv_arrived, wout_arrived, gate_sent, small, down_given]
        )
        gate_kept, gate_sent = fold_sum(scalars, gate_kept, gate_sent, far_bits[0], 1)
        wqkv_arrived, gate_sent, small = hold([], [wqkv_arrived, gate_sent, small])
        gate_kept, gate_sent = far_rest(gate_kept, gate_sent)
        small = lax.all_to_all(small, ("dp", "tensor"), 0, 0, tiled=True)

        def last_rows():
            block_x = swap(block_to_x, "tensor", 2)
            down_theirs = swap(down_given, "dp", pair_bit)

            def attn_step():
                own, sent = fold_both(
                    scalars, wqkv_kept, wqkv_arrived, wout_kept, wout_arrived, 1, groups
                )
                arrived = swap(sent, "dp", 1)
                up_pair = fold_sum(scalars, up_kept, up_sent, pair_bit, 1)
                (arrived,) = hold([up_pair], [arrived])
                return (*fold_sum(scalars, own, arrived, far_bits[0], 1), *up_pair)

            *attn_outs, block_x, down_theirs = hold(
                [], [*section(attn_step), block_x, down_theirs]
            )
            block_out = block_final(
                scalars, block_kept, block_arrived, block_from_l, hidden, block_x
            )
            down_share = join_cols(scalars, down_mine, down_theirs, w_down.shape[0] // 2).T
            return *attn_outs, block_out, down_share

        attn_kept, attn_sent, up_mine, up_given, block_out, down_share = section(last_rows)

        gate_sent, attn_sent, up_given, small = hold(
            [block_out, down_share], [gate_sent, attn_sent, up_given, small]
        )
        attn_kept, attn_sent = far_rest(attn_kept, attn_sent)
        up_theirs = swap(up_given, "dp", pair_bit)
        gate_mine, gate_given = fold_sum(scalars, gate_kept, gate_sent, pair_bit, 1)
        gate_theirs = swap(gate_given, "dp", pair_bit)
        small = jnp.sum(small, axis=0)
        up_theirs = hold([gate_given, small], [up_theirs])[0]
        up_share = join_cols(scalars, up_mine, up_theirs, w_up.shape[1] // 2)
        (attn_sent,) = hold([up_share], [attn_sent])
        share = add(attn_kept, attn_sent)
        kv_rows = share[:, width : width + HD]
        share_rows = kv_rows.shape[0] // tensor_size
        moved = []
        for mask in range(tensor_size):
            rows_for = lax.dynamic_slice_in_dim(
                kv_rows, (tensor_index ^ mask) * share_rows, share_rows, 0
            )
            moved.append(swap(rows_for, "tensor", mask) if mask else rows_for)
        query_share, out_share = share[:, :width], share[:, width + HD :].T
        gate_theirs, *moved = hold([query_share, out_share], [gate_theirs] + moved)
        gate_share = join_cols(scalars, gate_mine, gate_theirs, w_gate.shape[1] // 2)
        keyval_share = jnp.zeros((share_rows, 2 * KV * HD), f32)
        for mask in range(tensor_size):
            sender = tensor_index ^ mask
            column = (sender % 2) * (KV * HD) + (sender * local_heads // (HQ // KV)) * HD
            keyval_share = lax.dynamic_update_slice_in_dim(keyval_share, moved[mask], column, 1)
        sizes = [HQ * HD // devices, 2 * KV * HD // devices, gain_attn.shape[0] // devices]
        ends = [sizes[2], 2 * sizes[2], 2 * sizes[2] + sizes[0]]
        gain_one_share = small[: ends[0]]
        gain_two_share = small[ends[0] : ends[1]]
        query_bias_share = small[ends[1] : ends[2]]
        keyval_bias_share = small[ends[2] :]
        return (
            block_out,
            grad_rows,
            gain_one_share,
            query_share,
            query_bias_share,
            keyval_share,
            keyval_bias_share,
            out_share,
            gain_two_share,
            gate_share,
            up_share,
            down_share,
        )

    placed = (
        P(("dp", "tensor"), None),
        P("dp", None),
        P(),
        P("dp", "tensor"),
        P("tensor"),
        P("dp", None),
        P(),
        P("tensor", "dp"),
        P(),
        P("dp", "tensor"),
        P("dp", "tensor"),
        P("tensor", "dp"),
        P(("dp", "tensor"), None),
    )
    return jax.shard_map(
        local,
        mesh=mesh,
        in_specs=placed,
        out_specs=(
            P(("dp", "tensor"), None),
            P(("dp", "tensor"), None),
            P(("dp", "tensor")),
            P("dp", "tensor"),
            P(("dp", "tensor")),
            P(("dp", "tensor"), None),
            P(("dp", "tensor")),
            P("tensor", "dp"),
            P(("dp", "tensor")),
            P("dp", "tensor"),
            P("dp", "tensor"),
            P("tensor", "dp"),
        ),
        check_vma=False,
    )
```

```python
import math

import jax
import jax.numpy as jnp
from jax import lax
from jax.experimental import pallas as pl
from jax.experimental.pallas import tpu as pltpu
from jax.sharding import PartitionSpec as P

HQ = 12
KV = 2
HD = 128


epsilon = 1e-06
rope_base = 1000000.0
masked_score = -1e30
bf16 = jnp.bfloat16
f32 = jnp.float32


def positions_of(segment_row):
    index_row = jnp.arange(segment_row.shape[0], dtype=jnp.int32)
    starts = jnp.concatenate(
        [jnp.ones((1,), jnp.int32), (segment_row[1:] != segment_row[:-1]).astype(jnp.int32)]
    )
    first_index = lax.cummax(jnp.where(starts > 0, index_row, 0), axis=0)
    return index_row - first_index


def rotary(positions):
    inverse = rope_base ** (-(jnp.arange(HD // 2, dtype=jnp.float32) * 2.0 / HD))
    angles = positions.astype(jnp.float32)[:, None] * inverse[None, :]
    angles = jnp.concatenate([angles, angles], axis=1)
    return (jnp.cos(angles), jnp.sin(angles))


def norm_forward(values_in):
    row_scale = lax.rsqrt(jnp.mean(values_in * values_in, axis=-1, keepdims=True) + epsilon)
    return (values_in * row_scale, row_scale)


def norm_backward(grad_out, normed, row_scale, gain_vec):
    grad_normed = grad_out * gain_vec
    grad_in = row_scale * (
        grad_normed - normed * jnp.mean(grad_normed * normed, axis=-1, keepdims=True)
    )
    return (grad_in, jnp.sum(grad_out * normed, axis=0))


ANY = pl.BlockSpec(memory_space=pl.ANY)
WHOLE = pl.BlockSpec(memory_space=pltpu.VMEM)
SCALARS = pl.BlockSpec(memory_space=pltpu.SMEM)


def made(jobs, sems, first=0):
    return [
        pltpu.make_async_copy(src, dst, sems.at[first + at]) for at, (src, dst) in enumerate(jobs)
    ]


def start_all(jobs, sems):
    copies = made(jobs, sems)
    for copy in copies:
        copy.start()
    return copies


def wait_all(copies):
    for copy in copies:
        copy.wait()


def block(ref, at, rows):
    return ref.at[pl.ds(pl.multiple_of(at * rows, rows), rows)]


def turned(values, cosine, sine, sign):
    return values * cosine + sign * (pltpu.roll(values, HD // 2, 1) * sine)


def mm(left, right):
    return lax.dot_general(left, right, (((1,), (0,)), ((), ())), preferred_element_type=f32)


def mm_nt(left, right):
    return lax.dot_general(left, right, (((1,), (1,)), ((), ())), preferred_element_type=f32)


def mm_tn(left, right):
    return lax.dot_general(left, right, (((0,), (0,)), ((), ())), preferred_element_type=f32)


def hold(due, release):
    out = lax.optimization_barrier((tuple(due), tuple(release)))
    return out[1]


def section(body):
    outs = jax.eval_shape(body)
    return lax.cond(
        lax.optimization_barrier(jnp.bool_(True)),
        body,
        lambda: jax.tree.map(lambda out: jnp.zeros(out.shape, out.dtype), outs),
    )


def solution(mesh):
    dp_size = mesh.shape["dp"]
    tensor_size = mesh.shape["tensor"]
    pair_bit = 2
    far_bits = []
    bit = dp_size // 2
    while bit > pair_bit:
        far_bits.append(bit)
        bit //= 2
    ring_bits = far_bits + [1]

    def swap(array, axis, bit):
        size = mesh.shape[axis]
        with jax.named_scope(f"swap_{axis}_{bit}"):
            return lax.ppermute(array, axis, [(i, i ^ bit) for i in range(size)])

    def masks_of(bits):
        masks = [0]
        for bit in bits:
            masks = masks + [mask ^ bit for mask in masks]
        return masks

    def rows_of(*pieces):
        return jnp.concatenate(pieces, axis=0)

    def far_pieces(piece):
        pieces = [piece]
        for bit in far_bits:
            pieces = pieces + [swap(part, "dp", bit) for part in pieces]
        return pieces

    def fold(total, axis, bit):
        half = total.shape[0] // 2
        return total[:half], swap(total[half:].astype(bf16), axis, bit)

    def add(kept, arrived):
        return kept.astype(f32) + arrived.astype(f32)

    ring_masks = masks_of(ring_bits)
    ring_mask = sum(ring_bits)
    count = len(ring_masks)


    def ffn_jobs(dp_index, refs, offsets, held):
        rows = held.shape[0] // dp_size
        jobs = []
        for mask, ref, offset in zip(ring_masks, refs, offsets):
            base = jnp.bitwise_xor(jnp.bitwise_and(dp_index, ring_mask), mask)
            for low in (0, 1):
                jobs.append(
                    (
                        ref.at[pl.ds(offset + low * rows, rows)],
                        block(held, base + low * pair_bit, rows),
                    )
                )
        return jobs

    def row_jobs(refs, held):
        jobs, start = [], 0
        for ref in refs:
            jobs.append((ref, held.at[pl.ds(start, ref.shape[0])]))
            start += ref.shape[0]
        return jobs

    def attn_jobs(dp_index, refs, pieces, held):
        rows = held.shape[0] // dp_size
        return [
            (
                ref.at[pl.ds(first, rows)],
                block(held, jnp.bitwise_xor(dp_index, mask), rows),
            )
            for ref, (_, first, mask) in zip(refs, pieces)
        ]

    def arrays_of(pieces):
        return [piece[0] for piece in pieces]

    token_masks = ((0, 2), (1, 3))

    def token_jobs(tensor_index, pair, other, held):
        rows = held.shape[0] // 4
        jobs = []
        for masks, ref in zip(token_masks, (pair, other)):
            for at, mask in enumerate(masks):
                spot = jnp.bitwise_xor(tensor_index, mask)
                jobs.append((ref.at[pl.ds(at * rows, rows)], block(held, spot, rows)))
        return jobs

    def quarter_jobs(tensor_index, refs, held):
        rows = held.shape[0] // 4
        return [
            (ref, block(held, jnp.bitwise_xor(tensor_index, mask), rows))
            for ref, mask in zip(refs, (0, 2, 1, 3))
        ]

    def back(jobs):
        return [(dst, src) for src, dst in jobs]

    def ffn_up(scalars, pieces, gate_pieces, up_pieces):
        tokens, model = sum(piece.shape[0] for piece in pieces), pieces[0].shape[1]
        units = gate_pieces[0][0].shape[1]
        rows = tokens // 2
        many = len(pieces)
        early = 2

        def kernel(scal, *refs):
            parts = refs[:many]
            gates = refs[many : many + count]
            ups = refs[many + count : many + 2 * count]
            acts_ref, mixed_ref, silu_ref, back_ref, acts, gate_w, up_w, sems = refs[
                many + 2 * count :
            ]
            jobs = row_jobs(parts, acts)
            gate_jobs = ffn_jobs(scal[0], gates, [at for _, at in gate_pieces], gate_w)
            up_jobs = ffn_jobs(scal[0], ups, [at for _, at in up_pieces], up_w)
            step = pl.program_id(0)

            @pl.when(step == 0)
            def _():
                copies = start_all(jobs[:early] + gate_jobs + jobs[early:] + up_jobs, sems)
                wait_all(copies[: early + 2 * count])

            @pl.when(step == 1)
            def _():
                wait_all(made(jobs[early:], sems, early + 2 * count))

            spot = pl.ds(pl.multiple_of(step * rows, rows), rows)
            rows_in = acts[spot, :]
            acts_ref[...] = rows_in
            gate = mm(rows_in, gate_w[...])

            @pl.when(step == 0)
            def _():
                wait_all(made(up_jobs, sems, many + 2 * count))

            up = mm(rows_in, up_w[...])
            sig = jax.nn.sigmoid(gate)
            silu = gate * sig
            mixed_ref[...] = (silu * up).astype(bf16)
            silu_ref[...] = silu.astype(bf16)
            back_ref[...] = (up * sig * (1.0 + gate * (1.0 - sig))).astype(bf16)

        out = jax.ShapeDtypeStruct((tokens, units), bf16)
        spec = pl.BlockSpec((rows, units), lambda i: (i, 0))
        return pl.pallas_call(
            kernel,
            grid=(2,),
            in_specs=[SCALARS] + [ANY] * (many + 2 * count),
            out_specs=[pl.BlockSpec((rows, model), lambda i: (i, 0))] + [spec] * 3,
            out_shape=[jax.ShapeDtypeStruct((tokens, model), bf16)] + [out] * 3,
            scratch_shapes=[
                pltpu.VMEM((tokens, model), bf16),
                pltpu.VMEM((model, units), bf16),
                pltpu.VMEM((model, units), bf16),
                pltpu.SemaphoreType.DMA((many + 4 * count,)),
            ],
            name="ffn_up",
        )(
            scalars,
            *pieces,
            *[ref for ref, _ in gate_pieces],
            *[ref for ref, _ in up_pieces],
        )

    def ffn_back(scalars, cots, down_pieces, gate_pieces, up_pieces, silu, back_part):
        many = len(cots)
        tokens, model = sum(piece.shape[0] for piece in cots), cots[0].shape[1]
        units = silu.shape[1]
        rows = tokens // 2
        lists = (down_pieces, gate_pieces, up_pieces)

        def kernel(scal, *refs):
            parts = refs[:many]
            pieces = [refs[many + at * count : many + (at + 1) * count] for at in range(3)]
            silu_ref, back_ref, grad_gate_ref, grad_up_ref, out_ref = refs[
                many + 3 * count : many + 3 * count + 5
            ]
            cot, *held = refs[many + 3 * count + 5 : -1]
            sems = refs[-1]
            jobs = row_jobs(parts, cot)
            for at in range(3):
                jobs += ffn_jobs(scal[0], pieces[at], [spot for _, spot in lists[at]], held[at])
            first = pl.program_id(0) == 0
            early = many + 2 * count

            @pl.when(first)
            def _():
                wait_all(start_all(jobs, sems)[:early])

            spot = pl.ds(pl.multiple_of(pl.program_id(0) * rows, rows), rows)
            grad_mixed = mm(cot[spot, :], held[0][...])
            grad_gate = (grad_mixed * back_ref[...].astype(f32)).astype(bf16)
            grad_up = (grad_mixed * silu_ref[...].astype(f32)).astype(bf16)
            grad_gate_ref[...] = grad_gate
            grad_up_ref[...] = grad_up

            @pl.when(first)
            def _():
                wait_all(made(jobs[early:], sems, early))

            out_ref[...] = (
                mm_nt(grad_gate, held[1][...]) + mm_nt(grad_up, held[2][...])
            ).astype(bf16)

        out = jax.ShapeDtypeStruct((tokens, units), bf16)
        spec = pl.BlockSpec((rows, units), lambda i: (i, 0))
        wide = pl.BlockSpec((rows, model), lambda i: (i, 0))
        return pl.pallas_call(
            kernel,
            grid=(2,),
            in_specs=[SCALARS] + [ANY] * (many + 3 * count) + [spec, spec],
            out_specs=[spec, spec, wide],
            out_shape=[out, out, jax.ShapeDtypeStruct((tokens, model), bf16)],
            scratch_shapes=[pltpu.VMEM((tokens, model), bf16)]
            + [pltpu.VMEM((model, units), bf16)] * 3
            + [pltpu.SemaphoreType.DMA((many + 6 * count,))],
            name="ffn_back",
        )(scalars, *cots, *[ref for pieces in lists for ref, _ in pieces], silu, back_part)

    def ffn_rows(scalars, left, pieces, model, name):
        tokens, units = left.shape
        rows = tokens // 2

        def kernel(scal, left_ref, *refs):
            parts = refs[:count]
            out_ref, held, sems = refs[count:]

            @pl.when(pl.program_id(0) == 0)
            def _():
                wait_all(
                    start_all(ffn_jobs(scal[0], parts, [at for _, at in pieces], held), sems)
                )

            out_ref[...] = mm_nt(left_ref[...], held[...]).astype(bf16)

        return pl.pallas_call(
            kernel,
            grid=(2,),
            in_specs=[SCALARS, pl.BlockSpec((rows, units), lambda i: (i, 0))] + [ANY] * count,
            out_specs=pl.BlockSpec((rows, model), lambda i: (i, 0)),
            out_shape=jax.ShapeDtypeStruct((tokens, model), bf16),
            scratch_shapes=[
                pltpu.VMEM((model, units), bf16),
                pltpu.SemaphoreType.DMA((2 * count,)),
            ],
            name=name,
        )(scalars, left, *[ref for ref, _ in pieces])

    def ffn_grad(scalars, own_pieces, core_pieces, low, high, name):
        pieces = [*own_pieces, *core_pieces]
        many = len(own_pieces)
        tokens, model = low.shape[0], pieces[0].shape[1]
        units = low.shape[1]
        shard = model // dp_size
        wide = 384
        groups = wide // (2 * shard)

        def kernel(scal, *refs):
            def stack(parts):
                values = [part[...] for part in parts]
                return values[0] if len(values) == 1 else jnp.concatenate(values, axis=0)

            low_ref, high_ref, kept_ref, sent_ref = refs[2 * many :]
            total = mm_tn(stack(refs[:many]), low_ref[...])
            total = total + mm_tn(stack(refs[many : 2 * many]), high_ref[...])
            total = total.astype(bf16)
            odd = jnp.bitwise_and(scal[0], 1) == 1
            for group in range(groups):
                first = total[group * 2 * shard : group * 2 * shard + shard]
                second = total[group * 2 * shard + shard : (group + 1) * 2 * shard]
                spot = pl.ds(group * shard, shard)
                kept_ref[spot, :] = jnp.where(odd, second, first)
                sent_ref[spot, :] = jnp.where(odd, first, second)

        out = jax.ShapeDtypeStruct((model // 2, units), bf16)
        spec = pl.BlockSpec((wide // 2, units), lambda i: (i, 0))
        whole = pl.BlockSpec((tokens, units), lambda i: (0, 0))
        return pl.pallas_call(
            kernel,
            grid=(model // wide,),
            in_specs=[SCALARS]
            + [pl.BlockSpec((piece.shape[0], wide), lambda i: (0, i)) for piece in pieces]
            + [whole, whole],
            out_specs=[spec] * 2,
            out_shape=[out] * 2,
            name=name,
        )(scalars, *pieces, low, high)

    def is_high(scal, bit):
        return jnp.bitwise_and(scal[0], bit) != 0

    def whole_call(kernel, outs, name, *args):
        return pl.pallas_call(
            kernel,
            in_specs=[SCALARS] + [WHOLE] * (len(args) - 1),
            out_specs=[WHOLE] * len(outs),
            out_shape=[jax.ShapeDtypeStruct(shape, kind) for shape, kind in outs],
            name=name,
        )(*args)

    def split_cols(scalars, *arrays):
        rows, half = arrays[0].shape[0], arrays[0].shape[1] // 2
        wide = -(-half // 128) * 128
        many = len(arrays)

        def kernel(scal, *refs):
            mine_ref, sent_ref = refs[many:]
            flag = is_high(scal, pair_bit)
            mine_ref[...] = jnp.zeros_like(mine_ref)
            sent_ref[...] = jnp.zeros_like(sent_ref)
            for at in range(many):
                low, high = refs[at][:, :half], refs[at][:, half:]
                mine_ref[at * rows : (at + 1) * rows, :half] = jnp.where(flag, high, low)
                sent_ref[at * rows : (at + 1) * rows, :half] = jnp.where(flag, low, high)

        return whole_call(
            kernel, [((many * rows, wide), bf16)] * 2, "split_cols", scalars, *arrays
        )

    def join_rows(scalars, mine, theirs, at, many):
        rows, columns = mine.shape[0] // many, mine.shape[1]
        spot = pl.ds(at * rows, rows)

        def kernel(scal, mine_ref, theirs_ref, out_ref):
            flag = is_high(scal, pair_bit)
            out_ref[:rows, :] = jnp.where(flag, theirs_ref[spot, :], mine_ref[spot, :])
            out_ref[rows:, :] = jnp.where(flag, mine_ref[spot, :], theirs_ref[spot, :])

        return whole_call(
            kernel, [((2 * rows, columns), bf16)], "join_rows", scalars, mine, theirs
        )[0]

    def join_cols(scalars, mine, theirs, columns):
        rows = mine.shape[0]

        def kernel(scal, mine_ref, theirs_ref, out_ref):
            flag = is_high(scal, pair_bit)
            mine = mine_ref[:, :columns].astype(f32)
            theirs = theirs_ref[:, :columns].astype(f32)
            out_ref[:, :columns] = jnp.where(flag, theirs, mine)
            out_ref[:, columns:] = jnp.where(flag, mine, theirs)

        return whole_call(
            kernel, [((rows, 2 * columns), f32)], "join_cols", scalars, mine, theirs
        )[0]

    def fold_sum(scalars, kept, arrived, bit, outer):
        rows, columns = kept.shape[0] // 2, kept.shape[1]
        part = rows // outer

        def kernel(scal, kept_ref, arrived_ref, own_ref, sent_ref):
            flag = is_high(scal, bit)
            for at in range(outer):
                first = pl.ds(2 * at * part, part)
                second = pl.ds((2 * at + 1) * part, part)
                low = kept_ref[first, :].astype(f32) + arrived_ref[first, :].astype(f32)
                high = kept_ref[second, :].astype(f32) + arrived_ref[second, :].astype(f32)
                spot = pl.ds(at * part, part)
                own_ref[spot, :] = jnp.where(flag, high, low).astype(bf16)
                sent_ref[spot, :] = jnp.where(flag, low, high).astype(bf16)

        return whole_call(
            kernel, [((rows, columns), bf16)] * 2, "fold_sum", scalars, kept, arrived
        )

    def norm_two(scalars, rows_in, kept, sums, arrived, gain):
        rows, columns = rows_in.shape

        def kernel(scal, kept_ref, sums_ref, in_ref, arrived_ref, gain_ref, hidden_ref, out_ref):
            hidden = in_ref[...].astype(f32) + kept_ref[...].astype(f32)
            hidden = hidden + sums_ref[...].astype(f32) + arrived_ref[...].astype(f32)
            hidden_ref[...] = hidden
            out_ref[...] = (norm_forward(hidden)[0] * gain_ref[...]).astype(bf16)

        return part_call(
            kernel, [((rows, columns), f32), ((rows, columns), bf16)], "norm_two", scalars,
            [(kept, rows, 0), (sums, rows, 0)], [rows_in, arrived, gain],
        )

    def norm_one_back(scalars, rows_in, kept, sums, arrived, gain, given):
        rows, columns = rows_in.shape

        def kernel(scal, kept_ref, sums_ref, in_ref, arrived_ref, gain_ref, given_ref, out_ref):
            grad_out = kept_ref[...].astype(f32) + sums_ref[...].astype(f32)
            grad_out = grad_out + arrived_ref[...].astype(f32)
            normed, row_scale = norm_forward(in_ref[...].astype(f32))
            grad_normed = grad_out * gain_ref[...]
            grad_in = row_scale * (
                grad_normed - normed * jnp.mean(grad_normed * normed, axis=-1, keepdims=True)
            )
            out_ref[...] = (given_ref[...] + grad_in).astype(bf16)

        return part_call(
            kernel, [((rows, columns), bf16)], "norm_one_back", scalars,
            [(kept, rows, 0), (sums, rows, 0)], [rows_in, arrived, gain, given],
        )[0]

    def join_both(scalars, first, mine, theirs):
        rows, columns = mine.shape[0] // 2, mine.shape[1]

        def kernel(scal, first_ref, mine_ref, theirs_ref, out_ref, both_ref):
            flag = is_high(scal, pair_bit)
            low = jnp.where(flag, theirs_ref[:rows, :], mine_ref[:rows, :])
            high = jnp.where(flag, mine_ref[:rows, :], theirs_ref[:rows, :])
            out_ref[:rows, :] = low
            out_ref[rows:, :] = high
            both_ref[: 2 * rows, :] = first_ref[...]
            both_ref[2 * rows : 3 * rows, :] = low
            both_ref[3 * rows :, :] = high

        return whole_call(
            kernel,
            [((2 * rows, columns), bf16), ((4 * rows, columns), bf16)],
            "join_both", scalars, first, mine, theirs,
        )

    def halves(scalars, first, second):
        rows, columns = first.shape[0] // 2, first.shape[1]

        def kernel(scal, first_ref, second_ref, out_a_ref, out_b_ref):
            out_a_ref[...] = first_ref[:rows, :]
            out_b_ref[...] = second_ref[rows:, :]

        return whole_call(
            kernel, [((rows, columns), bf16)] * 2, "halves", scalars, first, second
        )

    def fold_both(scalars, first, first_arrived, second, second_arrived, bit, outer):
        rows = first.shape[0] // 2
        columns = (first.shape[1], second.shape[1])
        part = rows // outer

        def kernel(scal, first_ref, first_in_ref, second_ref, second_in_ref, own_ref, sent_ref):
            flag = is_high(scal, bit)
            for lanes, kept_ref, arrived_ref in (
                (slice(0, columns[0]), first_ref, first_in_ref),
                (slice(columns[0], columns[0] + columns[1]), second_ref, second_in_ref),
            ):
                for at in range(outer):
                    low_spot = pl.ds(2 * at * part, part)
                    high_spot = pl.ds((2 * at + 1) * part, part)
                    low = kept_ref[low_spot, :].astype(f32) + arrived_ref[low_spot, :].astype(f32)
                    high = kept_ref[high_spot, :].astype(f32) + arrived_ref[high_spot, :].astype(f32)
                    spot = pl.ds(at * part, part)
                    own_ref[spot, lanes] = jnp.where(flag, high, low)
                    sent_ref[spot, lanes] = jnp.where(flag, low, high).astype(bf16)

        outs = [((rows, sum(columns)), f32), ((rows, sum(columns)), bf16)]
        return whole_call(
            kernel, outs, "fold_both", scalars, first, first_arrived, second, second_arrived
        )

    def rows_block(rows, columns, at):
        return pl.BlockSpec((rows, columns), lambda i: (at, 0))

    def part_call(kernel, outs, name, scalars, parts, rest):
        return pl.pallas_call(
            kernel,
            grid=(1,),
            in_specs=[SCALARS]
            + [rows_block(rows, array.shape[1], at) for array, rows, at in parts]
            + [WHOLE] * len(rest),
            out_specs=[WHOLE] * len(outs),
            out_shape=[jax.ShapeDtypeStruct(shape, kind) for shape, kind in outs],
            name=name,
        )(scalars, *[array for array, _, _ in parts], *rest)

    def part_sum(scalars, kept, arrived, rows, at, pieces):
        columns, size = kept.shape[1], rows // pieces

        def kernel(scal, kept_ref, arrived_ref, *out_refs):
            for piece, ref in enumerate(out_refs):
                spot = pl.ds(piece * size, size)
                ref[...] = (
                    kept_ref[spot, :].astype(f32) + arrived_ref[spot, :].astype(f32)
                ).astype(bf16)

        return part_call(
            kernel, [((size, columns), bf16)] * pieces, "part_sum", scalars,
            [(kept, rows, at), (arrived, rows, at)], [],
        )

    def spread_rest(scalars, kept, arrived, far_x, far_l):
        rows, columns = kept.shape[0] // 4, kept.shape[1]
        half = rows // 2

        def kernel(scal, *refs):
            keeps, arrives = refs[:3], refs[3:6]
            far_x_ref, far_l_ref, own_ref, x_ref, l_ref = refs[6:]
            own_ref[...] = keeps[0][...].astype(f32) + arrives[0][...].astype(f32)
            to_x = keeps[1][...].astype(f32) + arrives[1][...].astype(f32)
            x_ref[:half, :] = to_x[:half].astype(bf16)
            x_ref[half:, :] = (to_x[half:] + far_l_ref[...].astype(f32)).astype(bf16)
            to_l = keeps[2][...].astype(f32) + arrives[2][...].astype(f32)
            l_ref[:half, :] = (to_l[:half] + far_x_ref[...].astype(f32)).astype(bf16)
            l_ref[half:, :] = to_l[half:].astype(bf16)

        outs = [((rows, columns), f32), ((rows, columns), bf16), ((rows, columns), bf16)]
        return part_call(
            kernel, outs, "spread_rest", scalars,
            [(array, rows, at) for array in (kept, arrived) for at in range(3)], [far_x, far_l],
        )

    def block_x_sum(scalars, kept, arrived, from_l):
        rows, columns = kept.shape[0] // 4, kept.shape[1]

        def kernel(scal, kept_ref, arrived_ref, from_ref, out_ref):
            out_ref[...] = (
                kept_ref[...].astype(f32)
                + arrived_ref[...].astype(f32)
                + from_ref[...].astype(f32)
            ).astype(bf16)

        return part_call(
            kernel, [((rows, columns), bf16)], "block_x_sum", scalars,
            [(kept, rows, 1), (arrived, rows, 1), (from_l, rows, 1)], [],
        )[0]

    def block_final(scalars, kept, arrived, from_l, hidden, from_x):
        rows, columns = hidden.shape

        def kernel(scal, kept_ref, arrived_ref, from_ref, hidden_ref, x_ref, out_ref):
            total = hidden_ref[...] + kept_ref[...].astype(f32) + arrived_ref[...].astype(f32)
            out_ref[...] = (total + from_ref[...].astype(f32) + x_ref[...].astype(f32)).astype(bf16)

        return part_call(
            kernel, [((rows, columns), bf16)], "block_final", scalars,
            [(kept, rows, 0), (arrived, rows, 0), (from_l, rows, 0)], [hidden, from_x],
        )[0]

    def give(total, scal, kept_ref, sent_ref):
        part = pair_bit * (total.shape[0] // dp_size)
        flag = is_high(scal, pair_bit)
        for at in range(total.shape[0] // (2 * part)):
            low = total[2 * at * part : (2 * at + 1) * part]
            high = total[(2 * at + 1) * part : (2 * at + 2) * part]
            kept_ref[pl.ds(at * part, part), :] = jnp.where(flag, high, low)
            sent_ref[pl.ds(at * part, part), :] = jnp.where(flag, low, high)

    def project(scalars, pair, core, pieces, bias, cosine, sine):
        tokens, model = 2 * pair.shape[0], pair.shape[1]
        columns = pieces[0][0].shape[1]
        width = columns - HD

        def kernel(scal, pair_ref, core_ref, bias_ref, cos_ref, sin_ref, *refs):
            query_ref, kv_ref, acts, held, sems = refs[dp_size:]
            wait_all(
                start_all(
                    attn_jobs(scal[0], refs[:dp_size], pieces, held)
                    + token_jobs(scal[1], pair_ref, core_ref, acts),
                    sems,
                )
            )
            is_value = jnp.bitwise_and(scal[1], 1) == 1
            rows = tokens // 4
            for at in range(4):
                spot = pl.ds(at * rows, rows)
                out = mm(acts[spot, :], held[...]) + bias_ref[...]
                cosine_rows, sine_rows = cos_ref[spot, :], sin_ref[spot, :]
                for head in range(width // HD):
                    query_ref[spot, head * HD : (head + 1) * HD] = turned(
                        out[:, head * HD : (head + 1) * HD], cosine_rows, sine_rows, 1.0
                    ).astype(bf16)
                kv = out[:, width:]
                kv_ref[spot, :] = jnp.where(
                    is_value, kv, turned(kv, cosine_rows, sine_rows, 1.0)
                ).astype(bf16)

        return pl.pallas_call(
            kernel,
            in_specs=[SCALARS, ANY, ANY, WHOLE, WHOLE, WHOLE] + [ANY] * dp_size,
            out_specs=[WHOLE, WHOLE],
            out_shape=[
                jax.ShapeDtypeStruct((tokens, width), bf16),
                jax.ShapeDtypeStruct((tokens, HD), bf16),
            ],
            scratch_shapes=[
                pltpu.VMEM((tokens, model), bf16),
                pltpu.VMEM((model, columns), bf16),
                pltpu.SemaphoreType.DMA((dp_size + 4,)),
            ],
            name="project",
        )(scalars, pair, core, bias, cosine, sine, *arrays_of(pieces))

    def probabilities(query, keys, start_rows, first):
        scores = mm_nt(query, keys) * (1.0 / math.sqrt(HD))
        column = lax.broadcasted_iota(jnp.int32, scores.shape, 1)
        row = lax.broadcasted_iota(jnp.int32, scores.shape, 0) + first
        allowed = (column <= row) & (column >= start_rows)
        scores = jnp.where(allowed, scores, masked_score)
        top = jnp.max(scores, axis=1, keepdims=True)
        raised = jnp.exp(scores - top)
        return raised * (1.0 / jnp.sum(raised, axis=1, keepdims=True))

    def attend(scalars, query, kv_own, kv_other, starts):
        tokens, width = query.shape
        rows = tokens // 4

        def kernel(scal, query_ref, own_ref, other_ref, start_ref, context_ref):
            is_value = jnp.bitwise_and(scal[1], 1) == 1
            own, other = own_ref[...], other_ref[...]
            keys = jnp.where(is_value, other, own)
            values = jnp.where(is_value, own, other)
            for at in range(4):
                end = (at + 1) * rows
                spot = pl.ds(at * rows, rows)
                for head in range(width // HD):
                    lanes = slice(head * HD, (head + 1) * HD)
                    probs = probabilities(
                        query_ref[spot, lanes], keys[:end], start_ref[spot, :], at * rows
                    )
                    context_ref[spot, lanes] = mm(probs.astype(bf16), values[:end]).astype(bf16)

        return whole_call(
            kernel, [((tokens, width), bf16)], "attend", scalars, query, kv_own, kv_other, starts
        )[0]

    def out_rows(scalars, context, pieces, model):
        tokens, width = context.shape
        rows = tokens // 4

        def kernel(scal, context_ref, *refs):
            kept_ref, sent_ref, held, part, sems, out_sems = refs[dp_size:]
            wait_all(start_all(attn_jobs(scal[0], refs[:dp_size], pieces, held), sems))
            jobs = back(token_jobs(scal[1], kept_ref, sent_ref, part))
            copies = made(jobs, out_sems)
            for at in (2, 3, 0, 1):
                mask = (0, 2, 1, 3)[at]
                spot = jnp.bitwise_xor(scal[1], mask)
                spot = pl.ds(pl.multiple_of(spot * rows, rows), rows)
                part[spot, :] = mm_nt(context_ref[spot, :], held[...]).astype(bf16)
                copies[at].start()
            wait_all(copies)

        half = jax.ShapeDtypeStruct((tokens // 2, model), bf16)
        return pl.pallas_call(
            kernel,
            in_specs=[SCALARS, WHOLE] + [ANY] * dp_size,
            out_specs=[ANY, ANY],
            out_shape=[half, half],
            scratch_shapes=[
                pltpu.VMEM((model, width), bf16),
                pltpu.VMEM((tokens, model), bf16),
                pltpu.SemaphoreType.DMA((dp_size,)),
                pltpu.SemaphoreType.DMA((4,)),
            ],
            name="out_rows",
        )(scalars, context, *arrays_of(pieces))

    def attend_back(
        scalars, query, kv_own, kv_other, starts, pieces, attn, context, cosine, sine
    ):
        tokens, width = query.shape
        model = attn[0].shape[1]
        rows = tokens // 4
        scale = 1.0 / math.sqrt(HD)

        def kernel(
            scal, query_ref, own_ref, other_ref, start_ref, attn_a, attn_b, attn_c, attn_d,
            context_ref, cos_ref, sin_ref, *refs,
        ):
            grad_query_ref, kv_kept_ref, kv_sent_ref, bias_ref, wout_ref, wout_sent_ref = refs[
                dp_size : dp_size + 6
            ]
            held, grads, grad_context, grad_key, grad_value, sems = refs[dp_size + 6 :]
            wait_all(
                start_all(
                    attn_jobs(scal[0], refs[:dp_size], pieces, held)
                    + quarter_jobs(scal[1], (attn_a, attn_b, attn_c, attn_d), grads),
                    sems,
                )
            )
            is_value = jnp.bitwise_and(scal[1], 1) == 1
            own, other = own_ref[...], other_ref[...]
            keys = jnp.where(is_value, other, own)
            values = jnp.where(is_value, own, other)
            for at in range(2):
                spot = pl.ds(at * 2 * rows, 2 * rows)
                grad_context[spot, :] = mm(grads[spot, :], held[...]).astype(bf16)
            give(mm_tn(grads[...], context_ref[...]).astype(bf16), scal, wout_ref, wout_sent_ref)
            grad_key[...] = jnp.zeros_like(grad_key)
            grad_value[...] = jnp.zeros_like(grad_value)
            bias_ref[...] = jnp.zeros_like(bias_ref)
            for at in range(4):
                end = (at + 1) * rows
                spot = pl.ds(at * rows, rows)
                upto = pl.ds(0, end)
                for head in range(width // HD):
                    lanes = slice(head * HD, (head + 1) * HD)
                    queries = query_ref[spot, lanes]
                    given = grad_context[spot, lanes]
                    probs = probabilities(queries, keys[:end], start_ref[spot, :], at * rows)
                    low = probs.astype(bf16)
                    grad_probs = mm_nt(given, values[:end])
                    delta = jnp.sum(low.astype(f32) * grad_probs, axis=1, keepdims=True)
                    grad_scores = (probs * (grad_probs - delta)).astype(bf16)
                    grad_query = turned(
                        mm(grad_scores, keys[:end]) * scale, cos_ref[spot, :], sin_ref[spot, :], -1.0
                    )
                    grad_query_ref[spot, lanes] = grad_query.astype(bf16)
                    bias_ref[0:1, lanes] += jnp.sum(grad_query, axis=0, keepdims=True)
                    grad_key[upto, :] += mm_tn(grad_scores, queries)
                    grad_value[upto, :] += mm_tn(low, given)
            grad_keys = turned(grad_key[...] * scale, cos_ref[...], sin_ref[...], -1.0)
            grad_values = grad_value[...]
            bias_ref[0:1, width : width + HD] = jnp.sum(grad_keys, axis=0, keepdims=True)
            bias_ref[0:1, width + HD :] = jnp.sum(grad_values, axis=0, keepdims=True)
            kv_kept_ref[...] = jnp.where(is_value, grad_values, grad_keys)
            kv_sent_ref[...] = jnp.where(is_value, grad_keys, grad_values).astype(bf16)

        return pl.pallas_call(
            kernel,
            in_specs=[SCALARS] + [WHOLE] * 4 + [ANY] * 4 + [WHOLE] * 3 + [ANY] * dp_size,
            out_specs=[WHOLE] * 6,
            out_shape=[
                jax.ShapeDtypeStruct((tokens, width), bf16),
                jax.ShapeDtypeStruct((tokens, HD), f32),
                jax.ShapeDtypeStruct((tokens, HD), bf16),
                jax.ShapeDtypeStruct((8, width + 2 * HD), f32),
                jax.ShapeDtypeStruct((model // 2, width), bf16),
                jax.ShapeDtypeStruct((model // 2, width), bf16),
            ],
            scratch_shapes=[
                pltpu.VMEM((model, width), bf16),
                pltpu.VMEM((tokens, model), bf16),
                pltpu.VMEM((tokens, width), bf16),
                pltpu.VMEM((tokens, HD), f32),
                pltpu.VMEM((tokens, HD), f32),
                pltpu.SemaphoreType.DMA((dp_size + 4,)),
            ],
            name="attend_back",
        )(
            scalars, query, kv_own, kv_other, starts, *attn, context, cosine, sine,
            *arrays_of(pieces),
        )

    def project_back(scalars, grad_query, kv_kept, kv_arrived, pieces):
        tokens, width = grad_query.shape
        columns = pieces[0][0].shape[1]
        model = dp_size * shard_rows(pieces)
        rows = tokens // 4

        def kernel(scal, query_ref, kept_kv_ref, arrived_ref, *refs):
            grads_ref, kept_ref, sent_ref, held, part, sems, out_sems = refs[dp_size:]
            copies = start_all(attn_jobs(scal[0], refs[:dp_size], pieces, held), sems)
            grads_ref[:, :width] = query_ref[...]
            grads_ref[:, width:] = (kept_kv_ref[...] + arrived_ref[...].astype(f32)).astype(bf16)
            wait_all(copies)
            jobs = back(token_jobs(scal[1], kept_ref, sent_ref, part))
            copies = made(jobs, out_sems)
            for at in (2, 3, 0, 1):
                mask = (0, 2, 1, 3)[at]
                spot = jnp.bitwise_xor(scal[1], mask)
                spot = pl.ds(pl.multiple_of(spot * rows, rows), rows)
                part[spot, :] = mm_nt(grads_ref[spot, :], held[...]).astype(bf16)
                copies[at].start()
            wait_all(copies)

        half = jax.ShapeDtypeStruct((tokens // 2, model), bf16)
        return pl.pallas_call(
            kernel,
            in_specs=[SCALARS, WHOLE, WHOLE, WHOLE] + [ANY] * dp_size,
            out_specs=[WHOLE, ANY, ANY],
            out_shape=[jax.ShapeDtypeStruct((tokens, columns), bf16), half, half],
            scratch_shapes=[
                pltpu.VMEM((model, columns), bf16),
                pltpu.VMEM((tokens, model), bf16),
                pltpu.SemaphoreType.DMA((dp_size,)),
                pltpu.SemaphoreType.DMA((4,)),
            ],
            name="project_back",
        )(scalars, grad_query, kv_kept, kv_arrived, *arrays_of(pieces))

    def shard_rows(pieces):
        return min(piece[0].shape[0] for piece in pieces)

    def gain_rows_of(scalars, kept, sent, pair, core):
        rows, model = kept.shape[0] // 4, kept.shape[1]

        def kernel(scal, kept_ref, sent_ref, pair_ref, core_ref, gain_ref):
            @pl.when(pl.program_id(0) == 0)
            def _():
                gain_ref[...] = jnp.zeros_like(gain_ref)

            total = kept_ref[...].astype(f32) * pair_ref[...].astype(f32)
            total = total + sent_ref[...].astype(f32) * core_ref[...].astype(f32)
            gain_ref[0:1, :] += jnp.sum(total, axis=0, keepdims=True)

        return pl.pallas_call(
            kernel,
            grid=(4,),
            in_specs=[SCALARS] + [pl.BlockSpec((rows, model), lambda i: (i, 0))] * 4,
            out_specs=pl.BlockSpec((8, model), lambda i: (0, 0)),
            out_shape=jax.ShapeDtypeStruct((8, model), f32),
            name="gain_rows",
        )(scalars, kept, sent, pair, core)

    def project_grad(scalars, pair, core, grads):
        tokens, columns = grads.shape
        model = pair.shape[1]

        def kernel(scal, pair_ref, core_ref, grads_ref, kept_ref, sent_ref, acts, sems):
            wait_all(start_all(token_jobs(scal[1], pair_ref, core_ref, acts), sems))
            give(mm_tn(acts[...], grads_ref[...]).astype(bf16), scal, kept_ref, sent_ref)

        return pl.pallas_call(
            kernel,
            in_specs=[SCALARS, ANY, ANY, WHOLE],
            out_specs=[WHOLE] * 2,
            out_shape=[jax.ShapeDtypeStruct((model // 2, columns), bf16)] * 2,
            scratch_shapes=[
                pltpu.VMEM((tokens, model), bf16),
                pltpu.SemaphoreType.DMA((4,)),
            ],
            name="project_grad",
        )(scalars, pair, core, grads)

    def norm_two_back(scalars, own, from_x, from_l, hidden, gain, given):
        rows, model = own.shape

        def kernel(scal, own_ref, x_ref, l_ref, hidden_ref, gain_ref, given_ref, out_ref, low_ref, sum_ref):
            grad_out = own_ref[...] + x_ref[...].astype(f32) + l_ref[...].astype(f32)
            normed, row_scale = norm_forward(hidden_ref[...])
            grad_normed = grad_out * gain_ref[...]
            grad_in = row_scale * (
                grad_normed - normed * jnp.mean(grad_normed * normed, axis=-1, keepdims=True)
            )
            total = given_ref[...].astype(f32) + grad_in
            out_ref[...] = total
            low_ref[...] = total.astype(bf16)
            sum_ref[0:1, :] = jnp.sum(grad_out * normed, axis=0, keepdims=True)

        outs = [((rows, model), f32), ((rows, model), bf16), ((8, model), f32)]
        return whole_call(
            kernel, outs, "norm_two_back", scalars, own, from_x, from_l, hidden, gain, given
        )

    def local(
        block_input,
        segment_ids,
        gain_attn,
        w_query,
        b_query,
        w_keyval,
        b_keyval,
        w_out,
        gain_ffn,
        w_gate,
        w_up,
        w_down,
        cotangent,
    ):
        dp_index = lax.axis_index("dp")
        tensor_index = lax.axis_index("tensor")
        scalars = jnp.stack([dp_index, tensor_index]).astype(jnp.int32)
        local_heads = b_query.shape[0] // HD
        head_kv = tensor_index * local_heads // (HQ // KV)
        is_value = tensor_index % 2
        kv_column = is_value * (KV * HD) + head_kv * HD
        width = local_heads * HD

        groups = dp_size // 4

        def far_rest(kept, sent):
            arrived = swap(sent, "dp", far_bits[0])
            for bit in far_bits[1:]:
                kept, sent = fold_sum(scalars, kept, arrived, bit, 1)
                arrived = swap(sent, "dp", bit)
            return kept, arrived

        keyval_cols = lax.dynamic_slice_in_dim(w_keyval, kv_column, HD, 1)
        qkv_own = jnp.concatenate([w_query, keyval_cols], axis=1)
        shard = qkv_own.shape[0]
        qkv_far = far_pieces(qkv_own)
        qkv_l = swap(qkv_own, "dp", pair_bit)
        qkv_y = swap(qkv_own, "dp", 1)
        rows_float = block_input.astype(f32)
        normed_one, scale_one = norm_forward(rows_float)
        act_own = (normed_one * gain_attn).astype(bf16)
        act_x = swap(act_own, "tensor", 2)
        gate_mine, gate_sent = split_cols(scalars, w_gate)
        gate_theirs = swap(gate_sent, "dp", pair_bit)

        qkv_far_in, qkv_l, qkv_y, out_own, w_up_in, w_down_in, segments = hold(
            [gate_sent, act_own],
            [tuple(qkv_far[1:]), qkv_l, qkv_y, w_out.T, w_up, w_down, segment_ids],
        )
        far_rows = rows_of(*qkv_far_in)
        qkv_y2 = swap(rows_of(qkv_l, far_rows), "dp", 1)
        qkv_l2 = swap(far_rows, "dp", pair_bit)
        out_far = far_pieces(out_own)
        rest_mine, rest_sent = split_cols(scalars, w_up_in, w_down_in.T)
        positions = positions_of(segments[0])
        cosine, sine = rotary(positions)
        sine = jnp.where(jnp.arange(HD)[None, :] < HD // 2, -sine, sine)
        starts = (jnp.arange(positions.shape[0], dtype=jnp.int32) - positions)[:, None]
        qkv_bias = jnp.concatenate([b_query, lax.dynamic_slice_in_dim(b_keyval, kv_column, HD, 0)])[
            None, :
        ]

        qkv_y2, qkv_l2, act_pair, gate_theirs, out_half, cosine, sine, starts, rest_sent, cot_own = (
            hold(
                [],
                [
                    qkv_y2,
                    qkv_l2,
                    rows_of(act_own, act_x),
                    gate_theirs,
                    rows_of(*out_far),
                    cosine,
                    sine,
                    starts,
                    rest_sent,
                    cotangent,
                ],
            )
        )

        def gather_attn():
            return (
                swap(qkv_l2, "dp", 1),
                swap(act_pair, "tensor", 1),
                swap(out_half, "dp", pair_bit),
                join_rows(scalars, gate_mine, gate_theirs, 0, 1),
            )

        qkv_y3, act_c, out_l, gate_piece = section(gather_attn)

        qkv_y3, act_c, out_near, rest_sent, cot_core, gate_piece = hold(
            [], [qkv_y3, act_c, rows_of(out_half, out_l), rest_sent, cotangent, gate_piece]
        )
        gate_far = far_pieces(gate_piece)
        cot_x = swap(cot_core, "tensor", 2)
        rest_theirs = swap(rest_sent, "dp", pair_bit)
        out_y = swap(out_near, "dp", 1)
        far_masks = masks_of(far_bits)
        qkv_pieces = [(part, 0, mask) for part, mask in zip(qkv_far, far_masks)]
        qkv_pieces += [(qkv_l, 0, pair_bit), (qkv_y, 0, 1), (qkv_y2, 0, pair_bit ^ 1)]
        for at, mask in enumerate(far_masks[1:]):
            qkv_pieces += [
                (qkv_y2, (at + 1) * shard, mask ^ 1),
                (qkv_l2, at * shard, mask ^ pair_bit),
                (qkv_y3, at * shard, mask ^ pair_bit ^ 1),
            ]

        def attention():
            query_rot, kv_own = project(
                scalars, act_pair, act_c, qkv_pieces, qkv_bias, cosine, sine
            )
            kv_other = swap(kv_own, "tensor", 1)
            kv_other, cot_given = hold([], [kv_other, cot_core])
            cot_own_c = swap(cot_given, "tensor", 1)
            context = attend(scalars, query_rot, kv_own, kv_other, starts)
            context, cot_own_c = hold([], [context, cot_own_c])
            return query_rot, kv_own, kv_other, context, cot_own_c

        def out_pieces(near, far):
            pieces = []
            masks = masks_of(far_bits + [pair_bit])
            for at, mask in enumerate(masks):
                pieces += [(near, at * shard, mask), (far, at * shard, mask ^ 1)]
            return pieces

        query_rot, kv_own, kv_other, context, cot_own_c = section(attention)
        context, out_y = hold([], [context, out_y])
        out_parts = out_pieces(out_near, out_y)
        attn_kept, attn_sent = out_rows(scalars, context, out_parts, act_pair.shape[1])

        attn_sent, rest_theirs, cot_own_l = hold([cot_x], [attn_sent, rest_theirs, cotangent])

        def sum_cores():
            arrived = swap(attn_sent, "tensor", 1)
            return arrived, join_both(scalars, gate_piece, rest_mine, rest_theirs)

        attn_arrived, (up_piece, own_both) = section(sum_cores)
        attn_arrived, up_piece, own_both = hold([], [attn_arrived, up_piece, own_both])
        up_far = far_pieces(up_piece)
        own_y = swap(own_both, "dp", 1)
        cot_l = swap(cot_own_l, "dp", pair_bit)

        def sum_heads():
            (sent,) = part_sum(scalars, attn_kept, attn_arrived, block_input.shape[0], 1, 1)
            return norm_two(
                scalars, block_input, attn_kept, attn_arrived, swap(sent, "tensor", 2),
                gain_ffn[None, :],
            )

        hidden, two_own = section(sum_heads)

        two_own, gate_halves = hold([cot_l], [two_own, tuple(gate_far[1:])])
        gate_y2 = [swap(part, "dp", 1) for part in gate_halves]

        def gather_near():
            two_x = swap(two_own, "tensor", 2)
            two_l = swap(two_own, "dp", pair_bit)
            return two_x, two_l, join_rows(scalars, rest_mine, rest_theirs, 1, 2)

        two_x, two_l, down_piece = section(gather_near)

        rows = two_own.shape[0]
        two_x, two_l, up_halves = hold([own_y, gate_y2], [two_x, two_l, tuple(up_far[1:])])
        up_y2 = [swap(part, "dp", 1) for part in up_halves]

        def gather_rest():
            given_a, given_b = halves(scalars, two_l, two_x)
            far_a = swap(given_a, "tensor", 2)
            far_b = swap(given_b, "dp", pair_bit)

            def cores():
                given, arrived = [two_x, two_l, two_own], []
                for at in range(3):
                    part = swap(given[at], "tensor", 1)
                    part, *given = hold([], [part] + given)
                    arrived.append(part)
                return arrived

            arrived = section(cores)
            return hold([], [far_a, far_b, *arrived])

        far_a, far_b, two_x_c, two_l_c, two_own_c = section(gather_rest)
        far_a, far_b, down_piece = hold([], [far_a, far_b, down_piece])
        down_far = far_pieces(down_piece)

        def gather_far():
            return swap(far_a, "tensor", 1), swap(far_b, "tensor", 1)

        far_a_c, far_b_c = section(gather_far)
        two_pieces = [two_own, two_x, two_l]
        two_pieces_c = [two_own_c, two_x_c, two_l_c]

        size = gate_piece.shape[0]
        gate_pieces = [(part, 0) for part in [*gate_far]] + [
            (part, 0) for part in [own_y, *gate_y2]
        ]
        far_a, far_b, far_a_c, far_b_c, down_piece_y, cot_x, cot_l, up_y2 = hold(
            [], [far_a, far_b, far_a_c, far_b_c, down_piece, cot_x, cot_l, tuple(up_y2)]
        )
        up_pieces = [(part, 0) for part in [*up_far]] + [(own_y, size)] + [
            (part, 0) for part in up_y2
        ]
        two_pieces += [far_a, far_b]
        two_pieces_c += [far_a_c, far_b_c]

        def feed_own():
            down_y1 = swap(down_piece_y, "dp", 1)
            cot_far = swap(cot_l, "tensor", 2)
            x_c = swap(cot_x, "tensor", 1)
            own = ffn_up(scalars, two_pieces, gate_pieces, up_pieces)
            down_y1, cot_far, x_c = hold([own], [down_y1, cot_far, x_c])
            return down_y1, cot_far, x_c, own

        down_y1, cot_far, cot_x_c, (acts_a, mixed_a, silu_a, back_a) = section(feed_own)

        mixed_a, cot_l_in = hold([], [mixed_a, cot_l])

        def feed_core():
            l_c = swap(cot_l_in, "tensor", 1)
            far_c = swap(cot_far, "tensor", 1)
            core = ffn_up(scalars, two_pieces_c, gate_pieces, up_pieces)
            l_c, far_c = hold([core], [l_c, far_c])
            return l_c, far_c, core

        cot_l_c, cot_far_c, (acts_b, mixed_b, silu_b, back_b) = section(feed_core)

        cots = [cotangent, cot_x, cot_l, cot_far]
        cots_c = [cot_own_c, cot_x_c, cot_l_c, cot_far_c]
        mixed_b, down_halves = hold([down_y1], [mixed_b, tuple(down_far[1:])])
        down_y2 = tuple(swap(part, "dp", 1) for part in down_halves)
        down_kept, down_sent = section(
            lambda: ffn_grad(scalars, cots, cots_c, mixed_a, mixed_b, "grad_down")
        )
        down_sent, down_y2 = hold([], [down_sent, down_y2])
        down_pieces = [(part, 0) for part in [*down_far, down_y1, *down_y2]]

        down_sent, silu_b = hold([], [down_sent, silu_b])
        down_sent = swap(down_sent, "dp", 1)

        def back_all():
            gate_b, up_b, two_sent = ffn_back(
                scalars, cots_c, down_pieces, gate_pieces, up_pieces, silu_b, back_b
            )
            (two_sent,) = hold([], [two_sent])
            arrived = swap(two_sent, "tensor", 1)
            gate_a, up_a, kept = ffn_back(
                scalars, cots, down_pieces, gate_pieces, up_pieces, silu_a, back_a
            )
            (kept,) = hold([], [kept])
            far = part_sum(scalars, kept, arrived, kept.shape[0] // 4, 3, 2)
            return gate_a, up_a, gate_b, up_b, kept, arrived, *far

        gate_a, up_a, gate_b, up_b, two_kept, two_arrived, far_a, far_b = section(back_all)

        far_a, far_b, mixed_b = hold([], [far_a, far_b, mixed_b])
        model = far_a.shape[1]

        def spread_far():
            far_x = swap(far_a, "tensor", 2)
            far_l = swap(far_b, "dp", pair_bit)

            def block_rows():
                sent = ffn_rows(scalars, mixed_b, down_pieces, model, "block_rows")
                (sent,) = hold([], [sent])
                arrived = swap(sent, "tensor", 1)
                kept = ffn_rows(scalars, mixed_a, down_pieces, model, "block_rows")
                return hold([], [kept, arrived])

            outs = section(block_rows)
            outs, far_x, far_l = hold([], [outs, far_x, far_l])
            return (*outs, *spread_rest(scalars, two_kept, two_arrived, far_x, far_l))

        block_kept, block_arrived, own, to_x, to_l = section(spread_far)

        to_x, to_l, down_sent = hold([], [to_x, to_l, down_sent])

        def spread_near():
            from_x = swap(to_x, "tensor", 2)
            from_l = swap(to_l, "dp", pair_bit)
            up_grads = ffn_grad(scalars, [acts_a], [acts_b], up_a, up_b, "grad_up")
            down_pair = fold_sum(scalars, down_kept, down_sent, far_bits[0], 1)
            block_rows = 2 * own.shape[0]
            block_pair = part_sum(scalars, block_kept, block_arrived, block_rows, 1, 1)
            from_x, from_l = hold([up_grads, down_pair, block_pair], [from_x, from_l])
            return (
                *up_grads,
                *down_pair,
                *block_pair,
                *norm_two_back(
                    scalars, own, from_x, from_l, hidden, gain_ffn[None, :], cotangent
                ),
            )

        (
            up_kept, up_sent, down_kept, down_sent, block_sent, grad_hidden, attn_own, gain_two,
        ) = section(spread_near)

        attn_own, down_sent, up_sent, gate_b, block_sent = hold(
            [], [attn_own, down_sent, up_sent, gate_b, block_sent]
        )
        down_kept, down_sent = far_rest(down_kept, down_sent)
        up_sent = swap(up_sent, "dp", 1)
        block_from_l = swap(block_sent, "dp", pair_bit)

        def attention_back():
            def gather_back():
                attn_x = swap(attn_own, "tensor", 2)
                own_c = swap(attn_own, "tensor", 1)
                gate_grads = ffn_grad(scalars, [acts_a], [acts_b], gate_a, gate_b, "grad_gate")
                attn_x, own_c = hold([gate_grads], [attn_x, own_c])
                return (attn_x, own_c, *gate_grads)

            attn_x, own_c, gate_kept, gate_sent = section(gather_back)
            attn_x, own_c, gate_sent = hold([], [attn_x, own_c, gate_sent])
            x_c = swap(attn_x, "tensor", 1)
            outs = attend_back(
                scalars, query_rot, kv_own, kv_other, starts, out_parts,
                [attn_own, attn_x, own_c, x_c], context, cosine, sine,
            )
            return gate_kept, gate_sent, outs

        gate_kept, gate_sent, outs = section(attention_back)
        grad_query_low, kv_kept, kv_given, bias_rows, wout_kept, wout_sent = outs

        kv_given, up_sent = hold([], [kv_given, up_sent])

        def pass_keys():
            kv_arrived = swap(kv_given, "tensor", 1)
            up_pair = fold_sum(scalars, up_kept, up_sent, far_bits[0], 1)
            (kv_arrived,) = hold([up_pair], [kv_arrived])
            return kv_arrived, *up_pair

        kv_arrived, up_own, up_given = section(pass_keys)
        kv_arrived, up_given, wout_sent, gate_sent, down_sent, block_from_l = hold(
            [], [kv_arrived, up_given, wout_sent, gate_sent, down_sent, block_from_l]
        )
        wout_arrived = swap(wout_sent, "dp", pair_bit)
        devices = dp_size * tensor_size

        def input_grads():
            kv_in, gate_in, up_in = hold([], [kv_arrived, gate_sent, up_given])
            gate_y = swap(gate_in, "dp", 1)
            up_sum, up_far_sum = far_rest(up_own, up_in)

            def project_all():
                grad_qkv, one_kept, one_sent = project_back(
                    scalars, grad_query_low, kv_kept, kv_in, qkv_pieces
                )
                one_sent, grad_qkv = hold([], [one_sent, grad_qkv])
                arrived = swap(one_sent, "tensor", 1)
                wqkv_pair = project_grad(scalars, act_pair, act_c, grad_qkv)
                (arrived,) = hold([wqkv_pair], [arrived])
                wqkv_kept, wqkv_sent = wqkv_pair
                one_partner = one_sent
                (one_given,) = part_sum(scalars, one_kept, arrived, block_input.shape[0], 1, 1)
                one_arrived = arrived

                def first_norm_back():
                    arrived = swap(one_given, "tensor", 2)
                    wqkv_arrived = swap(wqkv_sent, "dp", pair_bit)
                    block = block_x_sum(scalars, block_kept, block_arrived, block_from_l)
                    down_pair = fold_sum(scalars, down_kept, down_sent, pair_bit, 1)
                    gain_rows = gain_rows_of(scalars, one_kept, one_partner, act_pair, act_c)
                    bias_keyval = jnp.zeros((2 * KV * HD,), f32)
                    bias_keyval = lax.dynamic_update_slice_in_dim(
                        bias_keyval, bias_rows[0, width : width + HD], head_kv * HD, 0
                    )
                    bias_keyval = lax.dynamic_update_slice_in_dim(
                        bias_keyval, bias_rows[0, width + HD :], KV * HD + head_kv * HD, 0
                    )
                    bias_query = lax.dynamic_update_slice_in_dim(
                        jnp.zeros((HQ * HD,), f32), bias_rows[0, :width], tensor_index * width, 0
                    )
                    parts = (gain_rows[0] / gain_attn, gain_two[0], bias_query, bias_keyval)
                    small = jnp.concatenate([part.reshape(devices, -1) for part in parts], axis=1)
                    (arrived,) = hold([block, small, down_pair], [arrived])
                    grad_rows = norm_one_back(
                        scalars, block_input, one_kept, one_arrived, arrived, gain_attn[None, :],
                        grad_hidden,
                    )
                    (wqkv_arrived,) = hold([grad_rows], [wqkv_arrived])
                    return (*down_pair, wqkv_kept, grad_rows, small, block, wqkv_arrived)

                return section(first_norm_back)

            outs = section(project_all)
            outs, gate_y, up_far_sum = hold([], [outs, gate_y, up_far_sum])
            return (up_sum, up_far_sum, gate_y, *outs)

        (
            up_kept, up_sent, gate_sent, down_mine, down_given, wqkv_kept, grad_rows, small,
            block_to_x, wqkv_arrived,
        ) = section(input_grads)

        wqkv_arrived, wout_arrived, gate_sent, small, down_given = hold(
            [], [wqkv_arrived, wout_arrived, gate_sent, small, down_given]
        )
        gate_kept, gate_sent = fold_sum(scalars, gate_kept, gate_sent, far_bits[0], 1)
        wqkv_arrived, gate_sent, small = hold([], [wqkv_arrived, gate_sent, small])
        gate_kept, gate_sent = far_rest(gate_kept, gate_sent)
        small = lax.all_to_all(small, ("dp", "tensor"), 0, 0, tiled=True)

        def last_rows():
            block_x = swap(block_to_x, "tensor", 2)
            down_theirs = swap(down_given, "dp", pair_bit)

            def attn_step():
                own, sent = fold_both(
                    scalars, wqkv_kept, wqkv_arrived, wout_kept, wout_arrived, 1, groups
                )
                arrived = swap(sent, "dp", 1)
                up_pair = fold_sum(scalars, up_kept, up_sent, pair_bit, 1)
                (arrived,) = hold([up_pair], [arrived])
                return (*fold_sum(scalars, own, arrived, far_bits[0], 1), *up_pair)

            *attn_outs, block_x, down_theirs = hold(
                [], [*section(attn_step), block_x, down_theirs]
            )
            block_out = block_final(
                scalars, block_kept, block_arrived, block_from_l, hidden, block_x
            )
            down_share = join_cols(scalars, down_mine, down_theirs, w_down.shape[0] // 2).T
            return *attn_outs, block_out, down_share

        attn_kept, attn_sent, up_mine, up_given, block_out, down_share = section(last_rows)

        gate_sent, attn_sent, up_given, small = hold(
            [block_out, down_share], [gate_sent, attn_sent, up_given, small]
        )
        attn_kept, attn_sent = far_rest(attn_kept, attn_sent)
        up_theirs = swap(up_given, "dp", pair_bit)
        gate_mine, gate_given = fold_sum(scalars, gate_kept, gate_sent, pair_bit, 1)
        gate_theirs = swap(gate_given, "dp", pair_bit)
        small = jnp.sum(small, axis=0)
        up_theirs = hold([gate_given, small], [up_theirs])[0]
        up_share = join_cols(scalars, up_mine, up_theirs, w_up.shape[1] // 2)
        (attn_sent,) = hold([up_share], [attn_sent])
        share = add(attn_kept, attn_sent)
        kv_rows = share[:, width : width + HD]
        share_rows = kv_rows.shape[0] // tensor_size
        moved = []
        for mask in range(tensor_size):
            rows_for = lax.dynamic_slice_in_dim(
                kv_rows, (tensor_index ^ mask) * share_rows, share_rows, 0
            )
            moved.append(swap(rows_for, "tensor", mask) if mask else rows_for)
        query_share, out_share = share[:, :width], share[:, width + HD :].T
        gate_theirs, *moved = hold([query_share, out_share], [gate_theirs] + moved)
        gate_share = join_cols(scalars, gate_mine, gate_theirs, w_gate.shape[1] // 2)
        keyval_share = jnp.zeros((share_rows, 2 * KV * HD), f32)
        for mask in range(tensor_size):
            sender = tensor_index ^ mask
            column = (sender % 2) * (KV * HD) + (sender * local_heads // (HQ // KV)) * HD
            keyval_share = lax.dynamic_update_slice_in_dim(keyval_share, moved[mask], column, 1)
        sizes = [HQ * HD // devices, 2 * KV * HD // devices, gain_attn.shape[0] // devices]
        ends = [sizes[2], 2 * sizes[2], 2 * sizes[2] + sizes[0]]
        gain_one_share = small[: ends[0]]
        gain_two_share = small[ends[0] : ends[1]]
        query_bias_share = small[ends[1] : ends[2]]
        keyval_bias_share = small[ends[2] :]
        return (
            block_out,
            grad_rows,
            gain_one_share,
            query_share,
            query_bias_share,
            keyval_share,
            keyval_bias_share,
            out_share,
            gain_two_share,
            gate_share,
            up_share,
            down_share,
        )

    placed = (
        P(("dp", "tensor"), None),
        P("dp", None),
        P(),
        P("dp", "tensor"),
        P("tensor"),
        P("dp", None),
        P(),
        P("tensor", "dp"),
        P(),
        P("dp", "tensor"),
        P("dp", "tensor"),
        P("tensor", "dp"),
        P(("dp", "tensor"), None),
    )
    return jax.shard_map(
        local,
        mesh=mesh,
        in_specs=placed,
        out_specs=(
            P(("dp", "tensor"), None),
            P(("dp", "tensor"), None),
            P(("dp", "tensor")),
            P("dp", "tensor"),
            P(("dp", "tensor")),
            P(("dp", "tensor"), None),
            P(("dp", "tensor")),
            P("tensor", "dp"),
            P(("dp", "tensor")),
            P("dp", "tensor"),
            P("dp", "tensor"),
            P("tensor", "dp"),
        ),
        check_vma=False,
    )
```

```python
import math

import jax
import jax.numpy as jnp
from jax import lax
from jax.experimental import pallas as pl
from jax.experimental.pallas import tpu as pltpu
from jax.sharding import PartitionSpec as P

HQ = 12
KV = 2
HD = 128


epsilon = 1e-06
rope_base = 1000000.0
masked_score = -1e30
bf16 = jnp.bfloat16
f32 = jnp.float32


def positions_of(segment_row):
    index_row = jnp.arange(segment_row.shape[0], dtype=jnp.int32)
    starts = jnp.concatenate(
        [jnp.ones((1,), jnp.int32), (segment_row[1:] != segment_row[:-1]).astype(jnp.int32)]
    )
    first_index = lax.cummax(jnp.where(starts > 0, index_row, 0), axis=0)
    return index_row - first_index


def rotary(positions):
    inverse = rope_base ** (-(jnp.arange(HD // 2, dtype=jnp.float32) * 2.0 / HD))
    angles = positions.astype(jnp.float32)[:, None] * inverse[None, :]
    angles = jnp.concatenate([angles, angles], axis=1)
    return (jnp.cos(angles), jnp.sin(angles))


def norm_forward(values_in):
    row_scale = lax.rsqrt(jnp.mean(values_in * values_in, axis=-1, keepdims=True) + epsilon)
    return (values_in * row_scale, row_scale)


def norm_backward(grad_out, normed, row_scale, gain_vec):
    grad_normed = grad_out * gain_vec
    grad_in = row_scale * (
        grad_normed - normed * jnp.mean(grad_normed * normed, axis=-1, keepdims=True)
    )
    return (grad_in, jnp.sum(grad_out * normed, axis=0))


ANY = pl.BlockSpec(memory_space=pl.ANY)
WHOLE = pl.BlockSpec(memory_space=pltpu.VMEM)
SCALARS = pl.BlockSpec(memory_space=pltpu.SMEM)


def made(jobs, sems, first=0):
    return [
        pltpu.make_async_copy(src, dst, sems.at[first + at]) for at, (src, dst) in enumerate(jobs)
    ]


def start_all(jobs, sems):
    copies = made(jobs, sems)
    for copy in copies:
        copy.start()
    return copies


def wait_all(copies):
    for copy in copies:
        copy.wait()


def block(ref, at, rows):
    return ref.at[pl.ds(pl.multiple_of(at * rows, rows), rows)]


def turned(values, cosine, sine, sign):
    return values * cosine + sign * (pltpu.roll(values, HD // 2, 1) * sine)


def mm(left, right):
    return lax.dot_general(left, right, (((1,), (0,)), ((), ())), preferred_element_type=f32)


def mm_nt(left, right):
    return lax.dot_general(left, right, (((1,), (1,)), ((), ())), preferred_element_type=f32)


def mm_tn(left, right):
    return lax.dot_general(left, right, (((0,), (0,)), ((), ())), preferred_element_type=f32)


def hold(due, release):
    out = lax.optimization_barrier((tuple(due), tuple(release)))
    return out[1]


def section(body):
    outs = jax.eval_shape(body)
    return lax.cond(
        lax.optimization_barrier(jnp.bool_(True)),
        body,
        lambda: jax.tree.map(lambda out: jnp.zeros(out.shape, out.dtype), outs),
    )


def solution(mesh):
    dp_size = mesh.shape["dp"]
    tensor_size = mesh.shape["tensor"]
    pair_bit = 2
    far_bits = []
    bit = dp_size // 2
    while bit > pair_bit:
        far_bits.append(bit)
        bit //= 2
    ring_bits = far_bits + [1]

    def swap(array, axis, bit):
        size = mesh.shape[axis]
        with jax.named_scope(f"swap_{axis}_{bit}"):
            return lax.ppermute(array, axis, [(i, i ^ bit) for i in range(size)])

    def masks_of(bits):
        masks = [0]
        for bit in bits:
            masks = masks + [mask ^ bit for mask in masks]
        return masks

    def rows_of(*pieces):
        return jnp.concatenate(pieces, axis=0)

    def far_pieces(piece):
        pieces = [piece]
        for bit in far_bits:
            pieces = pieces + [swap(part, "dp", bit) for part in pieces]
        return pieces

    def fold(total, axis, bit):
        half = total.shape[0] // 2
        return total[:half], swap(total[half:].astype(bf16), axis, bit)

    def add(kept, arrived):
        return kept.astype(f32) + arrived.astype(f32)

    ring_masks = masks_of(ring_bits)
    ring_mask = sum(ring_bits)
    count = len(ring_masks)


    def ffn_jobs(dp_index, refs, offsets, held):
        rows = held.shape[0] // dp_size
        jobs = []
        for mask, ref, offset in zip(ring_masks, refs, offsets):
            base = jnp.bitwise_xor(jnp.bitwise_and(dp_index, ring_mask), mask)
            for low in (0, 1):
                jobs.append(
                    (
                        ref.at[pl.ds(offset + low * rows, rows)],
                        block(held, base + low * pair_bit, rows),
                    )
                )
        return jobs

    def row_jobs(refs, held):
        jobs, start = [], 0
        for ref in refs:
            jobs.append((ref, held.at[pl.ds(start, ref.shape[0])]))
            start += ref.shape[0]
        return jobs

    def attn_jobs(dp_index, refs, pieces, held):
        rows = held.shape[0] // dp_size
        return [
            (
                ref.at[pl.ds(first, rows)],
                block(held, jnp.bitwise_xor(dp_index, mask), rows),
            )
            for ref, (_, first, mask) in zip(refs, pieces)
        ]

    def arrays_of(pieces):
        return [piece[0] for piece in pieces]

    token_masks = ((0, 2), (1, 3))

    def token_jobs(tensor_index, pair, other, held):
        rows = held.shape[0] // 4
        jobs = []
        for masks, ref in zip(token_masks, (pair, other)):
            for at, mask in enumerate(masks):
                spot = jnp.bitwise_xor(tensor_index, mask)
                jobs.append((ref.at[pl.ds(at * rows, rows)], block(held, spot, rows)))
        return jobs

    def quarter_jobs(tensor_index, refs, held):
        rows = held.shape[0] // 4
        return [
            (ref, block(held, jnp.bitwise_xor(tensor_index, mask), rows))
            for ref, mask in zip(refs, (0, 2, 1, 3))
        ]

    def back(jobs):
        return [(dst, src) for src, dst in jobs]

    def ffn_up(scalars, pieces, gate_pieces, up_pieces):
        tokens, model = sum(piece.shape[0] for piece in pieces), pieces[0].shape[1]
        units = gate_pieces[0][0].shape[1]
        rows = tokens // 2
        many = len(pieces)
        early = 2

        def kernel(scal, *refs):
            parts = refs[:many]
            gates = refs[many : many + count]
            ups = refs[many + count : many + 2 * count]
            acts_ref, mixed_ref, silu_ref, back_ref, acts, gate_w, up_w, sems = refs[
                many + 2 * count :
            ]
            jobs = row_jobs(parts, acts)
            gate_jobs = ffn_jobs(scal[0], gates, [at for _, at in gate_pieces], gate_w)
            up_jobs = ffn_jobs(scal[0], ups, [at for _, at in up_pieces], up_w)
            step = pl.program_id(0)

            @pl.when(step == 0)
            def _():
                copies = start_all(jobs[:early] + gate_jobs + jobs[early:] + up_jobs, sems)
                wait_all(copies[: early + 2 * count])

            @pl.when(step == 1)
            def _():
                wait_all(made(jobs[early:], sems, early + 2 * count))

            spot = pl.ds(pl.multiple_of(step * rows, rows), rows)
            rows_in = acts[spot, :]
            acts_ref[...] = rows_in
            gate = mm(rows_in, gate_w[...])

            @pl.when(step == 0)
            def _():
                wait_all(made(up_jobs, sems, many + 2 * count))

            up = mm(rows_in, up_w[...])
            sig = jax.nn.sigmoid(gate)
            silu = gate * sig
            mixed_ref[...] = (silu * up).astype(bf16)
            silu_ref[...] = silu.astype(bf16)
            back_ref[...] = (up * sig * (1.0 + gate * (1.0 - sig))).astype(bf16)

        out = jax.ShapeDtypeStruct((tokens, units), bf16)
        spec = pl.BlockSpec((rows, units), lambda i: (i, 0))
        return pl.pallas_call(
            kernel,
            grid=(2,),
            in_specs=[SCALARS] + [ANY] * (many + 2 * count),
            out_specs=[pl.BlockSpec((rows, model), lambda i: (i, 0))] + [spec] * 3,
            out_shape=[jax.ShapeDtypeStruct((tokens, model), bf16)] + [out] * 3,
            scratch_shapes=[
                pltpu.VMEM((tokens, model), bf16),
                pltpu.VMEM((model, units), bf16),
                pltpu.VMEM((model, units), bf16),
                pltpu.SemaphoreType.DMA((many + 4 * count,)),
            ],
            name="ffn_up",
        )(
            scalars,
            *pieces,
            *[ref for ref, _ in gate_pieces],
            *[ref for ref, _ in up_pieces],
        )

    def ffn_back(scalars, cots, down_pieces, gate_pieces, up_pieces, silu, back_part):
        many = len(cots)
        tokens, model = sum(piece.shape[0] for piece in cots), cots[0].shape[1]
        units = silu.shape[1]
        rows = tokens // 2
        lists = (down_pieces, gate_pieces, up_pieces)

        def kernel(scal, *refs):
            parts = refs[:many]
            pieces = [refs[many + at * count : many + (at + 1) * count] for at in range(3)]
            silu_ref, back_ref, grad_gate_ref, grad_up_ref, out_ref = refs[
                many + 3 * count : many + 3 * count + 5
            ]
            cot, *held = refs[many + 3 * count + 5 : -1]
            sems = refs[-1]
            jobs = row_jobs(parts, cot)
            for at in range(3):
                jobs += ffn_jobs(scal[0], pieces[at], [spot for _, spot in lists[at]], held[at])
            first = pl.program_id(0) == 0
            early = many + 2 * count

            @pl.when(first)
            def _():
                wait_all(start_all(jobs, sems)[:early])

            spot = pl.ds(pl.multiple_of(pl.program_id(0) * rows, rows), rows)
            grad_mixed = mm(cot[spot, :], held[0][...])
            grad_gate = (grad_mixed * back_ref[...].astype(f32)).astype(bf16)
            grad_up = (grad_mixed * silu_ref[...].astype(f32)).astype(bf16)
            grad_gate_ref[...] = grad_gate
            grad_up_ref[...] = grad_up

            @pl.when(first)
            def _():
                wait_all(made(jobs[early:], sems, early))

            out_ref[...] = (
                mm_nt(grad_gate, held[1][...]) + mm_nt(grad_up, held[2][...])
            ).astype(bf16)

        out = jax.ShapeDtypeStruct((tokens, units), bf16)
        spec = pl.BlockSpec((rows, units), lambda i: (i, 0))
        wide = pl.BlockSpec((rows, model), lambda i: (i, 0))
        return pl.pallas_call(
            kernel,
            grid=(2,),
            in_specs=[SCALARS] + [ANY] * (many + 3 * count) + [spec, spec],
            out_specs=[spec, spec, wide],
            out_shape=[out, out, jax.ShapeDtypeStruct((tokens, model), bf16)],
            scratch_shapes=[pltpu.VMEM((tokens, model), bf16)]
            + [pltpu.VMEM((model, units), bf16)] * 3
            + [pltpu.SemaphoreType.DMA((many + 6 * count,))],
            name="ffn_back",
        )(scalars, *cots, *[ref for pieces in lists for ref, _ in pieces], silu, back_part)

    def ffn_rows(scalars, left, pieces, model, name):
        tokens, units = left.shape
        rows = tokens // 2

        def kernel(scal, left_ref, *refs):
            parts = refs[:count]
            out_ref, held, sems = refs[count:]

            @pl.when(pl.program_id(0) == 0)
            def _():
                wait_all(
                    start_all(ffn_jobs(scal[0], parts, [at for _, at in pieces], held), sems)
                )

            out_ref[...] = mm_nt(left_ref[...], held[...]).astype(bf16)

        return pl.pallas_call(
            kernel,
            grid=(2,),
            in_specs=[SCALARS, pl.BlockSpec((rows, units), lambda i: (i, 0))] + [ANY] * count,
            out_specs=pl.BlockSpec((rows, model), lambda i: (i, 0)),
            out_shape=jax.ShapeDtypeStruct((tokens, model), bf16),
            scratch_shapes=[
                pltpu.VMEM((model, units), bf16),
                pltpu.SemaphoreType.DMA((2 * count,)),
            ],
            name=name,
        )(scalars, left, *[ref for ref, _ in pieces])

    def ffn_grad(scalars, own_pieces, core_pieces, low, high, name):
        pieces = [*own_pieces, *core_pieces]
        many = len(own_pieces)
        tokens, model = low.shape[0], pieces[0].shape[1]
        units = low.shape[1]
        shard = model // dp_size
        wide = 384
        groups = wide // (2 * shard)

        def kernel(scal, *refs):
            def stack(parts):
                values = [part[...] for part in parts]
                return values[0] if len(values) == 1 else jnp.concatenate(values, axis=0)

            low_ref, high_ref, kept_ref, sent_ref = refs[2 * many :]
            total = mm_tn(stack(refs[:many]), low_ref[...])
            total = total + mm_tn(stack(refs[many : 2 * many]), high_ref[...])
            total = total.astype(bf16)
            odd = jnp.bitwise_and(scal[0], 1) == 1
            for group in range(groups):
                first = total[group * 2 * shard : group * 2 * shard + shard]
                second = total[group * 2 * shard + shard : (group + 1) * 2 * shard]
                spot = pl.ds(group * shard, shard)
                kept_ref[spot, :] = jnp.where(odd, second, first)
                sent_ref[spot, :] = jnp.where(odd, first, second)

        out = jax.ShapeDtypeStruct((model // 2, units), bf16)
        spec = pl.BlockSpec((wide // 2, units), lambda i: (i, 0))
        whole = pl.BlockSpec((tokens, units), lambda i: (0, 0))
        return pl.pallas_call(
            kernel,
            grid=(model // wide,),
            in_specs=[SCALARS]
            + [pl.BlockSpec((piece.shape[0], wide), lambda i: (0, i)) for piece in pieces]
            + [whole, whole],
            out_specs=[spec] * 2,
            out_shape=[out] * 2,
            name=name,
        )(scalars, *pieces, low, high)

    def is_high(scal, bit):
        return jnp.bitwise_and(scal[0], bit) != 0

    def whole_call(kernel, outs, name, *args):
        return pl.pallas_call(
            kernel,
            in_specs=[SCALARS] + [WHOLE] * (len(args) - 1),
            out_specs=[WHOLE] * len(outs),
            out_shape=[jax.ShapeDtypeStruct(shape, kind) for shape, kind in outs],
            name=name,
        )(*args)

    def split_cols(scalars, *arrays):
        rows, half = arrays[0].shape[0], arrays[0].shape[1] // 2
        wide = -(-half // 128) * 128
        many = len(arrays)

        def kernel(scal, *refs):
            mine_ref, sent_ref = refs[many:]
            flag = is_high(scal, pair_bit)
            mine_ref[...] = jnp.zeros_like(mine_ref)
            sent_ref[...] = jnp.zeros_like(sent_ref)
            for at in range(many):
                low, high = refs[at][:, :half], refs[at][:, half:]
                mine_ref[at * rows : (at + 1) * rows, :half] = jnp.where(flag, high, low)
                sent_ref[at * rows : (at + 1) * rows, :half] = jnp.where(flag, low, high)

        return whole_call(
            kernel, [((many * rows, wide), bf16)] * 2, "split_cols", scalars, *arrays
        )

    def join_rows(scalars, mine, theirs, at, many):
        rows, columns = mine.shape[0] // many, mine.shape[1]
        spot = pl.ds(at * rows, rows)

        def kernel(scal, mine_ref, theirs_ref, out_ref):
            flag = is_high(scal, pair_bit)
            out_ref[:rows, :] = jnp.where(flag, theirs_ref[spot, :], mine_ref[spot, :])
            out_ref[rows:, :] = jnp.where(flag, mine_ref[spot, :], theirs_ref[spot, :])

        return whole_call(
            kernel, [((2 * rows, columns), bf16)], "join_rows", scalars, mine, theirs
        )[0]

    def join_cols(scalars, mine, theirs, columns):
        rows = mine.shape[0]

        def kernel(scal, mine_ref, theirs_ref, out_ref):
            flag = is_high(scal, pair_bit)
            mine = mine_ref[:, :columns].astype(f32)
            theirs = theirs_ref[:, :columns].astype(f32)
            out_ref[:, :columns] = jnp.where(flag, theirs, mine)
            out_ref[:, columns:] = jnp.where(flag, mine, theirs)

        return whole_call(
            kernel, [((rows, 2 * columns), f32)], "join_cols", scalars, mine, theirs
        )[0]

    def fold_sum(scalars, kept, arrived, bit, outer):
        rows, columns = kept.shape[0] // 2, kept.shape[1]
        part = rows // outer

        def kernel(scal, kept_ref, arrived_ref, own_ref, sent_ref):
            flag = is_high(scal, bit)
            for at in range(outer):
                first = pl.ds(2 * at * part, part)
                second = pl.ds((2 * at + 1) * part, part)
                low = kept_ref[first, :].astype(f32) + arrived_ref[first, :].astype(f32)
                high = kept_ref[second, :].astype(f32) + arrived_ref[second, :].astype(f32)
                spot = pl.ds(at * part, part)
                own_ref[spot, :] = jnp.where(flag, high, low).astype(bf16)
                sent_ref[spot, :] = jnp.where(flag, low, high).astype(bf16)

        wide = 384 if columns % 384 == 0 else columns
        spec = pl.BlockSpec((2 * rows, wide), lambda i: (0, i))
        return pl.pallas_call(
            kernel,
            grid=(columns // wide,),
            in_specs=[SCALARS, spec, spec],
            out_specs=[pl.BlockSpec((rows, wide), lambda i: (0, i))] * 2,
            out_shape=[jax.ShapeDtypeStruct((rows, columns), bf16)] * 2,
            name="fold_sum",
        )(scalars, kept, arrived)

    def norm_two(scalars, rows_in, kept, sums, arrived, gain):
        rows, columns = rows_in.shape

        def kernel(scal, kept_ref, sums_ref, in_ref, arrived_ref, gain_ref, hidden_ref, out_ref):
            hidden = in_ref[...].astype(f32) + kept_ref[...].astype(f32)
            hidden = hidden + sums_ref[...].astype(f32) + arrived_ref[...].astype(f32)
            hidden_ref[...] = hidden
            out_ref[...] = (norm_forward(hidden)[0] * gain_ref[...]).astype(bf16)

        return row_call(
            kernel, [((rows, columns), f32), ((rows, columns), bf16)], "norm_two", scalars,
            [(kept, rows, 0), (sums, rows, 0)], [rows_in, arrived, gain],
        )

    def norm_one_back(scalars, rows_in, kept, sums, arrived, gain, given):
        rows, columns = rows_in.shape

        def kernel(scal, kept_ref, sums_ref, in_ref, arrived_ref, gain_ref, given_ref, out_ref):
            grad_out = kept_ref[...].astype(f32) + sums_ref[...].astype(f32)
            grad_out = grad_out + arrived_ref[...].astype(f32)
            normed, row_scale = norm_forward(in_ref[...].astype(f32))
            grad_normed = grad_out * gain_ref[...]
            grad_in = row_scale * (
                grad_normed - normed * jnp.mean(grad_normed * normed, axis=-1, keepdims=True)
            )
            out_ref[...] = (given_ref[...] + grad_in).astype(bf16)

        return row_call(
            kernel, [((rows, columns), bf16)], "norm_one_back", scalars,
            [(kept, rows, 0), (sums, rows, 0)], [rows_in, arrived, gain, given],
        )[0]

    def join_both(scalars, first, mine, theirs):
        rows, columns = mine.shape[0] // 2, mine.shape[1]

        def kernel(scal, first_ref, mine_ref, theirs_ref, out_ref, both_ref):
            flag = is_high(scal, pair_bit)
            low = jnp.where(flag, theirs_ref[:rows, :], mine_ref[:rows, :])
            high = jnp.where(flag, mine_ref[:rows, :], theirs_ref[:rows, :])
            out_ref[:rows, :] = low
            out_ref[rows:, :] = high
            both_ref[: 2 * rows, :] = first_ref[...]
            both_ref[2 * rows : 3 * rows, :] = low
            both_ref[3 * rows :, :] = high

        return whole_call(
            kernel,
            [((2 * rows, columns), bf16), ((4 * rows, columns), bf16)],
            "join_both", scalars, first, mine, theirs,
        )

    def halves(scalars, first, second):
        rows, columns = first.shape[0] // 2, first.shape[1]

        def kernel(scal, first_ref, second_ref, out_a_ref, out_b_ref):
            out_a_ref[...] = first_ref[:rows, :]
            out_b_ref[...] = second_ref[rows:, :]

        return whole_call(
            kernel, [((rows, columns), bf16)] * 2, "halves", scalars, first, second
        )

    def fold_both(scalars, first, first_arrived, second, second_arrived, bit, outer):
        rows = first.shape[0] // 2
        columns = (first.shape[1], second.shape[1])
        part = rows // outer

        def kernel(scal, first_ref, first_in_ref, second_ref, second_in_ref, own_ref, sent_ref):
            flag = is_high(scal, bit)
            for lanes, kept_ref, arrived_ref in (
                (slice(0, columns[0]), first_ref, first_in_ref),
                (slice(columns[0], columns[0] + columns[1]), second_ref, second_in_ref),
            ):
                for at in range(outer):
                    low_spot = pl.ds(2 * at * part, part)
                    high_spot = pl.ds((2 * at + 1) * part, part)
                    low = kept_ref[low_spot, :].astype(f32) + arrived_ref[low_spot, :].astype(f32)
                    high = kept_ref[high_spot, :].astype(f32) + arrived_ref[high_spot, :].astype(f32)
                    spot = pl.ds(at * part, part)
                    own_ref[spot, lanes] = jnp.where(flag, high, low)
                    sent_ref[spot, lanes] = jnp.where(flag, low, high).astype(bf16)

        outs = [((rows, sum(columns)), f32), ((rows, sum(columns)), bf16)]
        return whole_call(
            kernel, outs, "fold_both", scalars, first, first_arrived, second, second_arrived
        )

    def rows_block(rows, columns, at):
        return pl.BlockSpec((rows, columns), lambda i: (at, 0))

    def part_call(kernel, outs, name, scalars, parts, rest):
        return pl.pallas_call(
            kernel,
            grid=(1,),
            in_specs=[SCALARS]
            + [rows_block(rows, array.shape[1], at) for array, rows, at in parts]
            + [WHOLE] * len(rest),
            out_specs=[WHOLE] * len(outs),
            out_shape=[jax.ShapeDtypeStruct(shape, kind) for shape, kind in outs],
            name=name,
        )(scalars, *[array for array, _, _ in parts], *rest)

    def row_call(kernel, outs, name, scalars, parts, rest):
        steps, rows = 4, parts[0][1]
        size = rows // steps

        def part_spec(columns, at):
            return pl.BlockSpec((size, columns), lambda i: (at * steps + i, 0))

        def rest_spec(array):
            if array.shape[0] == 1:
                return pl.BlockSpec(array.shape, lambda i: (0, 0))
            return part_spec(array.shape[1], 0)

        return pl.pallas_call(
            kernel,
            grid=(steps,),
            in_specs=[SCALARS]
            + [part_spec(array.shape[1], at) for array, _, at in parts]
            + [rest_spec(array) for array in rest],
            out_specs=[part_spec(shape[1], 0) for shape, _ in outs],
            out_shape=[jax.ShapeDtypeStruct(shape, kind) for shape, kind in outs],
            name=name,
        )(scalars, *[array for array, _, _ in parts], *rest)

    def part_sum(scalars, kept, arrived, rows, at, pieces):
        columns, size = kept.shape[1], rows // pieces

        def kernel(scal, kept_ref, arrived_ref, *out_refs):
            for piece, ref in enumerate(out_refs):
                spot = pl.ds(piece * size, size)
                ref[...] = (
                    kept_ref[spot, :].astype(f32) + arrived_ref[spot, :].astype(f32)
                ).astype(bf16)

        return part_call(
            kernel, [((size, columns), bf16)] * pieces, "part_sum", scalars,
            [(kept, rows, at), (arrived, rows, at)], [],
        )

    def spread_rest(scalars, kept, arrived, far_x, far_l):
        rows, columns = kept.shape[0] // 4, kept.shape[1]
        half = rows // 2

        def kernel(scal, *refs):
            keeps, arrives = refs[:3], refs[3:6]
            far_x_ref, far_l_ref, own_ref, x_ref, l_ref = refs[6:]
            own_ref[...] = keeps[0][...].astype(f32) + arrives[0][...].astype(f32)
            to_x = keeps[1][...].astype(f32) + arrives[1][...].astype(f32)
            x_ref[:half, :] = to_x[:half].astype(bf16)
            x_ref[half:, :] = (to_x[half:] + far_l_ref[...].astype(f32)).astype(bf16)
            to_l = keeps[2][...].astype(f32) + arrives[2][...].astype(f32)
            l_ref[:half, :] = (to_l[:half] + far_x_ref[...].astype(f32)).astype(bf16)
            l_ref[half:, :] = to_l[half:].astype(bf16)

        outs = [((rows, columns), f32), ((rows, columns), bf16), ((rows, columns), bf16)]
        return part_call(
            kernel, outs, "spread_rest", scalars,
            [(array, rows, at) for array in (kept, arrived) for at in range(3)], [far_x, far_l],
        )

    def block_x_sum(scalars, kept, arrived, from_l):
        rows, columns = kept.shape[0] // 4, kept.shape[1]

        def kernel(scal, kept_ref, arrived_ref, from_ref, out_ref):
            out_ref[...] = (
                kept_ref[...].astype(f32)
                + arrived_ref[...].astype(f32)
                + from_ref[...].astype(f32)
            ).astype(bf16)

        return part_call(
            kernel, [((rows, columns), bf16)], "block_x_sum", scalars,
            [(kept, rows, 1), (arrived, rows, 1), (from_l, rows, 1)], [],
        )[0]

    def block_final(scalars, kept, arrived, from_l, hidden, from_x):
        rows, columns = hidden.shape

        def kernel(scal, kept_ref, arrived_ref, from_ref, hidden_ref, x_ref, out_ref):
            total = hidden_ref[...] + kept_ref[...].astype(f32) + arrived_ref[...].astype(f32)
            out_ref[...] = (total + from_ref[...].astype(f32) + x_ref[...].astype(f32)).astype(bf16)

        return part_call(
            kernel, [((rows, columns), bf16)], "block_final", scalars,
            [(kept, rows, 0), (arrived, rows, 0), (from_l, rows, 0)], [hidden, from_x],
        )[0]

    def give(total, scal, kept_ref, sent_ref):
        part = pair_bit * (total.shape[0] // dp_size)
        flag = is_high(scal, pair_bit)
        for at in range(total.shape[0] // (2 * part)):
            low = total[2 * at * part : (2 * at + 1) * part]
            high = total[(2 * at + 1) * part : (2 * at + 2) * part]
            kept_ref[pl.ds(at * part, part), :] = jnp.where(flag, high, low)
            sent_ref[pl.ds(at * part, part), :] = jnp.where(flag, low, high)

    def project(scalars, pair, core, pieces, bias, cosine, sine):
        tokens, model = 2 * pair.shape[0], pair.shape[1]
        columns = pieces[0][0].shape[1]
        width = columns - HD

        def kernel(scal, pair_ref, core_ref, bias_ref, cos_ref, sin_ref, *refs):
            query_ref, kv_ref, acts, held, sems = refs[dp_size:]
            wait_all(
                start_all(
                    attn_jobs(scal[0], refs[:dp_size], pieces, held)
                    + token_jobs(scal[1], pair_ref, core_ref, acts),
                    sems,
                )
            )
            is_value = jnp.bitwise_and(scal[1], 1) == 1
            rows = tokens // 4
            for at in range(4):
                spot = pl.ds(at * rows, rows)
                out = mm(acts[spot, :], held[...]) + bias_ref[...]
                cosine_rows, sine_rows = cos_ref[spot, :], sin_ref[spot, :]
                for head in range(width // HD):
                    query_ref[spot, head * HD : (head + 1) * HD] = turned(
                        out[:, head * HD : (head + 1) * HD], cosine_rows, sine_rows, 1.0
                    ).astype(bf16)
                kv = out[:, width:]
                kv_ref[spot, :] = jnp.where(
                    is_value, kv, turned(kv, cosine_rows, sine_rows, 1.0)
                ).astype(bf16)

        return pl.pallas_call(
            kernel,
            in_specs=[SCALARS, ANY, ANY, WHOLE, WHOLE, WHOLE] + [ANY] * dp_size,
            out_specs=[WHOLE, WHOLE],
            out_shape=[
                jax.ShapeDtypeStruct((tokens, width), bf16),
                jax.ShapeDtypeStruct((tokens, HD), bf16),
            ],
            scratch_shapes=[
                pltpu.VMEM((tokens, model), bf16),
                pltpu.VMEM((model, columns), bf16),
                pltpu.SemaphoreType.DMA((dp_size + 4,)),
            ],
            name="project",
        )(scalars, pair, core, bias, cosine, sine, *arrays_of(pieces))

    def probabilities(query, keys, start_rows, first):
        scores = mm_nt(query, keys) * (1.0 / math.sqrt(HD))
        column = lax.broadcasted_iota(jnp.int32, scores.shape, 1)
        row = lax.broadcasted_iota(jnp.int32, scores.shape, 0) + first
        allowed = (column <= row) & (column >= start_rows)
        scores = jnp.where(allowed, scores, masked_score)
        top = jnp.max(scores, axis=1, keepdims=True)
        raised = jnp.exp(scores - top)
        return raised * (1.0 / jnp.sum(raised, axis=1, keepdims=True))

    def attend(scalars, query, kv_own, kv_other, starts):
        tokens, width = query.shape
        rows = tokens // 4

        def kernel(scal, query_ref, own_ref, other_ref, start_ref, context_ref):
            is_value = jnp.bitwise_and(scal[1], 1) == 1
            own, other = own_ref[...], other_ref[...]
            keys = jnp.where(is_value, other, own)
            values = jnp.where(is_value, own, other)
            for at in range(4):
                end = (at + 1) * rows
                spot = pl.ds(at * rows, rows)
                for head in range(width // HD):
                    lanes = slice(head * HD, (head + 1) * HD)
                    probs = probabilities(
                        query_ref[spot, lanes], keys[:end], start_ref[spot, :], at * rows
                    )
                    context_ref[spot, lanes] = mm(probs.astype(bf16), values[:end]).astype(bf16)

        return whole_call(
            kernel, [((tokens, width), bf16)], "attend", scalars, query, kv_own, kv_other, starts
        )[0]

    def out_rows(scalars, context, pieces, model):
        tokens, width = context.shape
        rows = tokens // 4

        def kernel(scal, context_ref, *refs):
            kept_ref, sent_ref, held, part, sems, out_sems = refs[dp_size:]
            wait_all(start_all(attn_jobs(scal[0], refs[:dp_size], pieces, held), sems))
            jobs = back(token_jobs(scal[1], kept_ref, sent_ref, part))
            copies = made(jobs, out_sems)
            for at in (2, 3, 0, 1):
                mask = (0, 2, 1, 3)[at]
                spot = jnp.bitwise_xor(scal[1], mask)
                spot = pl.ds(pl.multiple_of(spot * rows, rows), rows)
                part[spot, :] = mm_nt(context_ref[spot, :], held[...]).astype(bf16)
                copies[at].start()
            wait_all(copies)

        half = jax.ShapeDtypeStruct((tokens // 2, model), bf16)
        return pl.pallas_call(
            kernel,
            in_specs=[SCALARS, WHOLE] + [ANY] * dp_size,
            out_specs=[ANY, ANY],
            out_shape=[half, half],
            scratch_shapes=[
                pltpu.VMEM((model, width), bf16),
                pltpu.VMEM((tokens, model), bf16),
                pltpu.SemaphoreType.DMA((dp_size,)),
                pltpu.SemaphoreType.DMA((4,)),
            ],
            name="out_rows",
        )(scalars, context, *arrays_of(pieces))

    def attend_back(
        scalars, query, kv_own, kv_other, starts, pieces, attn, context, cosine, sine
    ):
        tokens, width = query.shape
        model = attn[0].shape[1]
        rows = tokens // 4
        scale = 1.0 / math.sqrt(HD)

        def kernel(
            scal, query_ref, own_ref, other_ref, start_ref, attn_a, attn_b, attn_c, attn_d,
            context_ref, cos_ref, sin_ref, *refs,
        ):
            grad_query_ref, kv_kept_ref, kv_sent_ref, bias_ref, wout_ref, wout_sent_ref = refs[
                dp_size : dp_size + 6
            ]
            held, grads, grad_context, grad_key, grad_value, sems = refs[dp_size + 6 :]
            wait_all(
                start_all(
                    attn_jobs(scal[0], refs[:dp_size], pieces, held)
                    + quarter_jobs(scal[1], (attn_a, attn_b, attn_c, attn_d), grads),
                    sems,
                )
            )
            is_value = jnp.bitwise_and(scal[1], 1) == 1
            own, other = own_ref[...], other_ref[...]
            keys = jnp.where(is_value, other, own)
            values = jnp.where(is_value, own, other)
            for at in range(2):
                spot = pl.ds(at * 2 * rows, 2 * rows)
                grad_context[spot, :] = mm(grads[spot, :], held[...]).astype(bf16)
            give(mm_tn(grads[...], context_ref[...]).astype(bf16), scal, wout_ref, wout_sent_ref)
            grad_key[...] = jnp.zeros_like(grad_key)
            grad_value[...] = jnp.zeros_like(grad_value)
            bias_ref[...] = jnp.zeros_like(bias_ref)
            for at in range(4):
                end = (at + 1) * rows
                spot = pl.ds(at * rows, rows)
                upto = pl.ds(0, end)
                for head in range(width // HD):
                    lanes = slice(head * HD, (head + 1) * HD)
                    queries = query_ref[spot, lanes]
                    given = grad_context[spot, lanes]
                    probs = probabilities(queries, keys[:end], start_ref[spot, :], at * rows)
                    low = probs.astype(bf16)
                    grad_probs = mm_nt(given, values[:end])
                    delta = jnp.sum(low.astype(f32) * grad_probs, axis=1, keepdims=True)
                    grad_scores = (probs * (grad_probs - delta)).astype(bf16)
                    grad_query = turned(
                        mm(grad_scores, keys[:end]) * scale, cos_ref[spot, :], sin_ref[spot, :], -1.0
                    )
                    grad_query_ref[spot, lanes] = grad_query.astype(bf16)
                    bias_ref[0:1, lanes] += jnp.sum(grad_query, axis=0, keepdims=True)
                    grad_key[upto, :] += mm_tn(grad_scores, queries)
                    grad_value[upto, :] += mm_tn(low, given)
            grad_keys = turned(grad_key[...] * scale, cos_ref[...], sin_ref[...], -1.0)
            grad_values = grad_value[...]
            bias_ref[0:1, width : width + HD] = jnp.sum(grad_keys, axis=0, keepdims=True)
            bias_ref[0:1, width + HD :] = jnp.sum(grad_values, axis=0, keepdims=True)
            kv_kept_ref[...] = jnp.where(is_value, grad_values, grad_keys)
            kv_sent_ref[...] = jnp.where(is_value, grad_keys, grad_values).astype(bf16)

        return pl.pallas_call(
            kernel,
            in_specs=[SCALARS] + [WHOLE] * 4 + [ANY] * 4 + [WHOLE] * 3 + [ANY] * dp_size,
            out_specs=[WHOLE] * 6,
            out_shape=[
                jax.ShapeDtypeStruct((tokens, width), bf16),
                jax.ShapeDtypeStruct((tokens, HD), f32),
                jax.ShapeDtypeStruct((tokens, HD), bf16),
                jax.ShapeDtypeStruct((8, width + 2 * HD), f32),
                jax.ShapeDtypeStruct((model // 2, width), bf16),
                jax.ShapeDtypeStruct((model // 2, width), bf16),
            ],
            scratch_shapes=[
                pltpu.VMEM((model, width), bf16),
                pltpu.VMEM((tokens, model), bf16),
                pltpu.VMEM((tokens, width), bf16),
                pltpu.VMEM((tokens, HD), f32),
                pltpu.VMEM((tokens, HD), f32),
                pltpu.SemaphoreType.DMA((dp_size + 4,)),
            ],
            name="attend_back",
        )(
            scalars, query, kv_own, kv_other, starts, *attn, context, cosine, sine,
            *arrays_of(pieces),
        )

    def project_back(scalars, grad_query, kv_kept, kv_arrived, pieces):
        tokens, width = grad_query.shape
        columns = pieces[0][0].shape[1]
        model = dp_size * shard_rows(pieces)
        rows = tokens // 4

        def kernel(scal, query_ref, kept_kv_ref, arrived_ref, *refs):
            grads_ref, kept_ref, sent_ref, held, part, sems, out_sems = refs[dp_size:]
            copies = start_all(attn_jobs(scal[0], refs[:dp_size], pieces, held), sems)
            grads_ref[:, :width] = query_ref[...]
            grads_ref[:, width:] = (kept_kv_ref[...] + arrived_ref[...].astype(f32)).astype(bf16)
            wait_all(copies)
            jobs = back(token_jobs(scal[1], kept_ref, sent_ref, part))
            copies = made(jobs, out_sems)
            for at in (2, 3, 0, 1):
                mask = (0, 2, 1, 3)[at]
                spot = jnp.bitwise_xor(scal[1], mask)
                spot = pl.ds(pl.multiple_of(spot * rows, rows), rows)
                part[spot, :] = mm_nt(grads_ref[spot, :], held[...]).astype(bf16)
                copies[at].start()
            wait_all(copies)

        half = jax.ShapeDtypeStruct((tokens // 2, model), bf16)
        return pl.pallas_call(
            kernel,
            in_specs=[SCALARS, WHOLE, WHOLE, WHOLE] + [ANY] * dp_size,
            out_specs=[WHOLE, ANY, ANY],
            out_shape=[jax.ShapeDtypeStruct((tokens, columns), bf16), half, half],
            scratch_shapes=[
                pltpu.VMEM((model, columns), bf16),
                pltpu.VMEM((tokens, model), bf16),
                pltpu.SemaphoreType.DMA((dp_size,)),
                pltpu.SemaphoreType.DMA((4,)),
            ],
            name="project_back",
        )(scalars, grad_query, kv_kept, kv_arrived, *arrays_of(pieces))

    def shard_rows(pieces):
        return min(piece[0].shape[0] for piece in pieces)

    def gain_rows_of(scalars, kept, sent, pair, core):
        rows, model = kept.shape[0] // 4, kept.shape[1]

        def kernel(scal, kept_ref, sent_ref, pair_ref, core_ref, gain_ref):
            @pl.when(pl.program_id(0) == 0)
            def _():
                gain_ref[...] = jnp.zeros_like(gain_ref)

            total = kept_ref[...].astype(f32) * pair_ref[...].astype(f32)
            total = total + sent_ref[...].astype(f32) * core_ref[...].astype(f32)
            gain_ref[0:1, :] += jnp.sum(total, axis=0, keepdims=True)

        return pl.pallas_call(
            kernel,
            grid=(4,),
            in_specs=[SCALARS] + [pl.BlockSpec((rows, model), lambda i: (i, 0))] * 4,
            out_specs=pl.BlockSpec((8, model), lambda i: (0, 0)),
            out_shape=jax.ShapeDtypeStruct((8, model), f32),
            name="gain_rows",
        )(scalars, kept, sent, pair, core)

    def project_grad(scalars, pair, core, grads):
        tokens, columns = grads.shape
        model = pair.shape[1]

        def kernel(scal, pair_ref, core_ref, grads_ref, kept_ref, sent_ref, acts, sems):
            wait_all(start_all(token_jobs(scal[1], pair_ref, core_ref, acts), sems))
            give(mm_tn(acts[...], grads_ref[...]).astype(bf16), scal, kept_ref, sent_ref)

        return pl.pallas_call(
            kernel,
            in_specs=[SCALARS, ANY, ANY, WHOLE],
            out_specs=[WHOLE] * 2,
            out_shape=[jax.ShapeDtypeStruct((model // 2, columns), bf16)] * 2,
            scratch_shapes=[
                pltpu.VMEM((tokens, model), bf16),
                pltpu.SemaphoreType.DMA((4,)),
            ],
            name="project_grad",
        )(scalars, pair, core, grads)

    def norm_two_back(scalars, own, from_x, from_l, hidden, gain, given):
        rows, model = own.shape

        def kernel(scal, own_ref, x_ref, l_ref, hidden_ref, gain_ref, given_ref, out_ref, low_ref, sum_ref):
            grad_out = own_ref[...] + x_ref[...].astype(f32) + l_ref[...].astype(f32)
            normed, row_scale = norm_forward(hidden_ref[...])
            grad_normed = grad_out * gain_ref[...]
            grad_in = row_scale * (
                grad_normed - normed * jnp.mean(grad_normed * normed, axis=-1, keepdims=True)
            )
            total = given_ref[...].astype(f32) + grad_in
            out_ref[...] = total
            low_ref[...] = total.astype(bf16)

            @pl.when(pl.program_id(0) == 0)
            def _():
                sum_ref[...] = jnp.zeros_like(sum_ref)

            sum_ref[0:1, :] += jnp.sum(grad_out * normed, axis=0, keepdims=True)

        spec = pl.BlockSpec((rows // 4, model), lambda i: (i, 0))
        return pl.pallas_call(
            kernel,
            grid=(4,),
            in_specs=[SCALARS] + [spec] * 4 + [pl.BlockSpec((1, model), lambda i: (0, 0)), spec],
            out_specs=[spec, spec, pl.BlockSpec((8, model), lambda i: (0, 0))],
            out_shape=[
                jax.ShapeDtypeStruct((rows, model), f32),
                jax.ShapeDtypeStruct((rows, model), bf16),
                jax.ShapeDtypeStruct((8, model), f32),
            ],
            name="norm_two_back",
        )(scalars, own, from_x, from_l, hidden, gain, given)

    def local(
        block_input,
        segment_ids,
        gain_attn,
        w_query,
        b_query,
        w_keyval,
        b_keyval,
        w_out,
        gain_ffn,
        w_gate,
        w_up,
        w_down,
        cotangent,
    ):
        dp_index = lax.axis_index("dp")
        tensor_index = lax.axis_index("tensor")
        scalars = jnp.stack([dp_index, tensor_index]).astype(jnp.int32)
        local_heads = b_query.shape[0] // HD
        head_kv = tensor_index * local_heads // (HQ // KV)
        is_value = tensor_index % 2
        kv_column = is_value * (KV * HD) + head_kv * HD
        width = local_heads * HD

        groups = dp_size // 4

        def far_rest(kept, sent):
            arrived = swap(sent, "dp", far_bits[0])
            for bit in far_bits[1:]:
                kept, sent = fold_sum(scalars, kept, arrived, bit, 1)
                arrived = swap(sent, "dp", bit)
            return kept, arrived

        keyval_cols = lax.dynamic_slice_in_dim(w_keyval, kv_column, HD, 1)
        qkv_own = jnp.concatenate([w_query, keyval_cols], axis=1)
        shard = qkv_own.shape[0]
        qkv_far = far_pieces(qkv_own)
        qkv_l = swap(qkv_own, "dp", pair_bit)
        qkv_y = swap(qkv_own, "dp", 1)
        rows_float = block_input.astype(f32)
        normed_one, scale_one = norm_forward(rows_float)
        act_own = (normed_one * gain_attn).astype(bf16)
        act_x = swap(act_own, "tensor", 2)
        gate_mine, gate_sent = split_cols(scalars, w_gate)
        gate_theirs = swap(gate_sent, "dp", pair_bit)

        qkv_far_in, qkv_l, qkv_y, out_own, w_up_in, w_down_in, segments = hold(
            [gate_sent, act_own],
            [tuple(qkv_far[1:]), qkv_l, qkv_y, w_out.T, w_up, w_down, segment_ids],
        )
        far_rows = rows_of(*qkv_far_in)
        qkv_y2 = swap(rows_of(qkv_l, far_rows), "dp", 1)
        qkv_l2 = swap(far_rows, "dp", pair_bit)
        out_far = far_pieces(out_own)
        rest_mine, rest_sent = split_cols(scalars, w_up_in, w_down_in.T)
        positions = positions_of(segments[0])
        cosine, sine = rotary(positions)
        sine = jnp.where(jnp.arange(HD)[None, :] < HD // 2, -sine, sine)
        starts = (jnp.arange(positions.shape[0], dtype=jnp.int32) - positions)[:, None]
        qkv_bias = jnp.concatenate([b_query, lax.dynamic_slice_in_dim(b_keyval, kv_column, HD, 0)])[
            None, :
        ]

        qkv_y2, qkv_l2, act_pair, gate_theirs, out_half, cosine, sine, starts, rest_sent, cot_own = (
            hold(
                [],
                [
                    qkv_y2,
                    qkv_l2,
                    rows_of(act_own, act_x),
                    gate_theirs,
                    rows_of(*out_far),
                    cosine,
                    sine,
                    starts,
                    rest_sent,
                    cotangent,
                ],
            )
        )

        def gather_attn():
            return (
                swap(qkv_l2, "dp", 1),
                swap(act_pair, "tensor", 1),
                swap(out_half, "dp", pair_bit),
                join_rows(scalars, gate_mine, gate_theirs, 0, 1),
            )

        qkv_y3, act_c, out_l, gate_piece = section(gather_attn)

        qkv_y3, act_c, out_near, rest_sent, cot_core, gate_piece = hold(
            [], [qkv_y3, act_c, rows_of(out_half, out_l), rest_sent, cotangent, gate_piece]
        )
        gate_far = far_pieces(gate_piece)
        cot_x = swap(cot_core, "tensor", 2)
        rest_theirs = swap(rest_sent, "dp", pair_bit)
        out_y = swap(out_near, "dp", 1)
        far_masks = masks_of(far_bits)
        qkv_pieces = [(part, 0, mask) for part, mask in zip(qkv_far, far_masks)]
        qkv_pieces += [(qkv_l, 0, pair_bit), (qkv_y, 0, 1), (qkv_y2, 0, pair_bit ^ 1)]
        for at, mask in enumerate(far_masks[1:]):
            qkv_pieces += [
                (qkv_y2, (at + 1) * shard, mask ^ 1),
                (qkv_l2, at * shard, mask ^ pair_bit),
                (qkv_y3, at * shard, mask ^ pair_bit ^ 1),
            ]

        def attention():
            query_rot, kv_own = project(
                scalars, act_pair, act_c, qkv_pieces, qkv_bias, cosine, sine
            )
            kv_other = swap(kv_own, "tensor", 1)
            kv_other, cot_given = hold([], [kv_other, cot_core])
            cot_own_c = swap(cot_given, "tensor", 1)
            context = attend(scalars, query_rot, kv_own, kv_other, starts)
            context, cot_own_c = hold([], [context, cot_own_c])
            return query_rot, kv_own, kv_other, context, cot_own_c

        def out_pieces(near, far):
            pieces = []
            masks = masks_of(far_bits + [pair_bit])
            for at, mask in enumerate(masks):
                pieces += [(near, at * shard, mask), (far, at * shard, mask ^ 1)]
            return pieces

        query_rot, kv_own, kv_other, context, cot_own_c = section(attention)
        context, out_y = hold([], [context, out_y])
        out_parts = out_pieces(out_near, out_y)
        attn_kept, attn_sent = out_rows(scalars, context, out_parts, act_pair.shape[1])

        attn_sent, rest_theirs, cot_own_l = hold([cot_x], [attn_sent, rest_theirs, cotangent])

        def sum_cores():
            arrived = swap(attn_sent, "tensor", 1)
            return arrived, join_both(scalars, gate_piece, rest_mine, rest_theirs)

        attn_arrived, (up_piece, own_both) = section(sum_cores)
        attn_arrived, up_piece, own_both = hold([], [attn_arrived, up_piece, own_both])
        up_far = far_pieces(up_piece)
        own_y = swap(own_both, "dp", 1)
        cot_l = swap(cot_own_l, "dp", pair_bit)

        def sum_heads():
            (sent,) = part_sum(scalars, attn_kept, attn_arrived, block_input.shape[0], 1, 1)
            return norm_two(
                scalars, block_input, attn_kept, attn_arrived, swap(sent, "tensor", 2),
                gain_ffn[None, :],
            )

        hidden, two_own = section(sum_heads)

        two_own, gate_halves = hold([cot_l], [two_own, tuple(gate_far[1:])])
        gate_y2 = [swap(part, "dp", 1) for part in gate_halves]

        def gather_near():
            two_x = swap(two_own, "tensor", 2)
            two_l = swap(two_own, "dp", pair_bit)
            return two_x, two_l, join_rows(scalars, rest_mine, rest_theirs, 1, 2)

        two_x, two_l, down_piece = section(gather_near)

        rows = two_own.shape[0]
        two_x, two_l, up_halves = hold([own_y, gate_y2], [two_x, two_l, tuple(up_far[1:])])
        up_y2 = [swap(part, "dp", 1) for part in up_halves]

        def gather_rest():
            given_a, given_b = halves(scalars, two_l, two_x)
            far_a = swap(given_a, "tensor", 2)
            far_b = swap(given_b, "dp", pair_bit)

            def cores():
                given, arrived = [two_x, two_l, two_own], []
                for at in range(3):
                    part = swap(given[at], "tensor", 1)
                    part, *given = hold([], [part] + given)
                    arrived.append(part)
                return arrived

            arrived = section(cores)
            return hold([], [far_a, far_b, *arrived])

        far_a, far_b, two_x_c, two_l_c, two_own_c = section(gather_rest)
        far_a, far_b, down_piece = hold([], [far_a, far_b, down_piece])
        down_far = far_pieces(down_piece)

        def gather_far():
            return swap(far_a, "tensor", 1), swap(far_b, "tensor", 1)

        far_a_c, far_b_c = section(gather_far)
        two_pieces = [two_own, two_x, two_l]
        two_pieces_c = [two_own_c, two_x_c, two_l_c]

        size = gate_piece.shape[0]
        gate_pieces = [(part, 0) for part in [*gate_far]] + [
            (part, 0) for part in [own_y, *gate_y2]
        ]
        far_a, far_b, far_a_c, far_b_c, down_piece_y, cot_x, cot_l, up_y2 = hold(
            [], [far_a, far_b, far_a_c, far_b_c, down_piece, cot_x, cot_l, tuple(up_y2)]
        )
        up_pieces = [(part, 0) for part in [*up_far]] + [(own_y, size)] + [
            (part, 0) for part in up_y2
        ]
        two_pieces += [far_a, far_b]
        two_pieces_c += [far_a_c, far_b_c]

        def feed_own():
            down_y1 = swap(down_piece_y, "dp", 1)
            cot_far = swap(cot_l, "tensor", 2)
            x_c = swap(cot_x, "tensor", 1)
            own = ffn_up(scalars, two_pieces, gate_pieces, up_pieces)
            down_y1, cot_far, x_c = hold([own], [down_y1, cot_far, x_c])
            return down_y1, cot_far, x_c, own

        down_y1, cot_far, cot_x_c, (acts_a, mixed_a, silu_a, back_a) = section(feed_own)

        mixed_a, cot_l_in = hold([], [mixed_a, cot_l])

        def feed_core():
            l_c = swap(cot_l_in, "tensor", 1)
            far_c = swap(cot_far, "tensor", 1)
            core = ffn_up(scalars, two_pieces_c, gate_pieces, up_pieces)
            l_c, far_c = hold([core], [l_c, far_c])
            return l_c, far_c, core

        cot_l_c, cot_far_c, (acts_b, mixed_b, silu_b, back_b) = section(feed_core)

        cots = [cotangent, cot_x, cot_l, cot_far]
        cots_c = [cot_own_c, cot_x_c, cot_l_c, cot_far_c]
        mixed_b, down_halves = hold([down_y1], [mixed_b, tuple(down_far[1:])])
        down_y2 = tuple(swap(part, "dp", 1) for part in down_halves)
        down_kept, down_sent = section(
            lambda: ffn_grad(scalars, cots, cots_c, mixed_a, mixed_b, "grad_down")
        )
        down_sent, down_y2 = hold([], [down_sent, down_y2])
        down_pieces = [(part, 0) for part in [*down_far, down_y1, *down_y2]]

        down_sent, silu_b = hold([], [down_sent, silu_b])
        down_sent = swap(down_sent, "dp", 1)

        def back_all():
            gate_b, up_b, two_sent = ffn_back(
                scalars, cots_c, down_pieces, gate_pieces, up_pieces, silu_b, back_b
            )
            (two_sent,) = hold([], [two_sent])
            arrived = swap(two_sent, "tensor", 1)
            gate_a, up_a, kept = ffn_back(
                scalars, cots, down_pieces, gate_pieces, up_pieces, silu_a, back_a
            )
            (kept,) = hold([], [kept])
            far = part_sum(scalars, kept, arrived, kept.shape[0] // 4, 3, 2)
            return gate_a, up_a, gate_b, up_b, kept, arrived, *far

        gate_a, up_a, gate_b, up_b, two_kept, two_arrived, far_a, far_b = section(back_all)

        far_a, far_b, mixed_b = hold([], [far_a, far_b, mixed_b])
        model = far_a.shape[1]

        def spread_far():
            far_x = swap(far_a, "tensor", 2)
            far_l = swap(far_b, "dp", pair_bit)

            def block_rows():
                sent = ffn_rows(scalars, mixed_b, down_pieces, model, "block_rows")
                (sent,) = hold([], [sent])
                arrived = swap(sent, "tensor", 1)
                kept = ffn_rows(scalars, mixed_a, down_pieces, model, "block_rows")
                return hold([], [kept, arrived])

            outs = section(block_rows)
            outs, far_x, far_l = hold([], [outs, far_x, far_l])
            return (*outs, *spread_rest(scalars, two_kept, two_arrived, far_x, far_l))

        block_kept, block_arrived, own, to_x, to_l = section(spread_far)

        to_x, to_l, down_sent = hold([], [to_x, to_l, down_sent])

        def spread_near():
            from_x = swap(to_x, "tensor", 2)
            from_l = swap(to_l, "dp", pair_bit)
            up_grads = ffn_grad(scalars, [acts_a], [acts_b], up_a, up_b, "grad_up")
            down_pair = fold_sum(scalars, down_kept, down_sent, far_bits[0], 1)
            block_rows = 2 * own.shape[0]
            block_pair = part_sum(scalars, block_kept, block_arrived, block_rows, 1, 1)
            from_x, from_l = hold([up_grads, down_pair, block_pair], [from_x, from_l])
            return (
                *up_grads,
                *down_pair,
                *block_pair,
                *norm_two_back(
                    scalars, own, from_x, from_l, hidden, gain_ffn[None, :], cotangent
                ),
            )

        (
            up_kept, up_sent, down_kept, down_sent, block_sent, grad_hidden, attn_own, gain_two,
        ) = section(spread_near)

        attn_own, down_sent, up_sent, gate_b, block_sent = hold(
            [], [attn_own, down_sent, up_sent, gate_b, block_sent]
        )
        down_kept, down_sent = far_rest(down_kept, down_sent)
        up_sent = swap(up_sent, "dp", 1)
        block_from_l = swap(block_sent, "dp", pair_bit)

        def attention_back():
            def gather_back():
                attn_x = swap(attn_own, "tensor", 2)
                own_c = swap(attn_own, "tensor", 1)
                gate_grads = ffn_grad(scalars, [acts_a], [acts_b], gate_a, gate_b, "grad_gate")
                attn_x, own_c = hold([gate_grads], [attn_x, own_c])
                return (attn_x, own_c, *gate_grads)

            attn_x, own_c, gate_kept, gate_sent = section(gather_back)
            attn_x, own_c, gate_sent = hold([], [attn_x, own_c, gate_sent])
            x_c = swap(attn_x, "tensor", 1)
            outs = attend_back(
                scalars, query_rot, kv_own, kv_other, starts, out_parts,
                [attn_own, attn_x, own_c, x_c], context, cosine, sine,
            )
            return gate_kept, gate_sent, outs

        gate_kept, gate_sent, outs = section(attention_back)
        grad_query_low, kv_kept, kv_given, bias_rows, wout_kept, wout_sent = outs

        kv_given, up_sent = hold([], [kv_given, up_sent])

        def pass_keys():
            kv_arrived = swap(kv_given, "tensor", 1)
            up_pair = fold_sum(scalars, up_kept, up_sent, far_bits[0], 1)
            (kv_arrived,) = hold([up_pair], [kv_arrived])
            return kv_arrived, *up_pair

        kv_arrived, up_own, up_given = section(pass_keys)
        kv_arrived, up_given, wout_sent, gate_sent, down_sent, block_from_l = hold(
            [], [kv_arrived, up_given, wout_sent, gate_sent, down_sent, block_from_l]
        )
        wout_arrived = swap(wout_sent, "dp", pair_bit)
        devices = dp_size * tensor_size

        def input_grads():
            kv_in, gate_in, up_in = hold([], [kv_arrived, gate_sent, up_given])
            gate_y = swap(gate_in, "dp", 1)
            up_sum, up_far_sum = far_rest(up_own, up_in)

            def project_all():
                grad_qkv, one_kept, one_sent = project_back(
                    scalars, grad_query_low, kv_kept, kv_in, qkv_pieces
                )
                one_sent, grad_qkv = hold([], [one_sent, grad_qkv])
                arrived = swap(one_sent, "tensor", 1)
                wqkv_pair = project_grad(scalars, act_pair, act_c, grad_qkv)
                (arrived,) = hold([wqkv_pair], [arrived])
                wqkv_kept, wqkv_sent = wqkv_pair
                one_partner = one_sent
                (one_given,) = part_sum(scalars, one_kept, arrived, block_input.shape[0], 1, 1)
                one_arrived = arrived

                def first_norm_back():
                    arrived = swap(one_given, "tensor", 2)
                    wqkv_arrived = swap(wqkv_sent, "dp", pair_bit)
                    block = block_x_sum(scalars, block_kept, block_arrived, block_from_l)
                    down_pair = fold_sum(scalars, down_kept, down_sent, pair_bit, 1)
                    gain_rows = gain_rows_of(scalars, one_kept, one_partner, act_pair, act_c)
                    bias_keyval = jnp.zeros((2 * KV * HD,), f32)
                    bias_keyval = lax.dynamic_update_slice_in_dim(
                        bias_keyval, bias_rows[0, width : width + HD], head_kv * HD, 0
                    )
                    bias_keyval = lax.dynamic_update_slice_in_dim(
                        bias_keyval, bias_rows[0, width + HD :], KV * HD + head_kv * HD, 0
                    )
                    bias_query = lax.dynamic_update_slice_in_dim(
                        jnp.zeros((HQ * HD,), f32), bias_rows[0, :width], tensor_index * width, 0
                    )
                    parts = (gain_rows[0] / gain_attn, gain_two[0], bias_query, bias_keyval)
                    small = jnp.concatenate([part.reshape(devices, -1) for part in parts], axis=1)
                    (arrived,) = hold([block, small, down_pair], [arrived])
                    grad_rows = norm_one_back(
                        scalars, block_input, one_kept, one_arrived, arrived, gain_attn[None, :],
                        grad_hidden,
                    )
                    (wqkv_arrived,) = hold([grad_rows], [wqkv_arrived])
                    return (*down_pair, wqkv_kept, grad_rows, small, block, wqkv_arrived)

                return section(first_norm_back)

            outs = section(project_all)
            outs, gate_y, up_far_sum = hold([], [outs, gate_y, up_far_sum])
            return (up_sum, up_far_sum, gate_y, *outs)

        (
            up_kept, up_sent, gate_sent, down_mine, down_given, wqkv_kept, grad_rows, small,
            block_to_x, wqkv_arrived,
        ) = section(input_grads)

        wqkv_arrived, wout_arrived, gate_sent, small, down_given = hold(
            [], [wqkv_arrived, wout_arrived, gate_sent, small, down_given]
        )
        gate_kept, gate_sent = fold_sum(scalars, gate_kept, gate_sent, far_bits[0], 1)
        wqkv_arrived, gate_sent, small = hold([], [wqkv_arrived, gate_sent, small])
        gate_kept, gate_sent = far_rest(gate_kept, gate_sent)
        small = lax.all_to_all(small, ("dp", "tensor"), 0, 0, tiled=True)

        def last_rows():
            block_x = swap(block_to_x, "tensor", 2)
            down_theirs = swap(down_given, "dp", pair_bit)

            def attn_step():
                own, sent = fold_both(
                    scalars, wqkv_kept, wqkv_arrived, wout_kept, wout_arrived, 1, groups
                )
                arrived = swap(sent, "dp", 1)
                up_pair = fold_sum(scalars, up_kept, up_sent, pair_bit, 1)
                (arrived,) = hold([up_pair], [arrived])
                return (*fold_sum(scalars, own, arrived, far_bits[0], 1), *up_pair)

            *attn_outs, block_x, down_theirs = hold(
                [], [*section(attn_step), block_x, down_theirs]
            )
            block_out = block_final(
                scalars, block_kept, block_arrived, block_from_l, hidden, block_x
            )
            down_share = join_cols(scalars, down_mine, down_theirs, w_down.shape[0] // 2).T
            return *attn_outs, block_out, down_share

        attn_kept, attn_sent, up_mine, up_given, block_out, down_share = section(last_rows)

        gate_sent, attn_sent, up_given, small = hold(
            [block_out, down_share], [gate_sent, attn_sent, up_given, small]
        )
        attn_kept, attn_sent = far_rest(attn_kept, attn_sent)
        up_theirs = swap(up_given, "dp", pair_bit)
        gate_mine, gate_given = fold_sum(scalars, gate_kept, gate_sent, pair_bit, 1)
        gate_theirs = swap(gate_given, "dp", pair_bit)
        small = jnp.sum(small, axis=0)
        up_theirs = hold([gate_given, small], [up_theirs])[0]
        up_share = join_cols(scalars, up_mine, up_theirs, w_up.shape[1] // 2)
        (attn_sent,) = hold([up_share], [attn_sent])
        share = add(attn_kept, attn_sent)
        kv_rows = share[:, width : width + HD]
        share_rows = kv_rows.shape[0] // tensor_size
        moved = []
        for mask in range(tensor_size):
            rows_for = lax.dynamic_slice_in_dim(
                kv_rows, (tensor_index ^ mask) * share_rows, share_rows, 0
            )
            moved.append(swap(rows_for, "tensor", mask) if mask else rows_for)
        query_share, out_share = share[:, :width], share[:, width + HD :].T
        gate_theirs, *moved = hold([query_share, out_share], [gate_theirs] + moved)
        gate_share = join_cols(scalars, gate_mine, gate_theirs, w_gate.shape[1] // 2)
        keyval_share = jnp.zeros((share_rows, 2 * KV * HD), f32)
        for mask in range(tensor_size):
            sender = tensor_index ^ mask
            column = (sender % 2) * (KV * HD) + (sender * local_heads // (HQ // KV)) * HD
            keyval_share = lax.dynamic_update_slice_in_dim(keyval_share, moved[mask], column, 1)
        sizes = [HQ * HD // devices, 2 * KV * HD // devices, gain_attn.shape[0] // devices]
        ends = [sizes[2], 2 * sizes[2], 2 * sizes[2] + sizes[0]]
        gain_one_share = small[: ends[0]]
        gain_two_share = small[ends[0] : ends[1]]
        query_bias_share = small[ends[1] : ends[2]]
        keyval_bias_share = small[ends[2] :]
        return (
            block_out,
            grad_rows,
            gain_one_share,
            query_share,
            query_bias_share,
            keyval_share,
            keyval_bias_share,
            out_share,
            gain_two_share,
            gate_share,
            up_share,
            down_share,
        )

    placed = (
        P(("dp", "tensor"), None),
        P("dp", None),
        P(),
        P("dp", "tensor"),
        P("tensor"),
        P("dp", None),
        P(),
        P("tensor", "dp"),
        P(),
        P("dp", "tensor"),
        P("dp", "tensor"),
        P("tensor", "dp"),
        P(("dp", "tensor"), None),
    )
    return jax.shard_map(
        local,
        mesh=mesh,
        in_specs=placed,
        out_specs=(
            P(("dp", "tensor"), None),
            P(("dp", "tensor"), None),
            P(("dp", "tensor")),
            P("dp", "tensor"),
            P(("dp", "tensor")),
            P(("dp", "tensor"), None),
            P(("dp", "tensor")),
            P("tensor", "dp"),
            P(("dp", "tensor")),
            P("dp", "tensor"),
            P("dp", "tensor"),
            P("tensor", "dp"),
        ),
        check_vma=False,
    )
```
